128 devices in a mesh: side: 4 (over z), blk: 32 (over x, y, core).
Axes of the slice: x: 4, y: 4, z: 4, core: 2. Of those that a mesh axis runs over, the one named last changes fastest.
Arguments:
- source: bfloat16 [65536, 256], P(('side', 'blk')), may hold values from -16 to 16
- target: bfloat16 [32768, 256], P('blk'), may hold values from -16 to 16
- pairs: int32 [1024, 4], P(('side', 'blk')), may hold values from 0 to 31, all different within a row; in each aligned block of 8 rows (0 to 7, 8 to 15, ...) at most 2 rows name the same one
- owner_map: int32 [32], replicated, may hold values from 0 to 31, each once
Outputs:
- source_potential: float32 [65536], P(('side', 'blk'))
- g_dual: float32 [32768], P('blk')
- mapped: bfloat16 [65536, 256], P(('side', 'blk'))
The draws below stay inside these ranges and needn't reach their ends.
Inputs may be any that keep to these rules, and one draw needn't show every extreme that they name: `pairs`: each row names 4 different target blocks. Within the rows of one device (aligned blocks of 8 rows) no block is named by more than 2 rows, and some block is named by exactly 2; every block is named by some row. `owner_map`: each block index once.
All inputs are finite; a program needn't handle non-finite values.
Results may differ from the reference program's by a relative error of at most 0.0047.
Values may be sent and summed in bfloat16 or wider, within the bound.
A program may use at most 64 MiB of HBM per device.

```python
import math
import jax
import jax.numpy as jnp
import numpy as np
from jax import lax

D = 256
BT = 1024
BS = 64
KT = 4
CAP = 2
ITERS = 2
SB_DEV = 8
NSB = 1024
NS = 65536
NT = 32768
N_BLK = 32


def draw_target(key, part):
    own_key = jax.random.fold_in(key, 1)
    values = jnp.clip(jax.random.normal(own_key, (NT, D), jnp.float32), -6.0, 6.0)
    return values.astype(jnp.bfloat16)


def draw_source(key, part):
    own_key = jax.random.fold_in(key, 2)
    values = jnp.clip(jax.random.normal(own_key, (NS, D), jnp.float32), -6.0, 6.0)
    return values.astype(jnp.bfloat16)


def routed_block(rng, own, number, rows, count, top, most, skew):
    sequence = jax.random.permutation(rng, count)
    heavy_load, ordinary = load_shares(count, rows * top, most, skew, True), load_shares(count, rows * top, most, skew, False)
    places = jnp.arange(count)

    def named(tallies, turn):
        used = int((tallies > 0).sum())
        fixed = max(1, used // 4)
        passed = fixed + (places - fixed + turn * (used - fixed)) % max(1, count - fixed)
        return jnp.zeros((count,), jnp.int32).at[sequence[jnp.where(places < fixed, places, passed)]].set(jnp.asarray(tallies, jnp.int32))

    tallies = jnp.where(number % 4 == 0, named(heavy_load, number // 4), named(ordinary, number - number // 4 - 1))
    mixed = jax.random.permutation(jax.random.fold_in(own, 3), count)
    donor, receiver = mixed[0:count // 2 * 2:2], mixed[1:count // 2 * 2:2]
    slack = jnp.minimum(tallies[donor] - 1, most - tallies[receiver]) // 2
    slack = jnp.where((donor == sequence[0]) | (receiver == sequence[0]) | (tallies[receiver] == 0), 0, jnp.maximum(slack, 0))
    passed = jax.random.randint(jax.random.fold_in(own, 4), (count // 2,), 0, 1 << 20) % (slack + 1)
    tallies = tallies.at[donor].add(-passed).at[receiver].add(passed)
    members = jnp.searchsorted(jnp.cumsum(tallies), jnp.arange(rows * top), side="right").astype(jnp.int32)
    grid = members.reshape(top, rows).T
    grid = grid[jax.random.permutation(jax.random.fold_in(own, 1), rows)]
    turn = jax.random.randint(jax.random.fold_in(own, 2), (rows, 1), 0, top)
    return jnp.take_along_axis(grid, (jnp.arange(top)[None, :] + turn) % top, axis=1)


def load_shares(amount, total, reach, skew, full):
    portions = [(1 << 20) // math.isqrt(rank ** skew) + 1 for rank in range(1, amount + 1)]
    largest = reach if full else min(reach, max(-(-total // amount), total * portions[0] // sum(portions)))
    least = 1 if total - largest >= amount - 1 else 0
    given, rest = [largest] + [least] * (amount - 1), total - largest - least * (amount - 1)
    while rest > 0:
        candidates = [i for i in range(1, amount) if given[i] < largest] or [i for i in range(1, amount) if given[i] < reach]
        pool, budget = sum([portions[i] for i in candidates]), rest
        for i in candidates:
            extra = min(reach - given[i], max(1, budget * portions[i] // pool), rest)
            given[i] = given[i] + extra
            rest = rest - extra
    return np.array(given)


def setup_inputs(seed: int = 0) -> dict:
    splits = jax.random.split(jax.random.key(seed), 5)
    source = draw_source(jax.random.fold_in(splits[4], 71), 0)
    target = draw_target(jax.random.fold_in(splits[4], 71), 0)
    pairs_keys = jax.random.split(jax.random.fold_in(splits[2], 1), NSB // SB_DEV)
    pairs_turns = jax.random.permutation(jax.random.fold_in(splits[2], 3), NSB // SB_DEV)
    pairs = jax.vmap(lambda own, number: routed_block(jax.random.fold_in(splits[2], 2), own, number, SB_DEV, N_BLK, KT, CAP, 2))(pairs_keys, pairs_turns).reshape((NSB, KT))
    owner_map = jax.random.permutation(splits[3], N_BLK).astype(jnp.int32)
    return dict(source=source, target=target, pairs=pairs, owner_map=owner_map)


eps_reg = 0.3
floor_value = -1e+30

def tile_logits(block, tiles):
    product = jnp.einsum('rd,kcd->krc', block.astype(jnp.float32), tiles.astype(jnp.float32))
    return product * (1.0 / (eps_reg * math.sqrt(D)))

def reference(source, target, pairs, owner_map):
    target_blocks = target.reshape(N_BLK, BT, D)
    source_blocks = source.reshape(NSB, BS, D)
    owners = owner_map[pairs].astype(jnp.int32)

    def row_pass(g_dual):
        g_blocks = g_dual.reshape(N_BLK, BT)

        def single(inputs):
            block, listed = inputs
            logits = tile_logits(block, target_blocks[listed]) + g_blocks[listed][:, None, :] / eps_reg
            highest = lax.optimization_barrier(jnp.max(logits, axis=(0, 2)))
            summed = lax.optimization_barrier(jnp.sum(jnp.exp(logits - highest[None, :, None]), axis=(0, 2)))
            return -eps_reg * (highest + jnp.log(summed))
        return lax.map(single, (source_blocks, owners)).reshape(NS)

    def column_update(source_potential):
        f_blocks = source_potential.reshape(NSB, BS)

        def accumulate_terms(carry, inputs):
            highest, summed = carry
            block, listed, f_values = inputs
            logits = tile_logits(block, target_blocks[listed]) + f_values[None, :, None] / eps_reg
            old_high = highest[listed]
            old_sum = summed[listed]
            raised = jnp.maximum(old_high, lax.optimization_barrier(jnp.max(logits, axis=1)))
            added = lax.optimization_barrier(jnp.sum(jnp.exp(logits - raised[:, None, :]), axis=1))
            new_sum = old_sum * jnp.exp(old_high - raised) + added
            return ((highest.at[listed].set(raised), summed.at[listed].set(new_sum)), None)
        start = (jnp.full((N_BLK, BT), floor_value, jnp.float32), jnp.zeros((N_BLK, BT), jnp.float32))
        (highest, summed), _ = lax.scan(accumulate_terms, start, (source_blocks, owners, f_blocks))
        return (-eps_reg * (highest + jnp.log(summed))).reshape(NT)

    def map_pass(g_dual):
        g_blocks = g_dual.reshape(N_BLK, BT)

        def single(inputs):
            block, listed = inputs
            tiles = target_blocks[listed]
            logits = tile_logits(block, tiles) + g_blocks[listed][:, None, :] / eps_reg
            highest = lax.optimization_barrier(jnp.max(logits, axis=2))
            weights = jnp.exp(logits - highest[:, :, None])
            summed = lax.optimization_barrier(jnp.sum(weights, axis=2))
            rounded = lax.optimization_barrier(weights.astype(jnp.bfloat16)).astype(jnp.float32)
            numerators = jnp.einsum('krc,kcd->krd', rounded, tiles.astype(jnp.float32))
            numerators = lax.optimization_barrier(numerators.astype(jnp.bfloat16)).astype(jnp.float32)
            best = lax.optimization_barrier(jnp.max(highest, axis=0))
            factors = jnp.exp(highest - best[None, :])
            weighted = lax.optimization_barrier(jnp.sum(factors[:, :, None] * numerators, axis=0))
            normalizer = lax.optimization_barrier(jnp.sum(factors * summed, axis=0))
            return (weighted / normalizer[:, None]).astype(jnp.bfloat16)
        return lax.map(single, (source_blocks, owners)).reshape(NS, D)
    g_dual = jnp.zeros((NT,), jnp.float32)
    source_potential = jnp.zeros((NS,), jnp.float32)
    for iteration in range(ITERS):
        source_potential = row_pass(g_dual)
        g_dual = column_update(source_potential)
    return (source_potential, g_dual, map_pass(g_dual))
```

```python
import functools
import math

import jax
import jax.numpy as jnp
from jax import lax
from jax.experimental import pallas as pl
from jax.experimental.pallas import tpu as pltpu
from jax.sharding import PartitionSpec as P

MESH = pl.DeviceIdType.MESH
NEG = -1e30
LOG2E = 1.4426950408889634
LN2 = 0.6931471805599453
REG = 0.3
ITERS = 2
NT = (((1,), (1,)), ((), ()))
F32 = jnp.float32
BF16 = jnp.bfloat16


def lse(parts):
    top = functools.reduce(jnp.maximum, parts)
    total = functools.reduce(jnp.add, [jnp.exp2(p - top) for p in parts])
    return top + jnp.log2(total)


def kernel(
    source, target, pairs, owner_map, f_out, g_out, mapped,
    src, tgt, tab, stab, sq, logits, weights, tgt_t, gcol, cmax, csum,
    rmax, rsum, rowbuf, ftab, frow, colbuf, ztot, numer, part, comb, pin, rin,
    hin, send_sem, recv_sem, local_sem,
):
    side = lax.axis_index("side")
    blk = lax.axis_index("blk")
    x = blk // 8
    y = (blk // 2) % 4
    c = blk % 2

    def at(kx=0, kc=0, ky=0, kz=0):
        xx = (x + kx) % 4
        yy = (y + ky) % 4
        cc = (c + kc) % 2
        zz = (side + kz) % 4
        return (zz, (xx * 4 + yy) * 2 + cc)

    count = [0]

    def transfer(source_ref, dest_ref, device):
        n = count[0]
        count[0] += 1
        return pltpu.make_async_remote_copy(
            src_ref=source_ref, dst_ref=dest_ref,
            send_sem=send_sem.at[n], recv_sem=recv_sem.at[n],
            device_id=device, device_id_type=MESH,
        )

    sent = []

    def go(copy):
        copy.start()
        sent.append(copy)
        return copy

    def dev(d):
        return pl.ds(d * 8, 8)

    row_peers = [(kx, kc) for kx in range(4) for kc in range(2)][1:]
    peers = [at(kx=kx, kc=kc) for kx, kc in row_peers]
    peers += [at(ky=k) for k in (1, 2, 3)] + [at(kz=k) for k in (1, 2, 3)]
    barrier = pltpu.get_barrier_semaphore()
    for peer in peers:
        pl.semaphore_signal(barrier, inc=1, device_id=peer, device_id_type=MESH)

    own_src = pltpu.make_async_copy(source, src.at[dev(0)], local_sem.at[0])
    own_src.start()
    own_tgt = pltpu.make_async_copy(target, tgt.at[0], local_sem.at[1])
    own_tgt.start()

    lane = lax.broadcasted_iota(jnp.int32, (8, 128), 1)
    sub = lax.broadcasted_iota(jnp.int32, (8, 128), 0)
    low = lane < 64
    low1 = low[0:1]

    seen = jnp.zeros((8, 128), jnp.int32)
    table = jnp.full((8, 128), 8, jnp.int32)
    for s in range(8):
        hit = lane == owner_map[pairs[s, 0]]
        for k in range(1, 4):
            hit = jnp.logical_or(hit, lane == owner_map[pairs[s, k]])
        table = jnp.where(jnp.logical_and(hit, seen == sub), s, table)
        seen = seen + jnp.where(hit, 1, 0)
    tab[0] = table

    pl.semaphore_wait(barrier, len(peers))

    A, B = pl.ds(0, 256), pl.ds(256, 256)
    s_p = go(transfer(source, src.at[dev(6)], at(kx=1)))
    s_m = go(transfer(source, src.at[dev(2)], at(kx=3)))
    HA, HB = pl.ds(0, 512), pl.ds(512, 512)
    t_p = go(transfer(target, tgt.at[3], at(ky=1)))
    t_m = go(transfer(target, tgt.at[1], at(ky=3)))
    s_c = go(transfer(source, src.at[dev(1)], at(kc=1)))
    tabs = []
    for kx, kc in row_peers:
        slot = ((-kx) % 4) * 2 + kc
        tabs.append(go(transfer(tab.at[0], tab.at[slot], at(kx=kx, kc=kc))))

    s_p.wait_recv()
    s_fp = go(transfer(src.at[pl.ds(48, 4)], src.at[pl.ds(32, 4)], at(kx=1)))
    s_cp = go(transfer(src.at[dev(6)], src.at[dev(7)], at(kc=1)))
    s_m.wait_recv()
    s_fm = go(transfer(src.at[pl.ds(20, 4)], src.at[pl.ds(36, 4)], at(kx=3)))
    s_cm = go(transfer(src.at[dev(2)], src.at[dev(3)], at(kc=1)))
    for t in tabs:
        t.wait_recv()
    own_src.wait()
    copy_tab = pltpu.make_async_copy(tab, stab, local_sem.at[2])
    copy_tab.start()
    s_fp.wait_recv()
    s_fm.wait_recv()
    s_c2 = go(transfer(src.at[dev(4)], src.at[dev(5)], at(kc=1)))
    t_p.wait_recv()
    t_fp = go(transfer(tgt.at[3, HA], tgt.at[2, HA], at(ky=1)))
    t_m.wait_recv()
    t_fm = go(transfer(tgt.at[1, HB], tgt.at[2, HB], at(ky=3)))
    copy_tab.wait()
    for t in (s_c, s_cp, s_cm, s_c2):
        t.wait_recv()
    own_tgt.wait()

    owner = [(x * 4 + (y + q) % 4) * 2 + c for q in range(4)]

    def block(d, q, r):
        return stab[d, r, owner[q]]

    ones = jnp.full((8, 128), NEG, F32)
    for d in range(8):
        ftab[d * 16 + 8] = ones

    scale = LOG2E / (REG * 16.0)
    eye = jnp.where(
        lax.broadcasted_iota(jnp.int32, (256, 256), 0)
        == lax.broadcasted_iota(jnp.int32, (256, 256), 1), 1.0, 0.0).astype(BF16)

    def logits_of(q):
        def pick(d, _):
            for r in range(2):
                b = jnp.minimum(block(d, q, r), 7)
                rows = src[d * 8 + b]
                sq[pl.ds(pl.multiple_of(d * 128 + r * 64, 64), 64), :] = rows
            return 0

        lax.fori_loop(0, 8, pick, 0)

        def chunk(j, _):
            rows = pl.ds(pl.multiple_of(j * 256, 256), 256)
            left = tgt[q, rows, :]
            for g in range(4):
                right = sq[pl.ds(g * 256, 256), :]
                out = lax.dot_general(left, right, NT, preferred_element_type=F32)
                logits[q, rows, pl.ds(g * 256, 256)] = out * scale
            return 0

        lax.fori_loop(0, 4, chunk, 0)

        def turn(j, _):
            rows = pl.ds(pl.multiple_of(j * 256, 256), 256)
            out = lax.dot_general(eye, tgt[q, rows, :], NT, preferred_element_type=F32)
            tgt_t[q, :, rows] = out.astype(BF16)
            return 0

        lax.fori_loop(0, 4, turn, 0)

    R = 32

    def fold(value, op):
        return op(value.reshape(R // 8, 8, 128), axis=0)

    def lanes(d):
        return pl.ds(d * 128, 128)

    def row_sweeps(q, with_g, keep):
        def shifted(rows):
            if with_g:
                g = gcol[q, rows, :]
                return [logits[q, rows, lanes(d)] + g for d in range(8)]
            return [logits[q, rows, lanes(d)] for d in range(8)]

        def first(i, tops):
            rows = pl.ds(pl.multiple_of(i * R, R), R)
            return tuple(jnp.maximum(t, fold(v, jnp.max)) for t, v in zip(tops, shifted(rows)))

        tops = lax.fori_loop(0, 1024 // R, first, (jnp.full((8, 128), NEG, F32),) * 8)
        tops = [jnp.max(t, axis=0, keepdims=True) for t in tops]

        def second(i, sums):
            rows = pl.ds(pl.multiple_of(i * R, R), R)
            new = []
            for d, v in enumerate(shifted(rows)):
                p = jnp.exp2(v - tops[d])
                if keep:
                    weights[q, rows, lanes(d)] = p.astype(BF16)
                new.append(sums[d] + fold(p, jnp.sum))
            return tuple(new)

        sums = lax.fori_loop(0, 1024 // R, second, (jnp.zeros((8, 128), F32),) * 8)
        for d in range(8):
            rmax[q, 0:1, lanes(d)] = tops[d]
            rsum[q, 0:1, lanes(d)] = jnp.sum(sums[d], axis=0, keepdims=True)

    def row_local(phase):
        packed = [None] * 4
        for d in range(8):
            terms = []
            for q in range(4):
                v = rmax[q, 0:1, lanes(d)] + jnp.log2(rsum[q, 0:1, lanes(d)])
                w = pltpu.roll(v, 64, 1)
                terms.append(jnp.where(sub == block(d, q, 0), jnp.where(low1, v, w), NEG))
                terms.append(jnp.where(sub == block(d, q, 1), jnp.where(low1, w, v), NEG))
            out = lse(terms)
            if d % 2 == 0:
                packed[d // 2] = out
            else:
                rowbuf[phase, 0, d // 2] = jnp.where(low, packed[d // 2], out)

    def row_start(phase):
        copies = []
        for kx, kc in row_peers:
            slot = ((-kx) % 4) * 2 + kc
            copies.append(go(transfer(rowbuf.at[phase, 0], rowbuf.at[phase, slot], at(kx=kx, kc=kc))))
        return copies

    def row_finish(phase, copies):
        for t in copies:
            t.wait_recv()
        for i in range(4):
            terms = [rowbuf[phase, 0, i]]
            for kx, kc in row_peers:
                v = rowbuf[phase, kx * 2 + kc, (i - kx) % 4]
                terms.append(pltpu.roll(v, 64, 1) if kc else v)
            total = -lse(terms)
            other = pltpu.roll(total, 64, 1)
            even = jnp.where(low, total, other)
            odd = jnp.where(low, other, total)
            for b in range(8):
                ftab[32 * i + b] = jnp.broadcast_to(even[b:b + 1], (8, 128))
                ftab[32 * i + 16 + b] = jnp.broadcast_to(odd[b:b + 1], (8, 128))

    def row_spread():
        for q in range(4):
            for d in range(8):
                f0 = ftab[d * 16 + block(d, q, 0)]
                f1 = ftab[d * 16 + block(d, q, 1)]
                frow[q, :, lanes(d)] = jnp.where(low, f0, f1)

    diag = (lax.broadcasted_iota(jnp.int32, (128, 128), 0)
            == lax.broadcasted_iota(jnp.int32, (128, 128), 1))
    C = 16

    def column(q, phase):
        fs = [frow[q, 0:1, lanes(d)] for d in range(8)]

        def body(i, _):
            rows = pl.ds(pl.multiple_of(i * C, C), C)
            ts = [logits[q, rows, lanes(d)] + fs[d] for d in range(8)]
            m = functools.reduce(jnp.maximum, ts)
            cmax[rows, :] = m
            csum[rows, :] = functools.reduce(jnp.add, [jnp.exp2(t - m) for t in ts])
            return 0

        lax.fori_loop(0, 1024 // C, body, 0)

        def merge(h, _):
            rows = pl.ds(pl.multiple_of(h * 512, 512), 512)
            m = cmax[rows, :]
            top = jnp.max(m, axis=1, keepdims=True)
            total = jnp.sum(csum[rows, :] * jnp.exp2(m - top), axis=1, keepdims=True)
            out = top + jnp.log2(total)
            lines = []
            for i in range(4):
                spread = jnp.broadcast_to(out[i * 128:(i + 1) * 128], (128, 128))
                lines.append(jnp.sum(jnp.where(diag, spread, 0.0), axis=0, keepdims=True))
            colbuf[phase, 0, q, pl.ds(pl.multiple_of(h * 4, 4), 4), :] = jnp.concatenate(lines, axis=0)
            return 0

        lax.fori_loop(0, 2, merge, 0)

    def column_exchange(phase):
        copies = []
        for k in (1, 2, 3):
            copies.append(go(transfer(colbuf.at[phase, 0], colbuf.at[phase, (-k) % 4], at(ky=k))))
        for t in copies:
            t.wait_recv()
        for q in range(4):
            terms = [colbuf[phase, k, (q - k) % 4] for k in range(4)]
            ztot[phase, 0, q] = lse(terms)
        copies = []
        for k in (1, 2, 3):
            copies.append(go(transfer(ztot.at[phase, 0], ztot.at[phase, (-k) % 4], at(kz=k))))
        for t in copies:
            t.wait_recv()
        last = phase == ITERS - 1
        for q in range(4):
            terms = [ztot[phase, (z - side + 4) % 4, q] for z in range(4)]
            total = -lse(terms)
            if last and q == 0:
                g_out[...] = total * (REG * LN2)
            for h in range(2):
                cols = []
                for i in range(4):
                    line = jnp.broadcast_to(total[h * 4 + i:h * 4 + i + 1], (128, 128))
                    cols.append(jnp.sum(jnp.where(diag, line, 0.0), axis=1, keepdims=True))
                for i in range(4):
                    gcol[q, pl.ds((h * 4 + i) * 128, 128), :] = jnp.broadcast_to(cols[i], (128, 128))

    for q in range(4):
        if q == 2:
            t_fp.wait_recv()
            t_fm.wait_recv()
        logits_of(q)
        row_sweeps(q, False, False)

    for phase in range(ITERS):
        if phase > 0:
            for q in range(4):
                row_sweeps(q, True, False)
        row_local(phase)
        row_finish(phase, row_start(phase))
        row_spread()
        if phase == ITERS - 1:
            even = jnp.concatenate([ftab[2 * i][0:1] for i in range(4)], axis=0)
            odd = jnp.concatenate([ftab[2 * i + 1][0:1] for i in range(4)], axis=0)
            f_out[...] = jnp.where(low[0:4], even, odd) * (REG * LN2)
        for q in range(4):
            column(q, phase)
        column_exchange(phase)

    for q in range(4):
        row_sweeps(q, True, True)
    row_local(ITERS)
    copies = row_start(ITERS)

    row_finish(ITERS, copies)
    row_spread()

    def numerators(q):
        def chunk(g, _):
            cols = pl.ds(pl.multiple_of(g * 256, 256), 256)
            out = jnp.dot(tgt_t[q], weights[q, :, cols], preferred_element_type=F32)
            factor = jnp.exp2(rmax[q, 0:1, cols] + frow[q, 0:1, cols])
            numer[q, :, cols] = (out * factor).astype(BF16)
            return 0

        lax.fori_loop(0, 4, chunk, 0)

    for q in range(4):
        numerators(q)

    row_id = lax.broadcasted_iota(jnp.int32, (512, 128), 0)
    col_id = lax.broadcasted_iota(jnp.int32, (512, 128), 1)
    same = (row_id % 64) == (col_id % 64)
    row_block = row_id // 64

    def assemble(d):
        picks, values = [], []
        for q in range(4):
            chosen = jnp.where(low1, block(d, q, 0), block(d, q, 1))
            hit = jnp.logical_and(same, row_block == chosen)
            picks.append(jnp.where(hit, 1.0, 0.0).astype(BF16))
            values.append(numer[q, :, lanes(d)])
        pick = jnp.concatenate(picks, axis=1)
        value = jnp.concatenate(values, axis=1)
        part[d] = lax.dot_general(pick, value, NT, preferred_element_type=F32).astype(BF16)

    def plus(*refs):
        return functools.reduce(jnp.add, [r[...].astype(F32) for r in refs])

    halves = (A, B)
    to_core = {}
    for kx in (2, 1, 3, 0):
        assemble(kx * 2 + 1)
        to_core[kx] = go(transfer(part.at[kx * 2 + 1], pin.at[kx], at(kc=1)))
    for kx in (2, 1, 3, 0):
        assemble(kx * 2)
    to_core[2].wait_recv()
    comb[2] = plus(part.at[4], pin.at[2]).astype(BF16)
    h_p = go(transfer(comb.at[2, A], hin.at[0], at(kx=1)))
    h_m = go(transfer(comb.at[2, B], hin.at[1], at(kx=3)))
    to_core[1].wait_recv()
    to_core[3].wait_recv()
    comb[1, B] = plus(part.at[2, B], pin.at[1, B]).astype(BF16)
    comb[3, A] = plus(part.at[6, A], pin.at[3, A]).astype(BF16)
    r_pb = go(transfer(comb.at[1, B], rin.at[0, B], at(kx=1)))
    r_ma = go(transfer(comb.at[3, A], rin.at[1, A], at(kx=3)))
    h_p.wait_recv()
    comb[1, A] = plus(part.at[2, A], pin.at[1, A], hin.at[0]).astype(BF16)
    r_pa = go(transfer(comb.at[1, A], rin.at[0, A], at(kx=1)))
    h_m.wait_recv()
    comb[3, B] = plus(part.at[6, B], pin.at[3, B], hin.at[1]).astype(BF16)
    r_mb = go(transfer(comb.at[3, B], rin.at[1, B], at(kx=3)))
    to_core[0].wait_recv()
    for t in (r_pb, r_ma, r_pa, r_mb):
        t.wait_recv()
    mapped[...] = plus(part.at[0], pin.at[0], rin.at[0], rin.at[1]).astype(BF16)

    for t in sent:
        t.wait_send()


COPIES = 5 + 7 + 2 + 2 + 1 + 2 + 7 * (ITERS + 1) + 6 * ITERS + 4 + 6


def shards(source, target, pairs, owner_map):
    any_space = pl.BlockSpec(memory_space=pl.ANY)
    smem = pl.BlockSpec(memory_space=pltpu.SMEM)
    vmem = pl.BlockSpec(memory_space=pltpu.VMEM)
    f, g, mapped = pl.pallas_call(
        kernel,
        out_shape=(
            jax.ShapeDtypeStruct((4, 128), F32),
            jax.ShapeDtypeStruct((8, 128), F32),
            jax.ShapeDtypeStruct((512, 256), BF16),
        ),
        in_specs=[any_space, any_space, smem, smem],
        out_specs=(vmem, vmem, vmem),
        scratch_shapes=[
            pltpu.VMEM((64, 64, 256), BF16),
            pltpu.VMEM((4, 1024, 256), BF16),
            pltpu.VMEM((8, 8, 128), jnp.int32),
            pltpu.SMEM((8, 8, 128), jnp.int32),
            pltpu.VMEM((1024, 256), BF16),
            pltpu.VMEM((4, 1024, 1024), F32),
            pltpu.VMEM((4, 1024, 1024), BF16),
            pltpu.VMEM((4, 256, 1024), BF16),
            pltpu.VMEM((4, 1024, 128), F32),
            pltpu.VMEM((1024, 128), F32),
            pltpu.VMEM((1024, 128), F32),
            pltpu.VMEM((4, 8, 1024), F32),
            pltpu.VMEM((4, 8, 1024), F32),
            pltpu.VMEM((ITERS + 1, 8, 4, 8, 128), F32),
            pltpu.VMEM((128, 8, 128), F32),
            pltpu.VMEM((4, 8, 1024), F32),
            pltpu.VMEM((ITERS, 4, 4, 8, 128), F32),
            pltpu.VMEM((ITERS, 4, 4, 8, 128), F32),
            pltpu.VMEM((4, 256, 1024), BF16),
            pltpu.VMEM((8, 512, 256), BF16),
            pltpu.VMEM((4, 512, 256), BF16),
            pltpu.VMEM((4, 512, 256), BF16),
            pltpu.VMEM((2, 512, 256), BF16),
            pltpu.VMEM((2, 256, 256), BF16),
            pltpu.SemaphoreType.DMA((COPIES,)),
            pltpu.SemaphoreType.DMA((COPIES,)),
            pltpu.SemaphoreType.DMA((3,)),
        ],
        compiler_params=pltpu.CompilerParams(
            collective_id=0, has_side_effects=True, vmem_limit_bytes=60 * 1024 * 1024
        ),
        name="sinkhorn",
    )(source.reshape(8, 64, 256), target, pairs, owner_map)
    return f.reshape(512), g.reshape(1024), mapped


def solution(mesh):
    return jax.shard_map(
        shards,
        mesh=mesh,
        in_specs=(P(("side", "blk"), None), P("blk", None), P(("side", "blk"), None), P()),
        out_specs=(P(("side", "blk")), P("blk"), P(("side", "blk"), None)),
        check_vma=False,
    )
```

```python
import functools
import math

import jax
import jax.numpy as jnp
from jax import lax
from jax.experimental import pallas as pl
from jax.experimental.pallas import tpu as pltpu
from jax.sharding import PartitionSpec as P

MESH = pl.DeviceIdType.MESH
NEG = -1e30
LOG2E = 1.4426950408889634
LN2 = 0.6931471805599453
REG = 0.3
ITERS = 2
NT = (((1,), (1,)), ((), ()))
F32 = jnp.float32
BF16 = jnp.bfloat16


def lse(parts):
    top = functools.reduce(jnp.maximum, parts)
    total = functools.reduce(jnp.add, [jnp.exp2(p - top) for p in parts])
    return top + jnp.log2(total)


def kernel(
    source, target, pairs, owner_map, f_out, g_out, mapped,
    src0, src1, src2, src3, src4, src5, src6, src7, tgt, tab, stab, sq, logits, weights, tgt_t, gcol, cmax, csum,
    rmax, rsum, rowbuf, ftab, frow, colbuf, ztot, numer, part, comb, pin, rin,
    hin, send_sem, recv_sem, local_sem,
):
    src = (src0, src1, src2, src3, src4, src5, src6, src7)
    side = lax.axis_index("side")
    blk = lax.axis_index("blk")
    x = blk // 8
    y = (blk // 2) % 4
    c = blk % 2

    def at(kx=0, kc=0, ky=0, kz=0):
        xx = (x + kx) % 4
        yy = (y + ky) % 4
        cc = (c + kc) % 2
        zz = (side + kz) % 4
        return (zz, (xx * 4 + yy) * 2 + cc)

    count = [0]

    def transfer(source_ref, dest_ref, device):
        n = count[0]
        count[0] += 1
        return pltpu.make_async_remote_copy(
            src_ref=source_ref, dst_ref=dest_ref,
            send_sem=send_sem.at[n], recv_sem=recv_sem.at[n],
            device_id=device, device_id_type=MESH,
        )

    sent = []

    def go(copy):
        copy.start()
        sent.append(copy)
        return copy

    row_peers = [(kx, kc) for kx in range(4) for kc in range(2)][1:]
    peers = [at(kx=kx, kc=kc) for kx, kc in row_peers]
    peers += [at(ky=k) for k in (1, 2, 3)] + [at(kz=k) for k in (1, 2, 3)]
    barrier = pltpu.get_barrier_semaphore()
    for peer in peers:
        pl.semaphore_signal(barrier, inc=1, device_id=peer, device_id_type=MESH)

    own_src = pltpu.make_async_copy(source, src[0], local_sem.at[0])
    own_src.start()
    own_tgt = pltpu.make_async_copy(target, tgt.at[0], local_sem.at[1])
    own_tgt.start()

    lane = lax.broadcasted_iota(jnp.int32, (8, 128), 1)
    sub = lax.broadcasted_iota(jnp.int32, (8, 128), 0)
    low = lane < 64
    low1 = low[0:1]

    seen = jnp.zeros((8, 128), jnp.int32)
    table = jnp.full((8, 128), 8, jnp.int32)
    for s in range(8):
        hit = lane == owner_map[pairs[0, s]]
        for k in range(1, 4):
            hit = jnp.logical_or(hit, lane == owner_map[pairs[k, s]])
        table = jnp.where(jnp.logical_and(hit, seen == sub), s, table)
        seen = seen + jnp.where(hit, 1, 0)
    tab[0] = table

    pl.semaphore_wait(barrier, len(peers))

    A, B = pl.ds(0, 256), pl.ds(256, 256)
    tabs = []
    for kx, kc in row_peers:
        slot = ((-kx) % 4) * 2 + kc
        tabs.append(go(transfer(tab.at[0], tab.at[slot], at(kx=kx, kc=kc))))

    D1, D2 = pl.ds(0, 192), pl.ds(192, 192)

    def part_of(kz, half=None):
        start = 384 + 160 * ((side + kz) % 4)
        if half is None:
            return pl.ds(pl.multiple_of(start, 32), 160)
        return pl.ds(pl.multiple_of(start + 80 * half, 16), 80)

    own = part_of(0)
    up, down = at(ky=1), at(ky=3)
    s_p = go(transfer(source, src[6], at(kx=1)))
    s_m = go(transfer(source, src[2], at(kx=3)))
    ys_p = go(transfer(target.at[own], tgt.at[3, own], up))
    ys_m = go(transfer(target.at[own], tgt.at[1, own], down))
    y1_p = go(transfer(target.at[D1], tgt.at[3, D1], up))
    y2_m = go(transfer(target.at[D2], tgt.at[1, D2], down))
    s_c = go(transfer(source, src[1], at(kc=1)))

    def z_both(k, rows):
        return (go(transfer(tgt.at[k, rows], tgt.at[k, rows], at(kz=1))),
                go(transfer(tgt.at[k, rows], tgt.at[k, rows], at(kz=3))))

    def z_on(k, z_p, z_m):
        out = []
        if z_p is not None:
            z_p.wait_recv()
            rows = part_of(3, 0)
            out.append(go(transfer(tgt.at[k, rows], tgt.at[k, rows], at(kz=1))))
        if z_m is not None:
            z_m.wait_recv()
            rows = part_of(1, 1)
            out.append(go(transfer(tgt.at[k, rows], tgt.at[k, rows], at(kz=3))))
        return out

    ys_p.wait_recv()
    ya = part_of(0, 0)
    yb = part_of(0, 1)
    y2a = go(transfer(tgt.at[3, ya], tgt.at[2, ya], up))
    z3 = z_both(3, own)
    ys_m.wait_recv()
    y2b = go(transfer(tgt.at[1, yb], tgt.at[2, yb], down))
    z1 = z_both(1, own)
    y2_p = go(transfer(target.at[D2], tgt.at[3, D2], up))
    y1_m = go(transfer(target.at[D1], tgt.at[1, D1], down))

    for t in tabs:
        t.wait_recv()
    copy_tab = pltpu.make_async_copy(tab, stab, local_sem.at[2])
    copy_tab.start()

    owner = [(x * 4 + (y + q) % 4) * 2 + c for q in range(4)]

    def block(d, q, r):
        return stab[d, r, owner[q]]

    ones = jnp.full((8, 128), NEG, F32)
    for d in range(8):
        ftab[d * 16 + 8] = ones

    scale = LOG2E / (REG * 16.0)
    eye = jnp.where(
        lax.broadcasted_iota(jnp.int32, (256, 256), 0)
        == lax.broadcasted_iota(jnp.int32, (256, 256), 1), 1.0, 0.0).astype(BF16)

    def unit(q, kx):
        for d in (2 * kx, 2 * kx + 1):
            for r in range(2):
                b = jnp.minimum(block(d, q, r), 7)
                sq[pl.ds(d * 128 + r * 64, 64), :] = src[d][b]
        wide = pl.ds(kx * 256, 256)
        right = sq[wide, :]

        def chunk(j, top):
            rows = pl.ds(pl.multiple_of(j * 256, 256), 256)
            out = lax.dot_general(tgt[q, rows, :], right, NT, preferred_element_type=F32) * scale
            logits[q, rows, wide] = out
            return jnp.maximum(top, jnp.max(out.reshape(32, 8, 256), axis=0))

        top = lax.fori_loop(0, 4, chunk, jnp.full((8, 256), NEG, F32))
        top = jnp.max(top, axis=0, keepdims=True)

        def total(j, sums):
            rows = pl.ds(pl.multiple_of(j * 512, 512), 512)
            p = jnp.exp2(logits[q, rows, wide] - top)
            return sums + jnp.sum(p.reshape(64, 8, 256), axis=0)

        sums = lax.fori_loop(0, 2, total, jnp.zeros((8, 256), F32))
        rmax[q, 0:1, wide] = top
        rsum[q, 0:1, wide] = jnp.sum(sums, axis=0, keepdims=True)

    def turn(q):
        def body(j, _):
            rows = pl.ds(pl.multiple_of(j * 512, 512), 512)
            out = lax.dot_general(eye, tgt[q, rows, :], NT, preferred_element_type=F32)
            tgt_t[q, :, rows] = out.astype(BF16)
            return 0

        lax.fori_loop(0, 2, body, 0)

    R = 128

    def fold(value, op):
        return op(value.reshape(R // 8, 8, 128), axis=0)

    def lanes(d):
        return pl.ds(d * 128, 128)

    def row_sweeps(q, with_g, keep):
        def shifted(rows):
            if with_g:
                g = gcol[q, rows, :]
                return [logits[q, rows, lanes(d)] + g for d in range(8)]
            return [logits[q, rows, lanes(d)] for d in range(8)]

        def first(i, tops):
            rows = pl.ds(pl.multiple_of(i * R, R), R)
            return tuple(jnp.maximum(t, fold(v, jnp.max)) for t, v in zip(tops, shifted(rows)))

        tops = lax.fori_loop(0, 1024 // R, first, (jnp.full((8, 128), NEG, F32),) * 8)
        tops = [jnp.max(t, axis=0, keepdims=True) for t in tops]

        def second(i, sums):
            rows = pl.ds(pl.multiple_of(i * R, R), R)
            new = []
            for d, v in enumerate(shifted(rows)):
                p = jnp.exp2(v - tops[d])
                if keep:
                    weights[q, rows, lanes(d)] = p.astype(BF16)
                new.append(sums[d] + fold(p, jnp.sum))
            return tuple(new)

        sums = lax.fori_loop(0, 1024 // R, second, (jnp.zeros((8, 128), F32),) * 8)
        for d in range(8):
            rmax[q, 0:1, lanes(d)] = tops[d]
            rsum[q, 0:1, lanes(d)] = jnp.sum(sums[d], axis=0, keepdims=True)

    def row_local(phase):
        packed = [None] * 4
        for d in range(8):
            terms = []
            for q in range(4):
                v = rmax[q, 0:1, lanes(d)] + jnp.log2(rsum[q, 0:1, lanes(d)])
                w = pltpu.roll(v, 64, 1)
                terms.append(jnp.where(sub == block(d, q, 0), jnp.where(low1, v, w), NEG))
                terms.append(jnp.where(sub == block(d, q, 1), jnp.where(low1, w, v), NEG))
            out = lse(terms)
            if d % 2 == 0:
                packed[d // 2] = out
            else:
                rowbuf[phase, 0, d // 2] = jnp.where(low, packed[d // 2], out)

    def row_start(phase):
        copies = []
        for kx, kc in row_peers:
            slot = ((-kx) % 4) * 2 + kc
            copies.append(go(transfer(rowbuf.at[phase, 0], rowbuf.at[phase, slot], at(kx=kx, kc=kc))))
        return copies

    def row_finish(phase, copies):
        for t in copies:
            t.wait_recv()
        for i in range(4):
            terms = [rowbuf[phase, 0, i]]
            for kx, kc in row_peers:
                v = rowbuf[phase, kx * 2 + kc, (i - kx) % 4]
                terms.append(pltpu.roll(v, 64, 1) if kc else v)
            total = -lse(terms)
            other = pltpu.roll(total, 64, 1)
            even = jnp.where(low, total, other)
            odd = jnp.where(low, other, total)
            for b in range(8):
                ftab[32 * i + b] = jnp.broadcast_to(even[b:b + 1], (8, 128))
                ftab[32 * i + 16 + b] = jnp.broadcast_to(odd[b:b + 1], (8, 128))

    def row_spread():
        for q in range(4):
            for d in range(8):
                f0 = ftab[d * 16 + block(d, q, 0)]
                f1 = ftab[d * 16 + block(d, q, 1)]
                frow[q, :, lanes(d)] = jnp.where(low, f0, f1)

    diag = (lax.broadcasted_iota(jnp.int32, (128, 128), 0)
            == lax.broadcasted_iota(jnp.int32, (128, 128), 1))
    C = 64

    def column(q, phase):
        fs = [frow[q, 0:1, lanes(d)] for d in range(8)]

        def body(i, _):
            rows = pl.ds(pl.multiple_of(i * C, C), C)
            ts = [logits[q, rows, lanes(d)] + fs[d] for d in range(8)]
            m = functools.reduce(jnp.maximum, ts)
            cmax[rows, :] = m
            csum[rows, :] = functools.reduce(jnp.add, [jnp.exp2(t - m) for t in ts])
            return 0

        lax.fori_loop(0, 1024 // C, body, 0)

        def merge(h, _):
            rows = pl.ds(pl.multiple_of(h * 512, 512), 512)
            m = cmax[rows, :]
            top = jnp.max(m, axis=1, keepdims=True)
            total = jnp.sum(csum[rows, :] * jnp.exp2(m - top), axis=1, keepdims=True)
            out = top + jnp.log2(total)
            lines = []
            for i in range(4):
                spread = jnp.broadcast_to(out[i * 128:(i + 1) * 128], (128, 128))
                lines.append(jnp.sum(jnp.where(diag, spread, 0.0), axis=0, keepdims=True))
            colbuf[phase, 0, q, pl.ds(pl.multiple_of(h * 4, 4), 4), :] = jnp.concatenate(lines, axis=0)
            return 0

        lax.fori_loop(0, 2, merge, 0)

    def column_exchange(phase):
        copies = []
        for k in (1, 2, 3):
            copies.append(go(transfer(colbuf.at[phase, 0], colbuf.at[phase, (-k) % 4], at(ky=k))))
        for t in copies:
            t.wait_recv()
        for q in range(4):
            terms = [colbuf[phase, k, (q - k) % 4] for k in range(4)]
            ztot[phase, 0, q] = lse(terms)
        copies = []
        for k in (1, 2, 3):
            copies.append(go(transfer(ztot.at[phase, 0], ztot.at[phase, (-k) % 4], at(kz=k))))
        for t in copies:
            t.wait_recv()
        last = phase == ITERS - 1
        for q in range(4):
            terms = [ztot[phase, (z - side + 4) % 4, q] for z in range(4)]
            total = -lse(terms)
            if last and q == 0:
                g_out[...] = total * (REG * LN2)
            for h in range(2):
                cols = []
                for i in range(4):
                    line = jnp.broadcast_to(total[h * 4 + i:h * 4 + i + 1], (128, 128))
                    cols.append(jnp.sum(jnp.where(diag, line, 0.0), axis=1, keepdims=True))
                for i in range(4):
                    gcol[q, pl.ds((h * 4 + i) * 128, 128), :] = jnp.broadcast_to(cols[i], (128, 128))

    own_src.wait()
    own_tgt.wait()
    s_c.wait_recv()
    copy_tab.wait()
    unit(0, 0)
    y1_p.wait_recv()
    y21 = go(transfer(tgt.at[3, D1], tgt.at[2, D1], up))
    y2_m.wait_recv()
    y22 = go(transfer(tgt.at[1, D2], tgt.at[2, D2], down))
    y2a.wait_recv()
    z2a = z_both(2, ya)
    y2b.wait_recv()
    z2b = z_both(2, yb)
    s_p.wait_recv()
    s_fp = go(transfer(src[6].at[pl.ds(0, 4)], src[4].at[pl.ds(0, 4)], at(kx=1)))
    s_cp = go(transfer(src[6], src[7], at(kc=1)))
    s_m.wait_recv()
    s_fm = go(transfer(src[2].at[pl.ds(4, 4)], src[4].at[pl.ds(4, 4)], at(kx=3)))
    s_cm = go(transfer(src[2], src[3], at(kc=1)))
    z3f = z_on(3, *z3)
    z1f = z_on(1, *z1)
    s_cp.wait_recv()
    unit(0, 3)
    s_cm.wait_recv()
    z2f = z_on(2, z2a[0], z2b[1])
    s_fp.wait_recv()
    s_fm.wait_recv()
    s_c2 = go(transfer(src[4], src[5], at(kc=1)))
    unit(0, 1)
    for t in (y2_p, *z3f):
        t.wait_recv()
    for kx in (0, 1, 3):
        unit(3, kx)
    for t in (y1_m, *z1f):
        t.wait_recv()
    for kx in (0, 1, 3):
        unit(1, kx)
    s_c2.wait_recv()
    for q in (0, 1, 3):
        unit(q, 2)
    for t in (y21, y22, z2a[1], z2b[0], *z2f):
        t.wait_recv()
    for kx in range(4):
        unit(2, kx)

    for phase in range(ITERS):
        if phase > 0:
            for q in range(4):
                row_sweeps(q, True, False)
        row_local(phase)
        copies = row_start(phase)
        if phase == 0:
            for q in range(4):
                turn(q)
        row_finish(phase, copies)
        row_spread()
        if phase == ITERS - 1:
            even = jnp.concatenate([ftab[2 * i][0:1] for i in range(4)], axis=0)
            odd = jnp.concatenate([ftab[2 * i + 1][0:1] for i in range(4)], axis=0)
            f_out[...] = jnp.where(low[0:4], even, odd) * (REG * LN2)
        for q in range(4):
            column(q, phase)
        column_exchange(phase)

    for q in range(4):
        row_sweeps(q, True, True)
    row_local(ITERS)
    copies = row_start(ITERS)

    def numerators(q):
        def chunk(g, _):
            cols = pl.ds(pl.multiple_of(g * 256, 256), 256)
            numer[q, :, cols] = jnp.dot(tgt_t[q], weights[q, :, cols], preferred_element_type=F32)
            return 0

        lax.fori_loop(0, 4, chunk, 0)

    for q in range(4):
        numerators(q)
    row_finish(ITERS, copies)
    row_spread()

    row_id = lax.broadcasted_iota(jnp.int32, (512, 128), 0)
    col_id = lax.broadcasted_iota(jnp.int32, (512, 128), 1)
    same = (row_id % 64) == (col_id % 64)
    row_block = row_id // 64

    def assemble(d):
        picks, values = [], []
        for q in range(4):
            chosen = jnp.where(low1, block(d, q, 0), block(d, q, 1))
            hit = jnp.logical_and(same, row_block == chosen)
            picks.append(jnp.where(hit, 1.0, 0.0).astype(BF16))
            factor = jnp.exp2(rmax[q, 0:1, lanes(d)] + frow[q, 0:1, lanes(d)])
            values.append((numer[q, :, lanes(d)] * factor).astype(BF16))
        pick = jnp.concatenate(picks, axis=1)
        value = jnp.concatenate(values, axis=1)
        part[d] = lax.dot_general(pick, value, NT, preferred_element_type=F32).astype(BF16)

    def plus(*refs):
        return functools.reduce(jnp.add, [r[...].astype(F32) for r in refs])

    halves = (A, B)
    to_core = {}

    def give(kx):
        assemble(kx * 2 + 1)
        to_core[kx] = go(transfer(part.at[kx * 2 + 1], pin.at[kx], at(kc=1)))

    give(2)
    assemble(4)
    give(1)
    to_core[2].wait_recv()
    comb[2] = plus(part.at[4], pin.at[2]).astype(BF16)
    h_p = go(transfer(comb.at[2, A], hin.at[0], at(kx=1)))
    h_m = go(transfer(comb.at[2, B], hin.at[1], at(kx=3)))
    give(3)
    assemble(2)
    to_core[1].wait_recv()
    comb[1, B] = plus(part.at[2, B], pin.at[1, B]).astype(BF16)
    r_pb = go(transfer(comb.at[1, B], rin.at[0, B], at(kx=1)))
    assemble(6)
    to_core[3].wait_recv()
    comb[3, A] = plus(part.at[6, A], pin.at[3, A]).astype(BF16)
    r_ma = go(transfer(comb.at[3, A], rin.at[1, A], at(kx=3)))
    give(0)
    h_p.wait_recv()
    comb[1, A] = plus(part.at[2, A], pin.at[1, A], hin.at[0]).astype(BF16)
    r_pa = go(transfer(comb.at[1, A], rin.at[0, A], at(kx=1)))
    h_m.wait_recv()
    comb[3, B] = plus(part.at[6, B], pin.at[3, B], hin.at[1]).astype(BF16)
    r_mb = go(transfer(comb.at[3, B], rin.at[1, B], at(kx=3)))
    assemble(0)
    to_core[0].wait_recv()
    for t in (r_pb, r_ma, r_pa, r_mb):
        t.wait_recv()
    mapped[...] = plus(part.at[0], pin.at[0], rin.at[0], rin.at[1]).astype(BF16)

    for t in sent:
        t.wait_send()


COPIES = 7 + 8 + 24 + 7 * (ITERS + 1) + 6 * ITERS + 4 + 6


def shards(source, target, pairs, owner_map):
    any_space = pl.BlockSpec(memory_space=pl.ANY)
    smem = pl.BlockSpec(memory_space=pltpu.SMEM)
    vmem = pl.BlockSpec(memory_space=pltpu.VMEM)
    f, g, mapped = pl.pallas_call(
        kernel,
        out_shape=(
            jax.ShapeDtypeStruct((4, 128), F32),
            jax.ShapeDtypeStruct((8, 128), F32),
            jax.ShapeDtypeStruct((512, 256), BF16),
        ),
        in_specs=[any_space, any_space, smem, smem],
        out_specs=(vmem, vmem, vmem),
        scratch_shapes=[
            *[pltpu.VMEM((8, 64, 256), BF16)] * 8,
            pltpu.VMEM((4, 1024, 256), BF16),
            pltpu.VMEM((8, 8, 128), jnp.int32),
            pltpu.SMEM((8, 8, 128), jnp.int32),
            pltpu.VMEM((1024, 256), BF16),
            pltpu.VMEM((4, 1024, 1024), F32),
            pltpu.VMEM((4, 1024, 1024), BF16),
            pltpu.VMEM((4, 256, 1024), BF16),
            pltpu.VMEM((4, 1024, 128), F32),
            pltpu.VMEM((1024, 128), F32),
            pltpu.VMEM((1024, 128), F32),
            pltpu.VMEM((4, 8, 1024), F32),
            pltpu.VMEM((4, 8, 1024), F32),
            pltpu.VMEM((ITERS + 1, 8, 4, 8, 128), F32),
            pltpu.VMEM((128, 8, 128), F32),
            pltpu.VMEM((4, 8, 1024), F32),
            pltpu.VMEM((ITERS, 4, 4, 8, 128), F32),
            pltpu.VMEM((ITERS, 4, 4, 8, 128), F32),
            pltpu.VMEM((4, 256, 1024), F32),
            pltpu.VMEM((8, 512, 256), BF16),
            pltpu.VMEM((4, 512, 256), BF16),
            pltpu.VMEM((4, 512, 256), BF16),
            pltpu.VMEM((2, 512, 256), BF16),
            pltpu.VMEM((2, 256, 256), BF16),
            pltpu.SemaphoreType.DMA((COPIES,)),
            pltpu.SemaphoreType.DMA((COPIES,)),
            pltpu.SemaphoreType.DMA((3,)),
        ],
        compiler_params=pltpu.CompilerParams(
            collective_id=0, has_side_effects=True, vmem_limit_bytes=60 * 1024 * 1024
        ),
        name="sinkhorn",
    )(source.reshape(8, 64, 256), target, pairs.T, owner_map)
    return f.reshape(512), g.reshape(1024), mapped


def solution(mesh):
    return jax.shard_map(
        shards,
        mesh=mesh,
        in_specs=(P(("side", "blk"), None), P("blk", None), P(("side", "blk"), None), P()),
        out_specs=(P(("side", "blk")), P("blk"), P(("side", "blk"), None)),
        check_vma=False,
    )
```

```python
import functools
import math

import jax
import jax.numpy as jnp
from jax import lax
from jax.experimental import pallas as pl
from jax.experimental.pallas import tpu as pltpu
from jax.sharding import PartitionSpec as P

MESH = pl.DeviceIdType.MESH
NEG = -1e30
LOG2E = 1.4426950408889634
LN2 = 0.6931471805599453
REG = 0.3
ITERS = 2
NT = (((1,), (1,)), ((), ()))
F32 = jnp.float32
BF16 = jnp.bfloat16


def lse(parts):
    top = functools.reduce(jnp.maximum, parts)
    total = functools.reduce(jnp.add, [jnp.exp2(p - top) for p in parts])
    return top + jnp.log2(total)


def kernel(
    source, target, pairs, owner_map, f_out, g_out, mapped,
    src0, src1, src2, src3, src4, src5, src6, src7, tgt, tab, stab, sq, logits, weights, tgt_t, gcol, cmax, csum,
    rmax, rsum, rowbuf, ftab, frow, colbuf, ztot, gpack, numer, part, comb, pin, rin,
    hin, send_sem, recv_sem, local_sem,
):
    src = (src0, src1, src2, src3, src4, src5, src6, src7)
    side = lax.axis_index("side")
    blk = lax.axis_index("blk")
    x = blk // 8
    y = (blk // 2) % 4
    c = blk % 2

    def at(kx=0, kc=0, ky=0, kz=0):
        xx = (x + kx) % 4
        yy = (y + ky) % 4
        cc = (c + kc) % 2
        zz = (side + kz) % 4
        return (zz, (xx * 4 + yy) * 2 + cc)

    def yi(k):
        return (y + k) % 4

    count = [0]

    def transfer(source_ref, dest_ref, device):
        n = count[0]
        count[0] += 1
        return pltpu.make_async_remote_copy(
            src_ref=source_ref, dst_ref=dest_ref,
            send_sem=send_sem.at[n], recv_sem=recv_sem.at[n],
            device_id=device, device_id_type=MESH,
        )

    sent = []

    def go(copy):
        copy.start()
        sent.append(copy)
        return copy

    row_peers = [(kx, kc) for kx in range(4) for kc in range(2)][1:]
    peers = [at(kx=kx, kc=kc) for kx, kc in row_peers]
    peers += [at(ky=k) for k in (1, 2, 3)] + [at(kz=k) for k in (1, 2, 3)]
    barrier = pltpu.get_barrier_semaphore()
    for peer in peers:
        pl.semaphore_signal(barrier, inc=1, device_id=peer, device_id_type=MESH)

    own_src = pltpu.make_async_copy(source, src[0], local_sem.at[0])
    own_src.start()
    own_tgt = pltpu.make_async_copy(target, tgt.at[y], local_sem.at[1])
    own_tgt.start()

    lane = lax.broadcasted_iota(jnp.int32, (8, 128), 1)
    sub = lax.broadcasted_iota(jnp.int32, (8, 128), 0)
    low = lane < 64
    low1 = low[0:1]

    seen = jnp.zeros((8, 128), jnp.int32)
    table = jnp.full((8, 128), 8, jnp.int32)
    for s in range(8):
        hit = lane == owner_map[pairs[0, s]]
        for k in range(1, 4):
            hit = jnp.logical_or(hit, lane == owner_map[pairs[k, s]])
        table = jnp.where(jnp.logical_and(hit, seen == sub), s, table)
        seen = seen + jnp.where(hit, 1, 0)
    tab[0] = table

    pl.semaphore_wait(barrier, len(peers))

    A, B = pl.ds(0, 256), pl.ds(256, 256)
    tabs = []
    for kx, kc in row_peers:
        slot = ((-kx) % 4) * 2 + kc
        tabs.append(go(transfer(tab.at[0], tab.at[slot], at(kx=kx, kc=kc))))

    D1, D2 = pl.ds(0, 192), pl.ds(192, 192)

    def part_of(kz, half=None):
        start = 384 + 160 * ((side + kz) % 4)
        if half is None:
            return pl.ds(pl.multiple_of(start, 32), 160)
        return pl.ds(pl.multiple_of(start + 80 * half, 16), 80)

    own = part_of(0)
    up, down = at(ky=1), at(ky=3)
    s_p = go(transfer(source, src[6], at(kx=1)))
    s_m = go(transfer(source, src[2], at(kx=3)))
    ys_p = go(transfer(target.at[own], tgt.at[y, own], up))
    ys_m = go(transfer(target.at[own], tgt.at[y, own], down))
    y1_p = go(transfer(target.at[D1], tgt.at[y, D1], up))
    y2_m = go(transfer(target.at[D2], tgt.at[y, D2], down))
    s_c = go(transfer(source, src[1], at(kc=1)))

    def z_both(k, rows):
        return (go(transfer(tgt.at[yi(k), rows], tgt.at[yi(k), rows], at(kz=1))),
                go(transfer(tgt.at[yi(k), rows], tgt.at[yi(k), rows], at(kz=3))))

    def z_on(k, z_p, z_m):
        out = []
        if z_p is not None:
            z_p.wait_recv()
            rows = part_of(3, 0)
            out.append(go(transfer(tgt.at[yi(k), rows], tgt.at[yi(k), rows], at(kz=1))))
        if z_m is not None:
            z_m.wait_recv()
            rows = part_of(1, 1)
            out.append(go(transfer(tgt.at[yi(k), rows], tgt.at[yi(k), rows], at(kz=3))))
        return out

    ys_p.wait_recv()
    ya = part_of(0, 0)
    yb = part_of(0, 1)
    y2a = go(transfer(tgt.at[yi(3), ya], tgt.at[yi(3), ya], up))
    z3 = z_both(3, own)
    ys_m.wait_recv()
    y2b = go(transfer(tgt.at[yi(1), yb], tgt.at[yi(1), yb], down))
    z1 = z_both(1, own)
    y2_p = go(transfer(target.at[D2], tgt.at[y, D2], up))
    y1_m = go(transfer(target.at[D1], tgt.at[y, D1], down))

    for t in tabs:
        t.wait_recv()
    copy_tab = pltpu.make_async_copy(tab, stab, local_sem.at[2])
    copy_tab.start()

    def block(d, q, r):
        return stab[d, r, (x * 4 + q) * 2 + c]

    ones = jnp.full((8, 128), NEG, F32)
    for d in range(8):
        ftab[d * 16 + 8] = ones

    scale = LOG2E / (REG * 16.0)
    eye = jnp.where(
        lax.broadcasted_iota(jnp.int32, (256, 256), 0)
        == lax.broadcasted_iota(jnp.int32, (256, 256), 1), 1.0, 0.0).astype(BF16)

    def unit(ky, kx):
        q = yi(ky)
        for d in (2 * kx, 2 * kx + 1):
            for r in range(2):
                b = jnp.minimum(block(d, q, r), 7)
                sq[pl.ds(d * 128 + r * 64, 64), :] = src[d][b]
        wide = pl.ds(kx * 256, 256)
        out = lax.dot_general(tgt[q], sq[wide, :], NT, preferred_element_type=F32) * scale
        logits[q, :, wide] = out
        top = jnp.max(jnp.max(out.reshape(128, 8, 256), axis=0), axis=0, keepdims=True)

        def total(j, sums):
            rows = pl.ds(pl.multiple_of(j * 512, 512), 512)
            p = jnp.exp2(logits[q, rows, wide] - top)
            return sums + jnp.sum(p.reshape(64, 8, 256), axis=0)

        sums = lax.fori_loop(0, 2, total, jnp.zeros((8, 256), F32))
        rmax[q, 0:1, wide] = top
        rsum[q, 0:1, wide] = jnp.sum(sums, axis=0, keepdims=True)

    def turn(q):
        def body(j, _):
            rows = pl.ds(pl.multiple_of(j * 512, 512), 512)
            out = lax.dot_general(eye, tgt[q, rows, :], NT, preferred_element_type=F32)
            tgt_t[q, :, rows] = out.astype(BF16)
            return 0

        lax.fori_loop(0, 2, body, 0)

    R = 128

    def fold(value, op):
        return op(value.reshape(R // 8, 8, 128), axis=0)

    def lanes(d):
        return pl.ds(d * 128, 128)

    def row_single(q):
        def body(i, carry):
            rows = pl.ds(pl.multiple_of(i * R, R), R)
            g = gcol[q, rows, :]
            new = []
            for d in range(8):
                m, total = carry[d]
                t = logits[q, rows, lanes(d)] + g
                top = jnp.maximum(m, fold(t, jnp.max))
                p = jnp.exp2(t.reshape(R // 8, 8, 128) - top)
                new.append((top, total * jnp.exp2(m - top) + jnp.sum(p, axis=0)))
            return tuple(new)

        start = (jnp.full((8, 128), NEG, F32), jnp.zeros((8, 128), F32))
        done = lax.fori_loop(0, 1024 // R, body, (start,) * 8)
        for d, (m, total) in enumerate(done):
            top = jnp.max(m, axis=0, keepdims=True)
            rmax[q, 0:1, lanes(d)] = top
            rsum[q, 0:1, lanes(d)] = jnp.sum(total * jnp.exp2(m - top), axis=0, keepdims=True)

    def row_sweeps(q, with_g, keep):
        def shifted(rows):
            if with_g:
                g = gcol[q, rows, :]
                return [logits[q, rows, lanes(d)] + g for d in range(8)]
            return [logits[q, rows, lanes(d)] for d in range(8)]

        def first(i, tops):
            rows = pl.ds(pl.multiple_of(i * R, R), R)
            return tuple(jnp.maximum(t, fold(v, jnp.max)) for t, v in zip(tops, shifted(rows)))

        tops = lax.fori_loop(0, 1024 // R, first, (jnp.full((8, 128), NEG, F32),) * 8)
        tops = [jnp.max(t, axis=0, keepdims=True) for t in tops]

        def second(i, sums):
            rows = pl.ds(pl.multiple_of(i * R, R), R)
            new = []
            for d, v in enumerate(shifted(rows)):
                p = jnp.exp2(v - tops[d])
                if keep:
                    weights[q, rows, lanes(d)] = p.astype(BF16)
                new.append(sums[d] + fold(p, jnp.sum))
            return tuple(new)

        sums = lax.fori_loop(0, 1024 // R, second, (jnp.zeros((8, 128), F32),) * 8)
        for d in range(8):
            rmax[q, 0:1, lanes(d)] = tops[d]
            rsum[q, 0:1, lanes(d)] = jnp.sum(sums[d], axis=0, keepdims=True)

    def row_local(phase):
        packed = [None] * 4
        for d in range(8):
            terms = []
            for q in range(4):
                v = rmax[q, 0:1, lanes(d)] + jnp.log2(rsum[q, 0:1, lanes(d)])
                w = pltpu.roll(v, 64, 1)
                terms.append(jnp.where(sub == block(d, q, 0), jnp.where(low1, v, w), NEG))
                terms.append(jnp.where(sub == block(d, q, 1), jnp.where(low1, w, v), NEG))
            out = lse(terms)
            if d % 2 == 0:
                packed[d // 2] = out
            else:
                rowbuf[phase, 0, d // 2] = jnp.where(low, packed[d // 2], out)

    def row_start(phase):
        copies = []
        for kx, kc in row_peers:
            slot = ((-kx) % 4) * 2 + kc
            copies.append(go(transfer(rowbuf.at[phase, 0], rowbuf.at[phase, slot], at(kx=kx, kc=kc))))
        return copies

    def row_finish(phase, copies):
        for t in copies:
            t.wait_recv()
        for i in range(4):
            terms = [rowbuf[phase, 0, i]]
            for kx, kc in row_peers:
                v = rowbuf[phase, kx * 2 + kc, (i - kx) % 4]
                terms.append(pltpu.roll(v, 64, 1) if kc else v)
            total = -lse(terms)
            other = pltpu.roll(total, 64, 1)
            even = jnp.where(low, total, other)
            odd = jnp.where(low, other, total)
            for b in range(8):
                ftab[32 * i + b] = jnp.broadcast_to(even[b:b + 1], (8, 128))
                ftab[32 * i + 16 + b] = jnp.broadcast_to(odd[b:b + 1], (8, 128))

    def row_spread():
        for q in range(4):
            for d in range(8):
                f0 = ftab[d * 16 + block(d, q, 0)]
                f1 = ftab[d * 16 + block(d, q, 1)]
                frow[q, :, lanes(d)] = jnp.where(low, f0, f1)

    diag = (lax.broadcasted_iota(jnp.int32, (128, 128), 0)
            == lax.broadcasted_iota(jnp.int32, (128, 128), 1))
    C = 128

    def column(q, phase):
        fs = [frow[q, 0:1, lanes(d)] for d in range(8)]

        def body(i, _):
            rows = pl.ds(pl.multiple_of(i * C, C), C)
            ts = [logits[q, rows, lanes(d)] + fs[d] for d in range(8)]
            m = functools.reduce(jnp.maximum, ts)
            cmax[rows, :] = m
            csum[rows, :] = functools.reduce(jnp.add, [jnp.exp2(t - m) for t in ts])
            return 0

        lax.fori_loop(0, 1024 // C, body, 0)

        def merge(h, _):
            rows = pl.ds(pl.multiple_of(h * 512, 512), 512)
            m = cmax[rows, :]
            top = jnp.max(m, axis=1, keepdims=True)
            total = jnp.sum(csum[rows, :] * jnp.exp2(m - top), axis=1, keepdims=True)
            out = top + jnp.log2(total)
            lines = []
            for i in range(4):
                spread = jnp.broadcast_to(out[i * 128:(i + 1) * 128], (128, 128))
                lines.append(jnp.sum(jnp.where(diag, spread, 0.0), axis=0, keepdims=True))
            colbuf[phase, 0, q, pl.ds(pl.multiple_of(h * 4, 4), 4), :] = jnp.concatenate(lines, axis=0)
            return 0

        lax.fori_loop(0, 2, merge, 0)

    def over_y(phase, q):
        return [go(transfer(colbuf.at[phase, 0, q], colbuf.at[phase, (-k) % 4, q], at(ky=k))) for k in (1, 2, 3)]

    def over_z(phase, q, copies):
        for t in copies:
            t.wait_recv()
        ztot[phase, 0, q] = lse([colbuf[phase, k, q] for k in range(4)])
        return [go(transfer(ztot.at[phase, 0, q], ztot.at[phase, (-k) % 4, q], at(kz=k))) for k in (1, 2, 3)]

    def column_done(phase, q, copies):
        for t in copies:
            t.wait_recv()
        total = -lse([ztot[phase, (z - side + 4) % 4, q] for z in range(4)])
        gpack[q] = total
        for h in range(2):
            cols = []
            for i in range(4):
                line = jnp.broadcast_to(total[h * 4 + i:h * 4 + i + 1], (128, 128))
                cols.append(jnp.sum(jnp.where(diag, line, 0.0), axis=1, keepdims=True))
            for i in range(4):
                gcol[q, pl.ds((h * 4 + i) * 128, 128), :] = jnp.broadcast_to(cols[i], (128, 128))

    def columns_then_rows(phase):
        ys, zs = {}, {}
        for q in range(4):
            column(q, phase)
            ys[q] = over_y(phase, q)
            if q >= 2:
                zs[q - 2] = over_z(phase, q - 2, ys[q - 2])
        zs[2] = over_z(phase, 2, ys[2])
        for q in range(4):
            column_done(phase, q, zs[q])
            if phase == ITERS - 1:
                row_sweeps(q, True, True)
            else:
                row_single(q)
            if q == 0:
                zs[3] = over_z(phase, 3, ys[3])

    own_src.wait()
    own_tgt.wait()
    s_c.wait_recv()
    copy_tab.wait()
    unit(0, 0)
    y1_p.wait_recv()
    y21 = go(transfer(tgt.at[yi(3), D1], tgt.at[yi(3), D1], up))
    y2_m.wait_recv()
    y22 = go(transfer(tgt.at[yi(1), D2], tgt.at[yi(1), D2], down))
    y2a.wait_recv()
    z2a = z_both(2, ya)
    y2b.wait_recv()
    z2b = z_both(2, yb)
    s_p.wait_recv()
    s_fp = go(transfer(src[6].at[pl.ds(0, 4)], src[4].at[pl.ds(0, 4)], at(kx=1)))
    s_cp = go(transfer(src[6], src[7], at(kc=1)))
    s_m.wait_recv()
    s_fm = go(transfer(src[2].at[pl.ds(4, 4)], src[4].at[pl.ds(4, 4)], at(kx=3)))
    s_cm = go(transfer(src[2], src[3], at(kc=1)))
    z3f = z_on(3, *z3)
    z1f = z_on(1, *z1)
    s_cp.wait_recv()
    unit(0, 3)
    s_cm.wait_recv()
    z2f = z_on(2, z2a[0], z2b[1])
    s_fp.wait_recv()
    s_fm.wait_recv()
    s_c2 = go(transfer(src[4], src[5], at(kc=1)))
    unit(0, 1)
    for t in (y2_p, *z3f):
        t.wait_recv()
    for kx in (0, 1, 3):
        unit(3, kx)
    for t in (y1_m, *z1f):
        t.wait_recv()
    for kx in (0, 1, 3):
        unit(1, kx)
    s_c2.wait_recv()
    for q in (0, 1, 3):
        unit(q, 2)
    for t in (y21, y22, z2a[1], z2b[0], *z2f):
        t.wait_recv()
    for kx in range(4):
        unit(2, kx)

    for phase in range(ITERS):
        row_local(phase)
        copies = row_start(phase)
        if phase == 0:
            for q in range(4):
                turn(q)
        row_finish(phase, copies)
        row_spread()
        if phase == ITERS - 1:
            even = jnp.concatenate([ftab[2 * i][0:1] for i in range(4)], axis=0)
            odd = jnp.concatenate([ftab[2 * i + 1][0:1] for i in range(4)], axis=0)
            f_out[...] = jnp.where(low[0:4], even, odd) * (REG * LN2)
        columns_then_rows(phase)

    g_out[...] = gpack[y] * (REG * LN2)
    row_local(ITERS)
    copies = row_start(ITERS)

    def numerators(q):
        def chunk(g, _):
            cols = pl.ds(pl.multiple_of(g * 256, 256), 256)
            numer[q, :, cols] = jnp.dot(tgt_t[q], weights[q, :, cols], preferred_element_type=F32)
            return 0

        lax.fori_loop(0, 4, chunk, 0)

    for q in range(4):
        numerators(q)
    row_finish(ITERS, copies)
    row_spread()

    row_id = lax.broadcasted_iota(jnp.int32, (512, 128), 0)
    col_id = lax.broadcasted_iota(jnp.int32, (512, 128), 1)
    same = (row_id % 64) == (col_id % 64)
    row_block = row_id // 64

    def assemble(d):
        picks, values = [], []
        for q in range(4):
            chosen = jnp.where(low1, block(d, q, 0), block(d, q, 1))
            hit = jnp.logical_and(same, row_block == chosen)
            picks.append(jnp.where(hit, 1.0, 0.0).astype(BF16))
            factor = jnp.exp2(rmax[q, 0:1, lanes(d)] + frow[q, 0:1, lanes(d)])
            values.append((numer[q, :, lanes(d)] * factor).astype(BF16))
        pick = jnp.concatenate(picks, axis=1)
        value = jnp.concatenate(values, axis=1)
        part[d] = lax.dot_general(pick, value, NT, preferred_element_type=F32).astype(BF16)

    def plus(*refs):
        return functools.reduce(jnp.add, [r[...].astype(F32) for r in refs])

    halves = (A, B)
    to_core = {}

    def give(kx):
        assemble(kx * 2 + 1)
        to_core[kx] = go(transfer(part.at[kx * 2 + 1], pin.at[kx], at(kc=1)))

    give(2)
    assemble(4)
    give(1)
    to_core[2].wait_recv()
    comb[2] = plus(part.at[4], pin.at[2]).astype(BF16)
    h_p = go(transfer(comb.at[2, A], hin.at[0], at(kx=1)))
    h_m = go(transfer(comb.at[2, B], hin.at[1], at(kx=3)))
    give(3)
    assemble(2)
    to_core[1].wait_recv()
    comb[1, B] = plus(part.at[2, B], pin.at[1, B]).astype(BF16)
    r_pb = go(transfer(comb.at[1, B], rin.at[0, B], at(kx=1)))
    assemble(6)
    to_core[3].wait_recv()
    comb[3, A] = plus(part.at[6, A], pin.at[3, A]).astype(BF16)
    r_ma = go(transfer(comb.at[3, A], rin.at[1, A], at(kx=3)))
    give(0)
    h_p.wait_recv()
    comb[1, A] = plus(part.at[2, A], pin.at[1, A], hin.at[0]).astype(BF16)
    r_pa = go(transfer(comb.at[1, A], rin.at[0, A], at(kx=1)))
    h_m.wait_recv()
    comb[3, B] = plus(part.at[6, B], pin.at[3, B], hin.at[1]).astype(BF16)
    r_mb = go(transfer(comb.at[3, B], rin.at[1, B], at(kx=3)))
    assemble(0)
    to_core[0].wait_recv()
    for t in (r_pb, r_ma, r_pa, r_mb):
        t.wait_recv()
    mapped[...] = plus(part.at[0], pin.at[0], rin.at[0], rin.at[1]).astype(BF16)

    for t in sent:
        t.wait_send()


COPIES = 7 + 8 + 24 + 7 * (ITERS + 1) + 24 * ITERS + 4 + 6


def shards(source, target, pairs, owner_map):
    any_space = pl.BlockSpec(memory_space=pl.ANY)
    smem = pl.BlockSpec(memory_space=pltpu.SMEM)
    vmem = pl.BlockSpec(memory_space=pltpu.VMEM)
    f, g, mapped = pl.pallas_call(
        kernel,
        out_shape=(
            jax.ShapeDtypeStruct((4, 128), F32),
            jax.ShapeDtypeStruct((8, 128), F32),
            jax.ShapeDtypeStruct((512, 256), BF16),
        ),
        in_specs=[any_space, any_space, smem, smem],
        out_specs=(vmem, vmem, vmem),
        scratch_shapes=[
            *[pltpu.VMEM((8, 64, 256), BF16)] * 8,
            pltpu.VMEM((4, 1024, 256), BF16),
            pltpu.VMEM((8, 8, 128), jnp.int32),
            pltpu.SMEM((8, 8, 128), jnp.int32),
            pltpu.VMEM((1024, 256), BF16),
            pltpu.VMEM((4, 1024, 1024), F32),
            pltpu.VMEM((4, 1024, 1024), BF16),
            pltpu.VMEM((4, 256, 1024), BF16),
            pltpu.VMEM((4, 1024, 128), F32),
            pltpu.VMEM((1024, 128), F32),
            pltpu.VMEM((1024, 128), F32),
            pltpu.VMEM((4, 8, 1024), F32),
            pltpu.VMEM((4, 8, 1024), F32),
            pltpu.VMEM((ITERS + 1, 8, 4, 8, 128), F32),
            pltpu.VMEM((128, 8, 128), F32),
            pltpu.VMEM((4, 8, 1024), F32),
            pltpu.VMEM((ITERS, 4, 4, 8, 128), F32),
            pltpu.VMEM((ITERS, 4, 4, 8, 128), F32),
            pltpu.VMEM((4, 8, 128), F32),
            pltpu.VMEM((4, 256, 1024), F32),
            pltpu.VMEM((8, 512, 256), BF16),
            pltpu.VMEM((4, 512, 256), BF16),
            pltpu.VMEM((4, 512, 256), BF16),
            pltpu.VMEM((2, 512, 256), BF16),
            pltpu.VMEM((2, 256, 256), BF16),
            pltpu.SemaphoreType.DMA((COPIES,)),
            pltpu.SemaphoreType.DMA((COPIES,)),
            pltpu.SemaphoreType.DMA((3,)),
        ],
        compiler_params=pltpu.CompilerParams(
            collective_id=0, has_side_effects=True, vmem_limit_bytes=60 * 1024 * 1024
        ),
        name="sinkhorn",
    )(source.reshape(8, 64, 256), target, pairs.T, owner_map)
    return f.reshape(512), g.reshape(1024), mapped


def solution(mesh):
    return jax.shard_map(
        shards,
        mesh=mesh,
        in_specs=(P(("side", "blk"), None), P("blk", None), P(("side", "blk"), None), P()),
        out_specs=(P(("side", "blk")), P("blk"), P(("side", "blk"), None)),
        check_vma=False,
    )
```

```python
import functools
import math

import jax
import jax.numpy as jnp
from jax import lax
from jax.experimental import pallas as pl
from jax.experimental.pallas import tpu as pltpu
from jax.sharding import PartitionSpec as P

MESH = pl.DeviceIdType.MESH
NEG = -1e30
LOG2E = 1.4426950408889634
LN2 = 0.6931471805599453
REG = 0.3
ITERS = 2
NT = (((1,), (1,)), ((), ()))
F32 = jnp.float32
BF16 = jnp.bfloat16


def lse(parts):
    top = functools.reduce(jnp.maximum, parts)
    total = functools.reduce(jnp.add, [jnp.exp2(p - top) for p in parts])
    return top + jnp.log2(total)


def kernel(
    source, target, pairs, owner_map, f_out, g_out, mapped,
    src0, src1, src2, src3, src4, src5, src6, src7, tgt, tab, stab, sq, logits, weights, tgt_t, gcol, cmax, csum,
    rmax, rsum, rowbuf, ftab, ltab, frow, colbuf, ztot, gpack, numer, part, comb, pin, rin, hin,
    stat, cstat, pstat, rstat, hstat, send_sem, recv_sem, local_sem,
):
    src = (src0, src1, src2, src3, src4, src5, src6, src7)
    side = lax.axis_index("side")
    blk = lax.axis_index("blk")
    x = blk // 8
    y = (blk // 2) % 4
    c = blk % 2

    def at(kx=0, kc=0, ky=0, kz=0):
        xx = (x + kx) % 4
        yy = (y + ky) % 4
        cc = (c + kc) % 2
        zz = (side + kz) % 4
        return (zz, (xx * 4 + yy) * 2 + cc)

    def yi(k):
        return (y + k) % 4

    count = [0]

    def transfer(source_ref, dest_ref, device):
        n = count[0]
        count[0] += 1
        return pltpu.make_async_remote_copy(
            src_ref=source_ref, dst_ref=dest_ref,
            send_sem=send_sem.at[n], recv_sem=recv_sem.at[n],
            device_id=device, device_id_type=MESH,
        )

    sent = []

    def go(copy):
        copy.start()
        sent.append(copy)
        return copy

    row_peers = [(kx, kc) for kx in range(4) for kc in range(2)][1:]
    peers = [at(kx=kx, kc=kc) for kx, kc in row_peers]
    peers += [at(ky=k) for k in (1, 2, 3)] + [at(kz=k) for k in (1, 2, 3)]
    barrier = pltpu.get_barrier_semaphore()
    for peer in peers:
        pl.semaphore_signal(barrier, inc=1, device_id=peer, device_id_type=MESH)

    own_src = pltpu.make_async_copy(source, src[0], local_sem.at[0])
    own_src.start()
    own_tgt = pltpu.make_async_copy(target, tgt.at[y], local_sem.at[1])
    own_tgt.start()

    lane = lax.broadcasted_iota(jnp.int32, (8, 128), 1)
    sub = lax.broadcasted_iota(jnp.int32, (8, 128), 0)
    low = lane < 64
    low1 = low[0:1]

    seen = jnp.zeros((8, 128), jnp.int32)
    table = jnp.full((8, 128), 8, jnp.int32)
    for s in range(8):
        hit = lane == owner_map[pairs[0, s]]
        for k in range(1, 4):
            hit = jnp.logical_or(hit, lane == owner_map[pairs[k, s]])
        table = jnp.where(jnp.logical_and(hit, seen == sub), s, table)
        seen = seen + jnp.where(hit, 1, 0)
    tab[0] = table

    pl.semaphore_wait(barrier, len(peers))

    A, B = pl.ds(0, 256), pl.ds(256, 256)
    tabs = []
    for kx, kc in row_peers:
        slot = ((-kx) % 4) * 2 + kc
        tabs.append(go(transfer(tab.at[0], tab.at[slot], at(kx=kx, kc=kc))))

    D1, D2 = pl.ds(0, 192), pl.ds(192, 192)

    def part_of(kz, half=None):
        start = 384 + 160 * ((side + kz) % 4)
        if half is None:
            return pl.ds(pl.multiple_of(start, 32), 160)
        return pl.ds(pl.multiple_of(start + 80 * half, 16), 80)

    own = part_of(0)
    up, down = at(ky=1), at(ky=3)
    s_p = go(transfer(source, src[6], at(kx=1)))
    s_m = go(transfer(source, src[2], at(kx=3)))
    ys_p = go(transfer(target.at[own], tgt.at[y, own], up))
    ys_m = go(transfer(target.at[own], tgt.at[y, own], down))
    y1_p = go(transfer(target.at[D1], tgt.at[y, D1], up))
    y2_m = go(transfer(target.at[D2], tgt.at[y, D2], down))
    s_c = go(transfer(source, src[1], at(kc=1)))

    def z_both(k, rows):
        return (go(transfer(tgt.at[yi(k), rows], tgt.at[yi(k), rows], at(kz=1))),
                go(transfer(tgt.at[yi(k), rows], tgt.at[yi(k), rows], at(kz=3))))

    def z_on(k, z_p, z_m):
        out = []
        if z_p is not None:
            z_p.wait_recv()
            rows = part_of(3, 0)
            out.append(go(transfer(tgt.at[yi(k), rows], tgt.at[yi(k), rows], at(kz=1))))
        if z_m is not None:
            z_m.wait_recv()
            rows = part_of(1, 1)
            out.append(go(transfer(tgt.at[yi(k), rows], tgt.at[yi(k), rows], at(kz=3))))
        return out

    ys_p.wait_recv()
    ya = part_of(0, 0)
    yb = part_of(0, 1)
    y2a = go(transfer(tgt.at[yi(3), ya], tgt.at[yi(3), ya], up))
    z3 = z_both(3, own)
    ys_m.wait_recv()
    y2b = go(transfer(tgt.at[yi(1), yb], tgt.at[yi(1), yb], down))
    z1 = z_both(1, own)
    y2_p = go(transfer(target.at[D2], tgt.at[y, D2], up))
    y1_m = go(transfer(target.at[D1], tgt.at[y, D1], down))

    for t in tabs:
        t.wait_recv()
    copy_tab = pltpu.make_async_copy(tab, stab, local_sem.at[2])
    copy_tab.start()

    def block(d, q, r):
        return stab[d, r, (x * 4 + q) * 2 + c]

    ones = jnp.full((8, 128), NEG, F32)
    for d in range(8):
        ftab[d * 16 + 8] = ones
        ltab[d * 16 + 8] = -ones

    scale = LOG2E / (REG * 16.0)
    eye = jnp.where(
        lax.broadcasted_iota(jnp.int32, (256, 256), 0)
        == lax.broadcasted_iota(jnp.int32, (256, 256), 1), 1.0, 0.0).astype(BF16)

    def unit(ky, kx):
        q = yi(ky)
        for d in (2 * kx, 2 * kx + 1):
            for r in range(2):
                b = jnp.minimum(block(d, q, r), 7)
                sq[pl.ds(d * 128 + r * 64, 64), :] = src[d][b]
        wide = pl.ds(kx * 256, 256)
        out = lax.dot_general(tgt[q], sq[wide, :], NT, preferred_element_type=F32) * scale
        logits[q, :, wide] = out
        top = jnp.max(jnp.max(out.reshape(128, 8, 256), axis=0), axis=0, keepdims=True)

        def total(j, sums):
            rows = pl.ds(pl.multiple_of(j * 512, 512), 512)
            p = jnp.exp2(logits[q, rows, wide] - top)
            return sums + jnp.sum(p.reshape(64, 8, 256), axis=0)

        sums = lax.fori_loop(0, 2, total, jnp.zeros((8, 256), F32))
        rmax[q, 0:1, wide] = top
        rsum[q, 0:1, wide] = jnp.sum(sums, axis=0, keepdims=True)

    def turn(q):
        def body(j, _):
            rows = pl.ds(pl.multiple_of(j * 512, 512), 512)
            out = lax.dot_general(eye, tgt[q, rows, :], NT, preferred_element_type=F32)
            tgt_t[q, :, rows] = out.astype(BF16)
            return 0

        lax.fori_loop(0, 2, body, 0)

    R = 128

    def fold(value, op):
        return op(value.reshape(R // 8, 8, 128), axis=0)

    def lanes(d):
        return pl.ds(d * 128, 128)

    def row_single(q):
        def body(i, carry):
            rows = pl.ds(pl.multiple_of(i * R, R), R)
            g = gcol[q, rows, :]
            new = []
            for d in range(8):
                m, total = carry[d]
                t = logits[q, rows, lanes(d)] + g
                top = jnp.maximum(m, fold(t, jnp.max))
                p = jnp.exp2(t.reshape(R // 8, 8, 128) - top)
                new.append((top, total * jnp.exp2(m - top) + jnp.sum(p, axis=0)))
            return tuple(new)

        start = (jnp.full((8, 128), NEG, F32), jnp.zeros((8, 128), F32))
        done = lax.fori_loop(0, 1024 // R, body, (start,) * 8)
        for d, (m, total) in enumerate(done):
            top = jnp.max(m, axis=0, keepdims=True)
            rmax[q, 0:1, lanes(d)] = top
            rsum[q, 0:1, lanes(d)] = jnp.sum(total * jnp.exp2(m - top), axis=0, keepdims=True)

    def row_sweeps(q, with_g, keep):
        def shifted(rows):
            if with_g:
                g = gcol[q, rows, :]
                return [logits[q, rows, lanes(d)] + g for d in range(8)]
            return [logits[q, rows, lanes(d)] for d in range(8)]

        def first(i, tops):
            rows = pl.ds(pl.multiple_of(i * R, R), R)
            return tuple(jnp.maximum(t, fold(v, jnp.max)) for t, v in zip(tops, shifted(rows)))

        tops = lax.fori_loop(0, 1024 // R, first, (jnp.full((8, 128), NEG, F32),) * 8)
        tops = [jnp.max(t, axis=0, keepdims=True) for t in tops]

        def second(i, sums):
            rows = pl.ds(pl.multiple_of(i * R, R), R)
            new = []
            for d, v in enumerate(shifted(rows)):
                p = jnp.exp2(v - tops[d])
                if keep:
                    weights[q, rows, lanes(d)] = p.astype(BF16)
                new.append(sums[d] + fold(p, jnp.sum))
            return tuple(new)

        sums = lax.fori_loop(0, 1024 // R, second, (jnp.zeros((8, 128), F32),) * 8)
        for d in range(8):
            rmax[q, 0:1, lanes(d)] = tops[d]
            rsum[q, 0:1, lanes(d)] = jnp.sum(sums[d], axis=0, keepdims=True)

    def row_sum(d):
        terms = []
        for q in range(4):
            v = rmax[q, 0:1, lanes(d)] + jnp.log2(rsum[q, 0:1, lanes(d)])
            w = pltpu.roll(v, 64, 1)
            terms.append(jnp.where(sub == block(d, q, 0), jnp.where(low1, v, w), NEG))
            terms.append(jnp.where(sub == block(d, q, 1), jnp.where(low1, w, v), NEG))
        return lse(terms)

    def row_local(phase):
        for i in range(4):
            rowbuf[phase, 0, i] = jnp.where(low, row_sum(2 * i), row_sum(2 * i + 1))

    def row_start(phase):
        copies = []
        for kx, kc in row_peers:
            slot = ((-kx) % 4) * 2 + kc
            copies.append(go(transfer(rowbuf.at[phase, 0], rowbuf.at[phase, slot], at(kx=kx, kc=kc))))
        return copies

    def row_finish(phase, copies):
        for t in copies:
            t.wait_recv()
        for i in range(4):
            terms = [rowbuf[phase, 0, i]]
            for kx, kc in row_peers:
                v = rowbuf[phase, kx * 2 + kc, (i - kx) % 4]
                terms.append(pltpu.roll(v, 64, 1) if kc else v)
            total = -lse(terms)
            other = pltpu.roll(total, 64, 1)
            even = jnp.where(low, total, other)
            odd = jnp.where(low, other, total)
            for b in range(8):
                ftab[32 * i + b] = jnp.broadcast_to(even[b:b + 1], (8, 128))
                ftab[32 * i + 16 + b] = jnp.broadcast_to(odd[b:b + 1], (8, 128))

    def row_spread():
        for q in range(4):
            for d in range(8):
                f0 = ftab[d * 16 + block(d, q, 0)]
                f1 = ftab[d * 16 + block(d, q, 1)]
                frow[q, :, lanes(d)] = jnp.where(low, f0, f1)

    diag = (lax.broadcasted_iota(jnp.int32, (128, 128), 0)
            == lax.broadcasted_iota(jnp.int32, (128, 128), 1))
    C = 128

    def column(q, phase):
        fs = [frow[q, 0:1, lanes(d)] for d in range(8)]

        def body(i, _):
            rows = pl.ds(pl.multiple_of(i * C, C), C)
            ts = [logits[q, rows, lanes(d)] + fs[d] for d in range(8)]
            m = functools.reduce(jnp.maximum, ts)
            cmax[rows, :] = m
            csum[rows, :] = functools.reduce(jnp.add, [jnp.exp2(t - m) for t in ts])
            return 0

        lax.fori_loop(0, 1024 // C, body, 0)

        def merge(h, _):
            rows = pl.ds(pl.multiple_of(h * 512, 512), 512)
            m = cmax[rows, :]
            top = jnp.max(m, axis=1, keepdims=True)
            total = jnp.sum(csum[rows, :] * jnp.exp2(m - top), axis=1, keepdims=True)
            out = top + jnp.log2(total)
            lines = []
            for i in range(4):
                spread = jnp.broadcast_to(out[i * 128:(i + 1) * 128], (128, 128))
                lines.append(jnp.sum(jnp.where(diag, spread, 0.0), axis=0, keepdims=True))
            colbuf[phase, 0, q, pl.ds(pl.multiple_of(h * 4, 4), 4), :] = jnp.concatenate(lines, axis=0)
            return 0

        lax.fori_loop(0, 2, merge, 0)

    def over_y(phase, q):
        return [go(transfer(colbuf.at[phase, 0, q], colbuf.at[phase, (-k) % 4, q], at(ky=k))) for k in (1, 2, 3)]

    def over_z(phase, q, copies):
        for t in copies:
            t.wait_recv()
        ztot[phase, 0, q] = lse([colbuf[phase, k, q] for k in range(4)])
        return [go(transfer(ztot.at[phase, 0, q], ztot.at[phase, (-k) % 4, q], at(kz=k))) for k in (1, 2, 3)]

    def column_done(phase, q, copies):
        for t in copies:
            t.wait_recv()
        total = -lse([ztot[phase, (z - side + 4) % 4, q] for z in range(4)])
        gpack[q] = total
        for h in range(2):
            cols = []
            for i in range(4):
                line = jnp.broadcast_to(total[h * 4 + i:h * 4 + i + 1], (128, 128))
                cols.append(jnp.sum(jnp.where(diag, line, 0.0), axis=1, keepdims=True))
            for i in range(4):
                gcol[q, pl.ds((h * 4 + i) * 128, 128), :] = jnp.broadcast_to(cols[i], (128, 128))

    def columns_then_rows(phase):
        ys, zs = {}, {}
        for q in range(4):
            column(q, phase)
            ys[q] = over_y(phase, q)
            if q >= 2:
                zs[q - 2] = over_z(phase, q - 2, ys[q - 2])
        zs[2] = over_z(phase, 2, ys[2])
        for q in range(4):
            column_done(phase, q, zs[q])
            if phase == ITERS - 1:
                row_sweeps(q, True, True)
            else:
                row_single(q)
            if q == 0:
                zs[3] = over_z(phase, 3, ys[3])

    own_src.wait()
    own_tgt.wait()
    s_c.wait_recv()
    copy_tab.wait()
    unit(0, 0)
    y1_p.wait_recv()
    y21 = go(transfer(tgt.at[yi(3), D1], tgt.at[yi(3), D1], up))
    y2_m.wait_recv()
    y22 = go(transfer(tgt.at[yi(1), D2], tgt.at[yi(1), D2], down))
    y2a.wait_recv()
    z2a = z_both(2, ya)
    y2b.wait_recv()
    z2b = z_both(2, yb)
    s_p.wait_recv()
    s_fp = go(transfer(src[6].at[pl.ds(0, 4)], src[4].at[pl.ds(0, 4)], at(kx=1)))
    s_cp = go(transfer(src[6], src[7], at(kc=1)))
    s_m.wait_recv()
    s_fm = go(transfer(src[2].at[pl.ds(4, 4)], src[4].at[pl.ds(4, 4)], at(kx=3)))
    s_cm = go(transfer(src[2], src[3], at(kc=1)))
    z3f = z_on(3, *z3)
    z1f = z_on(1, *z1)
    s_cp.wait_recv()
    unit(0, 3)
    s_cm.wait_recv()
    z2f = z_on(2, z2a[0], z2b[1])
    s_fp.wait_recv()
    s_fm.wait_recv()
    s_c2 = go(transfer(src[4], src[5], at(kc=1)))
    unit(0, 1)
    for t in (y2_p, *z3f):
        t.wait_recv()
    for kx in (0, 1, 3):
        unit(3, kx)
    for t in (y1_m, *z1f):
        t.wait_recv()
    for kx in (0, 1, 3):
        unit(1, kx)
    s_c2.wait_recv()
    for q in (0, 1, 3):
        unit(q, 2)
    for t in (y21, y22, z2a[1], z2b[0], *z2f):
        t.wait_recv()
    for kx in range(4):
        unit(2, kx)

    for phase in range(ITERS):
        row_local(phase)
        copies = row_start(phase)
        if phase == 0:
            for q in range(4):
                turn(q)
        row_finish(phase, copies)
        row_spread()
        if phase == ITERS - 1:
            even = jnp.concatenate([ftab[2 * i][0:1] for i in range(4)], axis=0)
            odd = jnp.concatenate([ftab[2 * i + 1][0:1] for i in range(4)], axis=0)
            f_out[...] = jnp.where(low[0:4], even, odd) * (REG * LN2)
        columns_then_rows(phase)

    g_out[...] = gpack[y] * (REG * LN2)
    row_id = lax.broadcasted_iota(jnp.int32, (64, 256), 0)
    col_id = lax.broadcasted_iota(jnp.int32, (64, 256), 1)
    same = row_id == col_id % 64
    col_block = col_id // 64

    def prepare(kx):
        for d in (2 * kx, 2 * kx + 1):
            out = row_sum(d)
            for b in range(8):
                ltab[d * 16 + b] = jnp.broadcast_to(out[b:b + 1], (8, 128))
            for h in range(2):
                pieces = [jnp.where(low1, out[b:b + 1], out[b + 1:b + 2]) for b in (4 * h, 4 * h + 2)]
                stat[d, h] = jnp.broadcast_to(jnp.concatenate(pieces, axis=1), (8, 256))
        wide = pl.ds(kx * 256, 256)
        for q in range(4):
            out = jnp.dot(tgt_t[q], weights[q, :, wide], preferred_element_type=F32)
            for i in range(2):
                d = 2 * kx + i
                one = jnp.where(low, ltab[d * 16 + block(d, q, 0)], ltab[d * 16 + block(d, q, 1)])
                factor = jnp.exp2(rmax[q, 0:1, lanes(d)] - one[0:1])
                numer[q, :, lanes(d)] = (out[:, i * 128:(i + 1) * 128] * factor).astype(BF16)

    def assemble(d):
        value = jnp.concatenate([numer[q, :, lanes(d)] for q in range(4)], axis=1)
        for h in range(2):
            picks = []
            for q in range(4):
                for r in range(2):
                    hit = jnp.logical_and(same, col_block == block(d, q, r) - 4 * h)
                    picks.append(jnp.where(hit, 1.0, 0.0).astype(BF16))
            pick = jnp.concatenate(picks, axis=0)
            part[d, h] = jnp.dot(value, pick, preferred_element_type=F32).astype(BF16)

    def merge(terms):
        stats = [st[...] for _, st in terms]
        joint = lse(stats)
        total = None
        for (value, _), st in zip(terms, stats):
            term = value[...].astype(F32).reshape(32, 8, 256) * jnp.exp2(st - joint)
            total = term if total is None else total + term
        return total.reshape(256, 256).astype(BF16), joint

    def own_part(d, h):
        return part.at[d, h], stat.at[d, h]

    def from_core(kx, h):
        return pin.at[kx, h], pstat.at[kx, h]

    to_core = {}

    def give(kx):
        d = kx * 2 + 1
        assemble(d)
        to_core[kx] = [go(transfer(part.at[d], pin.at[kx], at(kc=1))),
                       go(transfer(stat.at[d], pstat.at[kx], at(kc=1)))]

    def take(copies):
        for t in copies:
            t.wait_recv()

    def join(kx, h, extra=()):
        comb[kx, h], cstat[kx, h] = merge([own_part(2 * kx, h), from_core(kx, h), *extra])

    def pass_on(kx, h, n, far, device):
        values, stats = (hin, hstat) if far else (rin, rstat)
        index = (n,) if far else (n, h)
        return [go(transfer(comb.at[kx, h], values.at[index], device)),
                go(transfer(cstat.at[kx, h], stats.at[index], device))]

    right, left = at(kx=1), at(kx=3)
    prepare(2)
    give(2)
    assemble(4)
    prepare(1)
    take(to_core[2])
    join(2, 0)
    h_p = pass_on(2, 0, 0, True, right)
    join(2, 1)
    h_m = pass_on(2, 1, 1, True, left)
    give(1)
    assemble(2)
    prepare(3)
    take(to_core[1])
    join(1, 1)
    r_p1 = pass_on(1, 1, 0, False, right)
    give(3)
    assemble(6)
    prepare(0)
    take(to_core[3])
    join(3, 0)
    r_m0 = pass_on(3, 0, 1, False, left)
    give(0)
    assemble(0)
    take(h_p)
    join(1, 0, [(hin.at[0], hstat.at[0])])
    r_p0 = pass_on(1, 0, 0, False, right)
    take(h_m)
    join(3, 1, [(hin.at[1], hstat.at[1])])
    r_m1 = pass_on(3, 1, 1, False, left)
    take(to_core[0])
    for h, copies in ((0, r_p0 + r_m0), (1, r_p1 + r_m1)):
        take(copies)
        out, _ = merge([own_part(0, h), from_core(0, h),
                        (rin.at[0, h], rstat.at[0, h]), (rin.at[1, h], rstat.at[1, h])])
        turned = lax.dot_general(eye, out, NT, preferred_element_type=F32)
        mapped[pl.ds(h * 256, 256), :] = turned.astype(BF16)

    for t in sent:
        t.wait_send()


COPIES = 7 + 8 + 24 + 7 * ITERS + 24 * ITERS + 20


def shards(source, target, pairs, owner_map):
    any_space = pl.BlockSpec(memory_space=pl.ANY)
    smem = pl.BlockSpec(memory_space=pltpu.SMEM)
    vmem = pl.BlockSpec(memory_space=pltpu.VMEM)
    f, g, mapped = pl.pallas_call(
        kernel,
        out_shape=(
            jax.ShapeDtypeStruct((4, 128), F32),
            jax.ShapeDtypeStruct((8, 128), F32),
            jax.ShapeDtypeStruct((512, 256), BF16),
        ),
        in_specs=[any_space, any_space, smem, smem],
        out_specs=(vmem, vmem, vmem),
        scratch_shapes=[
            *[pltpu.VMEM((8, 64, 256), BF16)] * 8,
            pltpu.VMEM((4, 1024, 256), BF16),
            pltpu.VMEM((8, 8, 128), jnp.int32),
            pltpu.SMEM((8, 8, 128), jnp.int32),
            pltpu.VMEM((1024, 256), BF16),
            pltpu.VMEM((4, 1024, 1024), F32),
            pltpu.VMEM((4, 1024, 1024), BF16),
            pltpu.VMEM((4, 256, 1024), BF16),
            pltpu.VMEM((4, 1024, 128), F32),
            pltpu.VMEM((1024, 128), F32),
            pltpu.VMEM((1024, 128), F32),
            pltpu.VMEM((4, 8, 1024), F32),
            pltpu.VMEM((4, 8, 1024), F32),
            pltpu.VMEM((ITERS, 8, 4, 8, 128), F32),
            pltpu.VMEM((128, 8, 128), F32),
            pltpu.VMEM((128, 8, 128), F32),
            pltpu.VMEM((4, 8, 1024), F32),
            pltpu.VMEM((ITERS, 4, 4, 8, 128), F32),
            pltpu.VMEM((ITERS, 4, 4, 8, 128), F32),
            pltpu.VMEM((4, 8, 128), F32),
            pltpu.VMEM((4, 256, 1024), BF16),
            pltpu.VMEM((8, 2, 256, 256), BF16),
            pltpu.VMEM((4, 2, 256, 256), BF16),
            pltpu.VMEM((4, 2, 256, 256), BF16),
            pltpu.VMEM((2, 2, 256, 256), BF16),
            pltpu.VMEM((2, 256, 256), BF16),
            pltpu.VMEM((8, 2, 8, 256), F32),
            pltpu.VMEM((4, 2, 8, 256), F32),
            pltpu.VMEM((4, 2, 8, 256), F32),
            pltpu.VMEM((2, 2, 8, 256), F32),
            pltpu.VMEM((2, 8, 256), F32),
            pltpu.SemaphoreType.DMA((COPIES,)),
            pltpu.SemaphoreType.DMA((COPIES,)),
            pltpu.SemaphoreType.DMA((3,)),
        ],
        compiler_params=pltpu.CompilerParams(
            collective_id=0, has_side_effects=True, vmem_limit_bytes=60 * 1024 * 1024
        ),
        name="sinkhorn",
    )(source.reshape(8, 64, 256), target, pairs.T, owner_map)
    return f.reshape(512), g.reshape(1024), mapped


def solution(mesh):
    return jax.shard_map(
        shards,
        mesh=mesh,
        in_specs=(P(("side", "blk"), None), P("blk", None), P(("side", "blk"), None), P()),
        out_specs=(P(("side", "blk")), P("blk"), P(("side", "blk"), None)),
        check_vma=False,
    )
```

```python
import functools
import math

import jax
import jax.numpy as jnp
from jax import lax
from jax.experimental import pallas as pl
from jax.experimental.pallas import tpu as pltpu
from jax.sharding import PartitionSpec as P

MESH = pl.DeviceIdType.MESH
NEG = -1e30
LOG2E = 1.4426950408889634
LN2 = 0.6931471805599453
REG = 0.3
ITERS = 2
NT = (((1,), (1,)), ((), ()))
F32 = jnp.float32
BF16 = jnp.bfloat16


def lse(parts):
    top = functools.reduce(jnp.maximum, parts)
    total = functools.reduce(jnp.add, [jnp.exp2(p - top) for p in parts])
    return top + jnp.log2(total)


def kernel(
    source, target, pairs, owner_map, f_out, g_out, mapped,
    src0, src1, src2, src3, src4, src5, src6, src7, tgt, tab, tabp, stab, sq, logits, weights, tgt_t, gcol, cmax, csum,
    rmax, rsum, rowbuf, ftab, ltab, frow, colbuf, ztot, gpack, numer, part, comb, pin, rin, hin,
    stat, cstat, pstat, rstat, hstat, send_sem, recv_sem, local_sem,
):
    src = (src0, src1, src2, src3, src4, src5, src6, src7)
    side = lax.axis_index("side")
    blk = lax.axis_index("blk")
    x = blk // 8
    y = (blk // 2) % 4
    c = blk % 2

    def at(kx=0, kc=0, ky=0, kz=0):
        xx = (x + kx) % 4
        yy = (y + ky) % 4
        cc = (c + kc) % 2
        zz = (side + kz) % 4
        return (zz, (xx * 4 + yy) * 2 + cc)

    def yi(k):
        return (y + k) % 4

    count = [0]

    def transfer(source_ref, dest_ref, device):
        n = count[0]
        count[0] += 1
        return pltpu.make_async_remote_copy(
            src_ref=source_ref, dst_ref=dest_ref,
            send_sem=send_sem.at[n], recv_sem=recv_sem.at[n],
            device_id=device, device_id_type=MESH,
        )

    sent = []

    def go(copy):
        copy.start()
        sent.append(copy)
        return copy

    row_peers = [(kx, kc) for kx in range(4) for kc in range(2)][1:]
    peers = [at(kx=kx, kc=kc) for kx, kc in row_peers]
    peers += [at(ky=k) for k in (1, 2, 3)] + [at(kz=k) for k in (1, 2, 3)]
    barrier = pltpu.get_barrier_semaphore()
    for peer in peers:
        pl.semaphore_signal(barrier, inc=1, device_id=peer, device_id_type=MESH)

    own_src = pltpu.make_async_copy(source, src[0], local_sem.at[0])
    own_src.start()
    own_tgt = pltpu.make_async_copy(target, tgt.at[y], local_sem.at[1])
    own_tgt.start()

    lane = lax.broadcasted_iota(jnp.int32, (8, 128), 1)
    sub = lax.broadcasted_iota(jnp.int32, (8, 128), 0)
    low = lane < 64
    low1 = low[0:1]

    target_lane = lane % 32
    turn_lane = lane // 32
    seen = jnp.zeros((8, 128), jnp.int32)
    table = jnp.full((8, 128), 8, jnp.int32)
    for s in range(8):
        hit = target_lane == owner_map[pairs[0, s]]
        for k in range(1, 4):
            hit = jnp.logical_or(hit, target_lane == owner_map[pairs[k, s]])
        table = jnp.where(jnp.logical_and(hit, seen == turn_lane), s, table)
        seen = seen + jnp.where(hit, 1, 0)
    tab[0] = table

    pl.semaphore_wait(barrier, len(peers))

    A, B = pl.ds(0, 256), pl.ds(256, 256)
    tabs = []
    for kx, kc in row_peers:
        slot = ((-kx) % 4) * 2 + kc
        tabs.append(go(transfer(tab.at[0], tab.at[slot], at(kx=kx, kc=kc))))

    D1, D2 = pl.ds(0, 224), pl.ds(224, 224)

    def part_of(kz, half=None):
        start = 448 + 144 * ((side + kz) % 4)
        if half is None:
            return pl.ds(pl.multiple_of(start, 16), 144)
        return pl.ds(pl.multiple_of(start + 80 * half, 16), (80, 64)[half])

    own = part_of(0)
    up, down = at(ky=1), at(ky=3)
    FA, FB = pl.ds(0, 4), pl.ds(4, 4)
    s_pa = go(transfer(source.at[FA], src[6].at[FA], at(kx=1)))
    s_mb = go(transfer(source.at[FB], src[2].at[FB], at(kx=3)))
    s_pb = go(transfer(source.at[FB], src[6].at[FB], at(kx=1)))
    s_ma = go(transfer(source.at[FA], src[2].at[FA], at(kx=3)))
    ys_p = go(transfer(target.at[own], tgt.at[y, own], up))
    ys_m = go(transfer(target.at[own], tgt.at[y, own], down))
    y1_p = go(transfer(target.at[D1], tgt.at[y, D1], up))
    y2_m = go(transfer(target.at[D2], tgt.at[y, D2], down))
    s_c = go(transfer(source, src[1], at(kc=1)))

    def z_both(k, rows):
        return (go(transfer(tgt.at[yi(k), rows], tgt.at[yi(k), rows], at(kz=1))),
                go(transfer(tgt.at[yi(k), rows], tgt.at[yi(k), rows], at(kz=3))))

    def z_on(k, z_p, z_m):
        out = []
        if z_p is not None:
            z_p.wait_recv()
            rows = part_of(3, 0)
            out.append(go(transfer(tgt.at[yi(k), rows], tgt.at[yi(k), rows], at(kz=1))))
        if z_m is not None:
            z_m.wait_recv()
            rows = part_of(1, 1)
            out.append(go(transfer(tgt.at[yi(k), rows], tgt.at[yi(k), rows], at(kz=3))))
        return out

    for t in tabs:
        t.wait_recv()
    listing = jnp.full((8, 128), 8, jnp.int32)
    for i in range(4):
        line = jnp.where(low, tab[2 * i], pltpu.roll(tab[2 * i + 1], 64, 1))
        listing = jnp.where(sub == i, line, listing)
    tabp[...] = listing
    copy_tab = pltpu.make_async_copy(tabp.at[pl.ds(0, 4)], stab, local_sem.at[2])
    copy_tab.start()

    ys_p.wait_recv()
    ya = part_of(0, 0)
    yb = part_of(0, 1)
    y2a = go(transfer(tgt.at[yi(3), ya], tgt.at[yi(3), ya], up))
    z3 = z_both(3, own)
    ys_m.wait_recv()
    y2b = go(transfer(tgt.at[yi(1), yb], tgt.at[yi(1), yb], down))
    z1 = z_both(1, own)
    y2_p = go(transfer(target.at[D2], tgt.at[y, D2], up))
    y1_m = go(transfer(target.at[D1], tgt.at[y, D1], down))

    def block(d, q, r):
        return stab[d // 2, (d % 2) * 64 + r * 32 + (x * 4 + q) * 2 + c]

    ones = jnp.full((8, 128), NEG, F32)
    for d in range(8):
        ftab[d * 16 + 8] = ones
        ltab[d * 16 + 8] = -ones

    scale = LOG2E / (REG * 16.0)
    eye = jnp.where(
        lax.broadcasted_iota(jnp.int32, (256, 256), 0)
        == lax.broadcasted_iota(jnp.int32, (256, 256), 1), 1.0, 0.0).astype(BF16)

    def unit(ky, kx):
        q = yi(ky)
        for d in (2 * kx, 2 * kx + 1):
            for r in range(2):
                b = jnp.minimum(block(d, q, r), 7)
                sq[pl.ds(d * 128 + r * 64, 64), :] = src[d][b]
        wide = pl.ds(kx * 256, 256)
        out = lax.dot_general(tgt[q], sq[wide, :], NT, preferred_element_type=F32) * scale
        logits[q, :, wide] = out
        top = jnp.max(jnp.max(out.reshape(128, 8, 256), axis=0), axis=0, keepdims=True)

        def total(j, sums):
            rows = pl.ds(pl.multiple_of(j * 512, 512), 512)
            p = jnp.exp2(logits[q, rows, wide] - top)
            return sums + jnp.sum(p.reshape(64, 8, 256), axis=0)

        sums = lax.fori_loop(0, 2, total, jnp.zeros((8, 256), F32))
        rmax[q, 0:1, wide] = top
        rsum[q, 0:1, wide] = jnp.sum(sums, axis=0, keepdims=True)

    def turn(q):
        def body(j, _):
            rows = pl.ds(pl.multiple_of(j * 512, 512), 512)
            out = lax.dot_general(eye, tgt[q, rows, :], NT, preferred_element_type=F32)
            tgt_t[q, :, rows] = out.astype(BF16)
            return 0

        lax.fori_loop(0, 2, body, 0)

    R = 128

    def fold(value, op):
        return op(value.reshape(R // 8, 8, 128), axis=0)

    def lanes(d):
        return pl.ds(d * 128, 128)

    def row_single(q):
        def body(i, carry):
            rows = pl.ds(pl.multiple_of(i * R, R), R)
            g = gcol[q, rows, :]
            new = []
            for d in range(8):
                m, total = carry[d]
                t = logits[q, rows, lanes(d)] + g
                top = jnp.maximum(m, fold(t, jnp.max))
                p = jnp.exp2(t.reshape(R // 8, 8, 128) - top)
                new.append((top, total * jnp.exp2(m - top) + jnp.sum(p, axis=0)))
            return tuple(new)

        start = (jnp.full((8, 128), NEG, F32), jnp.zeros((8, 128), F32))
        done = lax.fori_loop(0, 1024 // R, body, (start,) * 8)
        for d, (m, total) in enumerate(done):
            top = jnp.max(m, axis=0, keepdims=True)
            rmax[q, 0:1, lanes(d)] = top
            rsum[q, 0:1, lanes(d)] = jnp.sum(total * jnp.exp2(m - top), axis=0, keepdims=True)

    def row_keep(q, ds):
        height = 1024 // len(ds)

        def group(value, op):
            return op(value.reshape(height // 8, 8, 128), axis=0)

        def shifted(i):
            rows = pl.ds(pl.multiple_of(i * height, height), height)
            g = gcol[q, rows, :]
            return rows, [logits[q, rows, lanes(d)] + g for d in ds]

        def first(i, tops):
            return tuple(jnp.maximum(t, group(v, jnp.max)) for t, v in zip(tops, shifted(i)[1]))

        tops = lax.fori_loop(0, len(ds), first, (jnp.full((8, 128), NEG, F32),) * len(ds))
        tops = [jnp.max(t, axis=0, keepdims=True) for t in tops]

        def second(i, sums):
            rows, values = shifted(i)
            new = []
            for d, v, top, total in zip(ds, values, tops, sums):
                p = jnp.exp2(v - top)
                weights[q, rows, lanes(d)] = p.astype(BF16)
                new.append(total + group(p, jnp.sum))
            return tuple(new)

        sums = lax.fori_loop(0, len(ds), second, (jnp.zeros((8, 128), F32),) * len(ds))
        for d, top, total in zip(ds, tops, sums):
            rmax[q, 0:1, lanes(d)] = top
            rsum[q, 0:1, lanes(d)] = jnp.sum(total, axis=0, keepdims=True)

    def row_sum(d):
        terms = []
        for q in range(4):
            v = rmax[q, 0:1, lanes(d)] + jnp.log2(rsum[q, 0:1, lanes(d)])
            w = pltpu.roll(v, 64, 1)
            terms.append(jnp.where(sub == block(d, q, 0), jnp.where(low1, v, w), NEG))
            terms.append(jnp.where(sub == block(d, q, 1), jnp.where(low1, w, v), NEG))
        return lse(terms)

    def row_local(phase):
        for i in range(4):
            rowbuf[phase, 0, i] = jnp.where(low, row_sum(2 * i), row_sum(2 * i + 1))

    def row_start(phase):
        copies = []
        for kx, kc in row_peers:
            slot = ((-kx) % 4) * 2 + kc
            copies.append(go(transfer(rowbuf.at[phase, 0], rowbuf.at[phase, slot], at(kx=kx, kc=kc))))
        return copies

    def row_finish(phase, copies):
        for t in copies:
            t.wait_recv()
        for i in range(4):
            terms = [rowbuf[phase, 0, i]]
            for kx, kc in row_peers:
                v = rowbuf[phase, kx * 2 + kc, (i - kx) % 4]
                terms.append(pltpu.roll(v, 64, 1) if kc else v)
            total = -lse(terms)
            other = pltpu.roll(total, 64, 1)
            even = jnp.where(low, total, other)
            odd = jnp.where(low, other, total)
            for b in range(8):
                ftab[32 * i + b] = jnp.broadcast_to(even[b:b + 1], (8, 128))
                ftab[32 * i + 16 + b] = jnp.broadcast_to(odd[b:b + 1], (8, 128))

    def row_spread():
        for q in range(4):
            for d in range(8):
                f0 = ftab[d * 16 + block(d, q, 0)]
                f1 = ftab[d * 16 + block(d, q, 1)]
                frow[q, :, lanes(d)] = jnp.where(low, f0, f1)

    diag = (lax.broadcasted_iota(jnp.int32, (128, 128), 0)
            == lax.broadcasted_iota(jnp.int32, (128, 128), 1))
    C = 128

    def column(q, phase):
        fs = [frow[q, 0:1, lanes(d)] for d in range(8)]

        def body(i, _):
            rows = pl.ds(pl.multiple_of(i * C, C), C)
            ts = [logits[q, rows, lanes(d)] + fs[d] for d in range(8)]
            m = functools.reduce(jnp.maximum, ts)
            cmax[rows, :] = m
            csum[rows, :] = functools.reduce(jnp.add, [jnp.exp2(t - m) for t in ts])
            return 0

        lax.fori_loop(0, 1024 // C, body, 0)

        def merge(h, _):
            rows = pl.ds(pl.multiple_of(h * 512, 512), 512)
            m = cmax[rows, :]
            top = jnp.max(m, axis=1, keepdims=True)
            total = jnp.sum(csum[rows, :] * jnp.exp2(m - top), axis=1, keepdims=True)
            out = top + jnp.log2(total)
            lines = []
            for i in range(4):
                spread = jnp.broadcast_to(out[i * 128:(i + 1) * 128], (128, 128))
                lines.append(jnp.sum(jnp.where(diag, spread, 0.0), axis=0, keepdims=True))
            colbuf[phase, 0, q, pl.ds(pl.multiple_of(h * 4, 4), 4), :] = jnp.concatenate(lines, axis=0)
            return 0

        lax.fori_loop(0, 2, merge, 0)

    def over_y(phase, q):
        return [go(transfer(colbuf.at[phase, 0, q], colbuf.at[phase, (-k) % 4, q], at(ky=k))) for k in (1, 2, 3)]

    def over_z(phase, q, copies):
        for t in copies:
            t.wait_recv()
        ztot[phase, 0, q] = lse([colbuf[phase, k, q] for k in range(4)])
        return [go(transfer(ztot.at[phase, 0, q], ztot.at[phase, (-k) % 4, q], at(kz=k))) for k in (1, 2, 3)]

    def column_done(phase, q, copies):
        for t in copies:
            t.wait_recv()
        total = -lse([ztot[phase, (z - side + 4) % 4, q] for z in range(4)])
        gpack[q] = total
        for h in range(2):
            cols = []
            for i in range(4):
                line = jnp.broadcast_to(total[h * 4 + i:h * 4 + i + 1], (128, 128))
                cols.append(jnp.sum(jnp.where(diag, line, 0.0), axis=1, keepdims=True))
            for i in range(4):
                gcol[q, pl.ds((h * 4 + i) * 128, 128), :] = jnp.broadcast_to(cols[i], (128, 128))

    def columns_then_rows(phase):
        ys, zs = {}, {}
        for q in range(4):
            column(q, phase)
            ys[q] = over_y(phase, q)
            if q >= 2:
                zs[q - 2] = over_z(phase, q - 2, ys[q - 2])
        zs[2] = over_z(phase, 2, ys[2])
        for q in range(4):
            column_done(phase, q, zs[q])
            if phase < ITERS - 1:
                row_single(q)
            elif q < 3:
                row_keep(q, range(8))
            if q == 0:
                zs[3] = over_z(phase, 3, ys[3])

    own_src.wait()
    own_tgt.wait()
    s_c.wait_recv()
    copy_tab.wait()
    unit(0, 0)
    s_pa.wait_recv()
    s_fp = go(transfer(src[6].at[FA], src[4].at[FA], at(kx=1)))
    s_mb.wait_recv()
    s_fm = go(transfer(src[2].at[FB], src[4].at[FB], at(kx=3)))
    y1_p.wait_recv()
    y21 = go(transfer(tgt.at[yi(3), D1], tgt.at[yi(3), D1], up))
    y2_m.wait_recv()
    y22 = go(transfer(tgt.at[yi(1), D2], tgt.at[yi(1), D2], down))
    y2a.wait_recv()
    z2a = z_both(2, ya)
    y2b.wait_recv()
    z2b = z_both(2, yb)
    z3f = z_on(3, *z3)
    s_pb.wait_recv()
    s_cp = go(transfer(src[6], src[7], at(kc=1)))
    s_ma.wait_recv()
    s_cm = go(transfer(src[2], src[3], at(kc=1)))
    z1f = z_on(1, *z1)
    s_cp.wait_recv()
    unit(0, 3)
    s_cm.wait_recv()
    unit(0, 1)
    s_fp.wait_recv()
    s_c2a = go(transfer(src[4].at[FA], src[5].at[FA], at(kc=1)))
    s_fm.wait_recv()
    s_c2b = go(transfer(src[4].at[FB], src[5].at[FB], at(kc=1)))
    z2f = z_on(2, z2a[0], z2b[1])
    for t in (y2_p, *z3f):
        t.wait_recv()
    for kx in (0, 1, 3):
        unit(3, kx)
    s_c2a.wait_recv()
    s_c2b.wait_recv()
    unit(0, 2)
    unit(3, 2)
    for t in (y1_m, *z1f):
        t.wait_recv()
    for kx in range(4):
        unit(1, kx)
    for t in (y21, y22, z2a[1], z2b[0], *z2f):
        t.wait_recv()
    for kx in range(4):
        unit(2, kx)

    for phase in range(ITERS):
        row_local(phase)
        copies = row_start(phase)
        if phase == 0:
            for q in range(4):
                turn(q)
        row_finish(phase, copies)
        row_spread()
        if phase == ITERS - 1:
            even = jnp.concatenate([ftab[2 * i][0:1] for i in range(4)], axis=0)
            odd = jnp.concatenate([ftab[2 * i + 1][0:1] for i in range(4)], axis=0)
            f_out[...] = jnp.where(low[0:4], even, odd) * (REG * LN2)
        columns_then_rows(phase)

    g_out[...] = gpack[y] * (REG * LN2)
    row_id = lax.broadcasted_iota(jnp.int32, (64, 256), 0)
    col_id = lax.broadcasted_iota(jnp.int32, (64, 256), 1)
    same = row_id == col_id % 64
    col_block = col_id // 64

    def prepare(kx):
        row_keep(3, (2 * kx, 2 * kx + 1))
        for d in (2 * kx, 2 * kx + 1):
            out = row_sum(d)
            for b in range(8):
                ltab[d * 16 + b] = jnp.broadcast_to(out[b:b + 1], (8, 128))
            for h in range(2):
                pieces = [jnp.where(low1, out[b:b + 1], out[b + 1:b + 2]) for b in (4 * h, 4 * h + 2)]
                stat[d, h] = jnp.broadcast_to(jnp.concatenate(pieces, axis=1), (8, 256))
        wide = pl.ds(kx * 256, 256)
        for q in range(4):
            out = jnp.dot(tgt_t[q], weights[q, :, wide], preferred_element_type=F32)
            for i in range(2):
                d = 2 * kx + i
                one = jnp.where(low, ltab[d * 16 + block(d, q, 0)], ltab[d * 16 + block(d, q, 1)])
                factor = jnp.exp2(rmax[q, 0:1, lanes(d)] - one[0:1])
                numer[q, :, lanes(d)] = (out[:, i * 128:(i + 1) * 128] * factor).astype(BF16)

    def assemble(d):
        value = jnp.concatenate([numer[q, :, lanes(d)] for q in range(4)], axis=1)
        for h in range(2):
            picks = []
            for q in range(4):
                for r in range(2):
                    hit = jnp.logical_and(same, col_block == block(d, q, r) - 4 * h)
                    picks.append(jnp.where(hit, 1.0, 0.0).astype(BF16))
            pick = jnp.concatenate(picks, axis=0)
            part[d, h] = jnp.dot(value, pick, preferred_element_type=F32).astype(BF16)

    def merge(terms):
        stats = [st[...] for _, st in terms]
        joint = lse(stats)
        total = None
        for (value, _), st in zip(terms, stats):
            term = value[...].astype(F32).reshape(32, 8, 256) * jnp.exp2(st - joint)
            total = term if total is None else total + term
        return total.reshape(256, 256).astype(BF16), joint

    def own_part(d, h):
        return part.at[d, h], stat.at[d, h]

    def from_core(kx, h):
        return pin.at[kx, h], pstat.at[kx, h]

    to_core = {}

    def give(kx):
        d = kx * 2 + 1
        assemble(d)
        to_core[kx] = [go(transfer(part.at[d], pin.at[kx], at(kc=1))),
                       go(transfer(stat.at[d], pstat.at[kx], at(kc=1)))]

    def take(copies):
        for t in copies:
            t.wait_recv()

    def join(kx, h, extra=()):
        comb[kx, h], cstat[kx, h] = merge([own_part(2 * kx, h), from_core(kx, h), *extra])

    def pass_on(kx, h, n, far, device):
        values, stats = (hin, hstat) if far else (rin, rstat)
        index = (n,) if far else (n, h)
        return [go(transfer(comb.at[kx, h], values.at[index], device)),
                go(transfer(cstat.at[kx, h], stats.at[index], device))]

    right, left = at(kx=1), at(kx=3)
    prepare(2)
    give(2)
    assemble(4)
    prepare(1)
    take(to_core[2])
    join(2, 0)
    h_p = pass_on(2, 0, 0, True, right)
    join(2, 1)
    h_m = pass_on(2, 1, 1, True, left)
    give(1)
    assemble(2)
    prepare(3)
    take(to_core[1])
    join(1, 1)
    r_p1 = pass_on(1, 1, 0, False, right)
    give(3)
    assemble(6)
    prepare(0)
    take(to_core[3])
    join(3, 0)
    r_m0 = pass_on(3, 0, 1, False, left)
    give(0)
    assemble(0)
    take(h_p)
    join(1, 0, [(hin.at[0], hstat.at[0])])
    r_p0 = pass_on(1, 0, 0, False, right)
    take(h_m)
    join(3, 1, [(hin.at[1], hstat.at[1])])
    r_m1 = pass_on(3, 1, 1, False, left)
    take(to_core[0])
    for h, copies in ((0, r_p0 + r_m0), (1, r_p1 + r_m1)):
        take(copies)
        out, _ = merge([own_part(0, h), from_core(0, h),
                        (rin.at[0, h], rstat.at[0, h]), (rin.at[1, h], rstat.at[1, h])])
        turned = lax.dot_general(eye, out, NT, preferred_element_type=F32)
        mapped[pl.ds(h * 256, 256), :] = turned.astype(BF16)

    for t in sent:
        t.wait_send()


COPIES = 42 + 7 * ITERS + 24 * ITERS + 20


def hand_over(f_in, g_in, m_in, f_out, g_out, m_out, f, g, m, in_sem, out_sem):
    jobs = [(m_in.at[pl.ds(i * 128, 128)], m.at[pl.ds(i * 128, 128)], m_out.at[pl.ds(i * 128, 128)]) for i in range(4)]
    jobs += [(f_in, f, f_out), (g_in, g, g_out)]
    first = [pltpu.make_async_copy(a, b, in_sem.at[n]) for n, (a, b, _) in enumerate(jobs)]
    second = [pltpu.make_async_copy(b, o, out_sem.at[n]) for n, (_, b, o) in enumerate(jobs)]
    for copy in first:
        copy.start()
    for copy, follow in zip(first, second):
        copy.wait()
        follow.start()
    for copy in second:
        copy.wait()


def shards(source, target, pairs, owner_map):
    any_space = pl.BlockSpec(memory_space=pl.ANY)
    smem = pl.BlockSpec(memory_space=pltpu.SMEM)
    vmem = pl.BlockSpec(memory_space=pltpu.VMEM)
    f, g, mapped = pl.pallas_call(
        kernel,
        out_shape=(
            jax.ShapeDtypeStruct((4, 128), F32),
            jax.ShapeDtypeStruct((8, 128), F32),
            jax.ShapeDtypeStruct((512, 256), BF16),
        ),
        in_specs=[any_space, any_space, smem, smem],
        out_specs=(vmem, vmem, vmem),
        scratch_shapes=[
            *[pltpu.VMEM((8, 64, 256), BF16)] * 8,
            pltpu.VMEM((4, 1024, 256), BF16),
            pltpu.VMEM((8, 8, 128), jnp.int32),
            pltpu.VMEM((8, 128), jnp.int32),
            pltpu.SMEM((4, 128), jnp.int32),
            pltpu.VMEM((1024, 256), BF16),
            pltpu.VMEM((4, 1024, 1024), F32),
            pltpu.VMEM((4, 1024, 1024), BF16),
            pltpu.VMEM((4, 256, 1024), BF16),
            pltpu.VMEM((4, 1024, 128), F32),
            pltpu.VMEM((1024, 128), F32),
            pltpu.VMEM((1024, 128), F32),
            pltpu.VMEM((4, 8, 1024), F32),
            pltpu.VMEM((4, 8, 1024), F32),
            pltpu.VMEM((ITERS, 8, 4, 8, 128), F32),
            pltpu.VMEM((128, 8, 128), F32),
            pltpu.VMEM((128, 8, 128), F32),
            pltpu.VMEM((4, 8, 1024), F32),
            pltpu.VMEM((ITERS, 4, 4, 8, 128), F32),
            pltpu.VMEM((ITERS, 4, 4, 8, 128), F32),
            pltpu.VMEM((4, 8, 128), F32),
            pltpu.VMEM((4, 256, 1024), BF16),
            pltpu.VMEM((8, 2, 256, 256), BF16),
            pltpu.VMEM((4, 2, 256, 256), BF16),
            pltpu.VMEM((4, 2, 256, 256), BF16),
            pltpu.VMEM((2, 2, 256, 256), BF16),
            pltpu.VMEM((2, 256, 256), BF16),
            pltpu.VMEM((8, 2, 8, 256), F32),
            pltpu.VMEM((4, 2, 8, 256), F32),
            pltpu.VMEM((4, 2, 8, 256), F32),
            pltpu.VMEM((2, 2, 8, 256), F32),
            pltpu.VMEM((2, 8, 256), F32),
            pltpu.SemaphoreType.DMA((COPIES,)),
            pltpu.SemaphoreType.DMA((COPIES,)),
            pltpu.SemaphoreType.DMA((3,)),
        ],
        compiler_params=pltpu.CompilerParams(
            collective_id=0, has_side_effects=True, vmem_limit_bytes=60 * 1024 * 1024
        ),
        name="sinkhorn",
    )(source.reshape(8, 64, 256), target, pairs.T, owner_map)
    f, g, mapped = pl.pallas_call(
        hand_over,
        out_shape=(
            jax.ShapeDtypeStruct((4, 128), F32),
            jax.ShapeDtypeStruct((8, 128), F32),
            jax.ShapeDtypeStruct((512, 256), BF16),
        ),
        in_specs=[any_space] * 3,
        out_specs=(any_space,) * 3,
        scratch_shapes=[
            pltpu.VMEM((4, 128), F32),
            pltpu.VMEM((8, 128), F32),
            pltpu.VMEM((512, 256), BF16),
            pltpu.SemaphoreType.DMA((8,)),
            pltpu.SemaphoreType.DMA((8,)),
        ],
        name="hand_over",
    )(f, g, mapped)
    return f.reshape(512), g.reshape(1024), mapped


def solution(mesh):
    return jax.shard_map(
        shards,
        mesh=mesh,
        in_specs=(P(("side", "blk"), None), P("blk", None), P(("side", "blk"), None), P()),
        out_specs=(P(("side", "blk")), P("blk"), P(("side", "blk"), None)),
        check_vma=False,
    )
```

```python
import functools
import math

import jax
import jax.numpy as jnp
from jax import lax
from jax.experimental import pallas as pl
from jax.experimental.pallas import tpu as pltpu
from jax.sharding import PartitionSpec as P

MESH = pl.DeviceIdType.MESH
NEG = -1e30
LOG2E = 1.4426950408889634
LN2 = 0.6931471805599453
REG = 0.3
ITERS = 2
NT = (((1,), (1,)), ((), ()))
F32 = jnp.float32
BF16 = jnp.bfloat16


def lse(parts):
    top = functools.reduce(jnp.maximum, parts)
    total = functools.reduce(jnp.add, [jnp.exp2(p - top) for p in parts])
    return top + jnp.log2(total)


def kernel(
    source, target, pairs, owner_map, f_out, g_out, mapped,
    src0, src1, src2, src3, src4, src5, src6, src7, tgt, tab, tabp, stab, sq, logits, weights, tgt_t, gcol, cmax, csum,
    rmax, rsum, rowbuf, ftab, ltab, frow, colbuf, ztot, gpack, numer, part, comb, pin, rin, hin,
    stat, cstat, pstat, rstat, hstat, send_sem, recv_sem, local_sem,
):
    src = (src0, src1, src2, src3, src4, src5, src6, src7)
    side = lax.axis_index("side")
    blk = lax.axis_index("blk")
    x = blk // 8
    y = (blk // 2) % 4
    c = blk % 2

    def at(kx=0, kc=0, ky=0, kz=0):
        xx = (x + kx) % 4
        yy = (y + ky) % 4
        cc = (c + kc) % 2
        zz = (side + kz) % 4
        return (zz, (xx * 4 + yy) * 2 + cc)

    def yi(k):
        return (y + k) % 4

    count = [0]

    def transfer(source_ref, dest_ref, device):
        n = count[0]
        count[0] += 1
        return pltpu.make_async_remote_copy(
            src_ref=source_ref, dst_ref=dest_ref,
            send_sem=send_sem.at[n], recv_sem=recv_sem.at[n],
            device_id=device, device_id_type=MESH,
        )

    sent = []

    def go(copy):
        copy.start()
        sent.append(copy)
        return copy

    row_peers = [(kx, kc) for kx in range(4) for kc in range(2)][1:]
    peers = [at(kx=kx, kc=kc) for kx, kc in row_peers]
    peers += [at(ky=k) for k in (1, 2, 3)] + [at(kz=k) for k in (1, 2, 3)]
    barrier = pltpu.get_barrier_semaphore()
    for peer in peers:
        pl.semaphore_signal(barrier, inc=1, device_id=peer, device_id_type=MESH)

    own_src = pltpu.make_async_copy(source, src[0], local_sem.at[0])
    own_src.start()
    own_tgt = pltpu.make_async_copy(target, tgt.at[y], local_sem.at[1])
    own_tgt.start()

    lane = lax.broadcasted_iota(jnp.int32, (8, 128), 1)
    sub = lax.broadcasted_iota(jnp.int32, (8, 128), 0)
    low = lane < 64
    low1 = low[0:1]

    target_lane = lane % 32
    turn_lane = lane // 32
    seen = jnp.zeros((8, 128), jnp.int32)
    table = jnp.full((8, 128), 8, jnp.int32)
    for s in range(8):
        hit = target_lane == owner_map[pairs[0, s]]
        for k in range(1, 4):
            hit = jnp.logical_or(hit, target_lane == owner_map[pairs[k, s]])
        table = jnp.where(jnp.logical_and(hit, seen == turn_lane), s, table)
        seen = seen + jnp.where(hit, 1, 0)
    tab[0] = table

    pl.semaphore_wait(barrier, len(peers))

    A, B = pl.ds(0, 256), pl.ds(256, 256)
    tabs = []
    for kx, kc in row_peers:
        slot = ((-kx) % 4) * 2 + kc
        tabs.append(go(transfer(tab.at[0], tab.at[slot], at(kx=kx, kc=kc))))

    D1, D2 = pl.ds(0, 224), pl.ds(224, 224)

    def part_of(kz, half=None):
        start = 448 + 144 * ((side + kz) % 4)
        if half is None:
            return pl.ds(pl.multiple_of(start, 16), 144)
        return pl.ds(pl.multiple_of(start + 80 * half, 16), (80, 64)[half])

    own = part_of(0)
    up, down = at(ky=1), at(ky=3)
    FA, FB = pl.ds(0, 4), pl.ds(4, 4)
    s_pa = go(transfer(source.at[FA], src[6].at[FA], at(kx=1)))
    s_mb = go(transfer(source.at[FB], src[2].at[FB], at(kx=3)))
    s_pb = go(transfer(source.at[FB], src[6].at[FB], at(kx=1)))
    s_ma = go(transfer(source.at[FA], src[2].at[FA], at(kx=3)))
    ys_p = go(transfer(target.at[own], tgt.at[y, own], up))
    ys_m = go(transfer(target.at[own], tgt.at[y, own], down))
    y1_p = go(transfer(target.at[D1], tgt.at[y, D1], up))
    y2_m = go(transfer(target.at[D2], tgt.at[y, D2], down))
    s_c = go(transfer(source, src[1], at(kc=1)))

    def z_both(k, rows):
        return (go(transfer(tgt.at[yi(k), rows], tgt.at[yi(k), rows], at(kz=1))),
                go(transfer(tgt.at[yi(k), rows], tgt.at[yi(k), rows], at(kz=3))))

    def z_on(k, z_p, z_m):
        out = []
        if z_p is not None:
            z_p.wait_recv()
            rows = part_of(3, 0)
            out.append(go(transfer(tgt.at[yi(k), rows], tgt.at[yi(k), rows], at(kz=1))))
        if z_m is not None:
            z_m.wait_recv()
            rows = part_of(1, 1)
            out.append(go(transfer(tgt.at[yi(k), rows], tgt.at[yi(k), rows], at(kz=3))))
        return out

    for t in tabs:
        t.wait_recv()
    listing = jnp.full((8, 128), 8, jnp.int32)
    for i in range(4):
        line = jnp.where(low, tab[2 * i], pltpu.roll(tab[2 * i + 1], 64, 1))
        listing = jnp.where(sub == i, line, listing)
    tabp[...] = listing
    copy_tab = pltpu.make_async_copy(tabp.at[pl.ds(0, 4)], stab, local_sem.at[2])
    copy_tab.start()

    ys_p.wait_recv()
    ya = part_of(0, 0)
    yb = part_of(0, 1)
    y2a = go(transfer(tgt.at[yi(3), ya], tgt.at[yi(3), ya], up))
    z3 = z_both(3, own)
    ys_m.wait_recv()
    y2b = go(transfer(tgt.at[yi(1), yb], tgt.at[yi(1), yb], down))
    z1 = z_both(1, own)
    y2_p = go(transfer(target.at[D2], tgt.at[y, D2], up))
    y1_m = go(transfer(target.at[D1], tgt.at[y, D1], down))

    def block(d, q, r):
        return stab[d // 2, (d % 2) * 64 + r * 32 + (x * 4 + q) * 2 + c]

    ones = jnp.full((8, 128), NEG, F32)
    for d in range(8):
        ftab[d * 16 + 8] = ones
        ltab[d * 16 + 8] = -ones

    scale = LOG2E / (REG * 16.0)
    eye = jnp.where(
        lax.broadcasted_iota(jnp.int32, (256, 256), 0)
        == lax.broadcasted_iota(jnp.int32, (256, 256), 1), 1.0, 0.0).astype(BF16)

    def unit(ky, kx):
        q = yi(ky)
        for d in (2 * kx, 2 * kx + 1):
            for r in range(2):
                b = jnp.minimum(block(d, q, r), 7)
                sq[pl.ds(d * 128 + r * 64, 64), :] = src[d][b]
        wide = pl.ds(kx * 256, 256)
        out = lax.dot_general(tgt[q], sq[wide, :], NT, preferred_element_type=F32) * scale
        logits[q, :, wide] = out
        top = jnp.max(jnp.max(out.reshape(128, 8, 256), axis=0), axis=0, keepdims=True)

        sums = jnp.zeros((8, 256), F32)
        for j in range(8):
            p = jnp.exp2(logits[q, pl.ds(j * 128, 128), wide] - top)
            sums = sums + jnp.sum(p.reshape(16, 8, 256), axis=0)
        rmax[q, 0:1, wide] = top
        rsum[q, 0:1, wide] = jnp.sum(sums, axis=0, keepdims=True)

    def turn(q):
        def body(j, _):
            rows = pl.ds(pl.multiple_of(j * 512, 512), 512)
            out = lax.dot_general(eye, tgt[q, rows, :], NT, preferred_element_type=F32)
            tgt_t[q, :, rows] = out.astype(BF16)
            return 0

        lax.fori_loop(0, 2, body, 0)

    R = 128

    def fold(value, op):
        return op(value.reshape(R // 8, 8, 128), axis=0)

    def lanes(d):
        return pl.ds(d * 128, 128)

    def row_single(q):
        def body(i, carry):
            rows = pl.ds(pl.multiple_of(i * R, R), R)
            g = gcol[q, rows, :]
            new = []
            for d in range(8):
                m, total = carry[d]
                t = logits[q, rows, lanes(d)] + g
                top = jnp.maximum(m, fold(t, jnp.max))
                p = jnp.exp2(t.reshape(R // 8, 8, 128) - top)
                new.append((top, total * jnp.exp2(m - top) + jnp.sum(p, axis=0)))
            return tuple(new)

        start = (jnp.full((8, 128), NEG, F32), jnp.zeros((8, 128), F32))
        done = lax.fori_loop(0, 1024 // R, body, (start,) * 8)
        for d, (m, total) in enumerate(done):
            top = jnp.max(m, axis=0, keepdims=True)
            rmax[q, 0:1, lanes(d)] = top
            rsum[q, 0:1, lanes(d)] = jnp.sum(total * jnp.exp2(m - top), axis=0, keepdims=True)

    def row_keep(q, ds):
        height = 1024 // len(ds) if len(ds) > 2 else 256

        def group(value, op):
            return op(value.reshape(height // 8, 8, 128), axis=0)

        def shifted(i):
            rows = pl.ds(pl.multiple_of(i * height, height), height)
            g = gcol[q, rows, :]
            return rows, [logits[q, rows, lanes(d)] + g for d in ds]

        def first(i, tops):
            return tuple(jnp.maximum(t, group(v, jnp.max)) for t, v in zip(tops, shifted(i)[1]))

        tops = lax.fori_loop(0, 1024 // height, first, (jnp.full((8, 128), NEG, F32),) * len(ds))
        tops = [jnp.max(t, axis=0, keepdims=True) for t in tops]

        def second(i, sums):
            rows, values = shifted(i)
            new = []
            for d, v, top, total in zip(ds, values, tops, sums):
                p = jnp.exp2(v - top)
                weights[q, rows, lanes(d)] = p.astype(BF16)
                new.append(total + group(p, jnp.sum))
            return tuple(new)

        sums = lax.fori_loop(0, 1024 // height, second, (jnp.zeros((8, 128), F32),) * len(ds))
        for d, top, total in zip(ds, tops, sums):
            rmax[q, 0:1, lanes(d)] = top
            rsum[q, 0:1, lanes(d)] = jnp.sum(total, axis=0, keepdims=True)

    def row_sum(d):
        terms = []
        for q in range(4):
            v = rmax[q, 0:1, lanes(d)] + jnp.log2(rsum[q, 0:1, lanes(d)])
            w = pltpu.roll(v, 64, 1)
            terms.append(jnp.where(sub == block(d, q, 0), jnp.where(low1, v, w), NEG))
            terms.append(jnp.where(sub == block(d, q, 1), jnp.where(low1, w, v), NEG))
        return lse(terms)

    def row_local(phase):
        for i in range(4):
            rowbuf[phase, 0, i] = jnp.where(low, row_sum(2 * i), row_sum(2 * i + 1))

    def row_start(phase):
        copies = []
        for kx, kc in row_peers:
            slot = ((-kx) % 4) * 2 + kc
            copies.append(go(transfer(rowbuf.at[phase, 0], rowbuf.at[phase, slot], at(kx=kx, kc=kc))))
        return copies

    def row_finish(phase, copies):
        for t in copies:
            t.wait_recv()
        for i in range(4):
            terms = [rowbuf[phase, 0, i]]
            for kx, kc in row_peers:
                v = rowbuf[phase, kx * 2 + kc, (i - kx) % 4]
                terms.append(pltpu.roll(v, 64, 1) if kc else v)
            total = -lse(terms)
            other = pltpu.roll(total, 64, 1)
            even = jnp.where(low, total, other)
            odd = jnp.where(low, other, total)
            for b in range(8):
                ftab[32 * i + b] = jnp.broadcast_to(even[b:b + 1], (8, 128))
                ftab[32 * i + 16 + b] = jnp.broadcast_to(odd[b:b + 1], (8, 128))

    def row_spread():
        for q in range(4):
            for d in range(8):
                f0 = ftab[d * 16 + block(d, q, 0)]
                f1 = ftab[d * 16 + block(d, q, 1)]
                frow[q, :, lanes(d)] = jnp.where(low, f0, f1)

    diag = (lax.broadcasted_iota(jnp.int32, (128, 128), 0)
            == lax.broadcasted_iota(jnp.int32, (128, 128), 1))
    C = 128

    def column(q, phase):
        fs = [frow[q, 0:1, lanes(d)] for d in range(8)]

        def body(i, _):
            rows = pl.ds(pl.multiple_of(i * C, C), C)
            ts = [logits[q, rows, lanes(d)] + fs[d] for d in range(8)]
            m = functools.reduce(jnp.maximum, ts)
            cmax[rows, :] = m
            csum[rows, :] = functools.reduce(jnp.add, [jnp.exp2(t - m) for t in ts])
            return 0

        lax.fori_loop(0, 1024 // C, body, 0)

        def merge(h, _):
            rows = pl.ds(pl.multiple_of(h * 512, 512), 512)
            m = cmax[rows, :]
            top = jnp.max(m, axis=1, keepdims=True)
            total = jnp.sum(csum[rows, :] * jnp.exp2(m - top), axis=1, keepdims=True)
            out = top + jnp.log2(total)
            lines = []
            for i in range(4):
                spread = jnp.broadcast_to(out[i * 128:(i + 1) * 128], (128, 128))
                lines.append(jnp.sum(jnp.where(diag, spread, 0.0), axis=0, keepdims=True))
            colbuf[phase, 0, q, pl.ds(pl.multiple_of(h * 4, 4), 4), :] = jnp.concatenate(lines, axis=0)
            return 0

        lax.fori_loop(0, 2, merge, 0)

    def over_y(phase, q):
        return [go(transfer(colbuf.at[phase, 0, q], colbuf.at[phase, (-k) % 4, q], at(ky=k))) for k in (1, 2, 3)]

    def over_z(phase, q, copies):
        for t in copies:
            t.wait_recv()
        ztot[phase, 0, q] = lse([colbuf[phase, k, q] for k in range(4)])
        return [go(transfer(ztot.at[phase, 0, q], ztot.at[phase, (-k) % 4, q], at(kz=k))) for k in (1, 2, 3)]

    def column_done(phase, q, copies):
        for t in copies:
            t.wait_recv()
        total = -lse([ztot[phase, (z - side + 4) % 4, q] for z in range(4)])
        gpack[q] = total
        for h in range(2):
            cols = []
            for i in range(4):
                line = jnp.broadcast_to(total[h * 4 + i:h * 4 + i + 1], (128, 128))
                cols.append(jnp.sum(jnp.where(diag, line, 0.0), axis=1, keepdims=True))
            for i in range(4):
                gcol[q, pl.ds((h * 4 + i) * 128, 128), :] = jnp.broadcast_to(cols[i], (128, 128))

    def columns_then_rows(phase):
        ys, zs = {}, {}
        for q in range(4):
            column(q, phase)
            ys[q] = over_y(phase, q)
            if q >= 2:
                zs[q - 2] = over_z(phase, q - 2, ys[q - 2])
        zs[2] = over_z(phase, 2, ys[2])
        for q in range(4):
            column_done(phase, q, zs[q])
            if phase < ITERS - 1:
                row_single(q)
            elif q < 3:
                row_keep(q, range(8))
            if q == 0:
                zs[3] = over_z(phase, 3, ys[3])

    own_src.wait()
    own_tgt.wait()
    s_c.wait_recv()
    copy_tab.wait()
    unit(0, 0)
    s_pa.wait_recv()
    s_fp = go(transfer(src[6].at[FA], src[4].at[FA], at(kx=1)))
    s_mb.wait_recv()
    s_fm = go(transfer(src[2].at[FB], src[4].at[FB], at(kx=3)))
    y1_p.wait_recv()
    y21 = go(transfer(tgt.at[yi(3), D1], tgt.at[yi(3), D1], up))
    y2_m.wait_recv()
    y22 = go(transfer(tgt.at[yi(1), D2], tgt.at[yi(1), D2], down))
    y2a.wait_recv()
    z2a = z_both(2, ya)
    y2b.wait_recv()
    z2b = z_both(2, yb)
    z3f = z_on(3, *z3)
    s_pb.wait_recv()
    s_cp = go(transfer(src[6], src[7], at(kc=1)))
    s_ma.wait_recv()
    s_cm = go(transfer(src[2], src[3], at(kc=1)))
    z1f = z_on(1, *z1)
    s_cp.wait_recv()
    unit(0, 3)
    s_cm.wait_recv()
    unit(0, 1)
    s_fp.wait_recv()
    s_c2a = go(transfer(src[4].at[FA], src[5].at[FA], at(kc=1)))
    s_fm.wait_recv()
    s_c2b = go(transfer(src[4].at[FB], src[5].at[FB], at(kc=1)))
    z2f = z_on(2, z2a[0], z2b[1])
    for t in (y2_p, *z3f):
        t.wait_recv()
    for kx in (0, 1, 3):
        unit(3, kx)
    s_c2a.wait_recv()
    s_c2b.wait_recv()
    unit(0, 2)
    unit(3, 2)
    for t in (y1_m, *z1f):
        t.wait_recv()
    for kx in range(4):
        unit(1, kx)
    for t in (y21, y22, z2a[1], z2b[0], *z2f):
        t.wait_recv()
    for kx in range(4):
        unit(2, kx)

    for phase in range(ITERS):
        row_local(phase)
        copies = row_start(phase)
        if phase == 0:
            for q in range(4):
                turn(q)
        row_finish(phase, copies)
        row_spread()
        if phase == ITERS - 1:
            even = jnp.concatenate([ftab[2 * i][0:1] for i in range(4)], axis=0)
            odd = jnp.concatenate([ftab[2 * i + 1][0:1] for i in range(4)], axis=0)
            f_out[...] = jnp.where(low[0:4], even, odd) * (REG * LN2)
        columns_then_rows(phase)

    g_out[...] = gpack[y] * (REG * LN2)
    row_id = lax.broadcasted_iota(jnp.int32, (64, 256), 0)
    col_id = lax.broadcasted_iota(jnp.int32, (64, 256), 1)
    same = row_id == col_id % 64
    col_block = col_id // 64

    def prepare(kx):
        row_keep(3, (2 * kx, 2 * kx + 1))
        for d in (2 * kx, 2 * kx + 1):
            out = row_sum(d)
            for b in range(8):
                ltab[d * 16 + b] = jnp.broadcast_to(out[b:b + 1], (8, 128))
            for h in range(2):
                pieces = [jnp.where(low1, out[b:b + 1], out[b + 1:b + 2]) for b in (4 * h, 4 * h + 2)]
                stat[d, h] = jnp.broadcast_to(jnp.concatenate(pieces, axis=1), (8, 256))
        wide = pl.ds(kx * 256, 256)
        for q in range(4):
            out = jnp.dot(tgt_t[q], weights[q, :, wide], preferred_element_type=F32)
            for i in range(2):
                d = 2 * kx + i
                one = jnp.where(low, ltab[d * 16 + block(d, q, 0)], ltab[d * 16 + block(d, q, 1)])
                factor = jnp.exp2(rmax[q, 0:1, lanes(d)] - one[0:1])
                numer[q, :, lanes(d)] = (out[:, i * 128:(i + 1) * 128] * factor).astype(BF16)

    def assemble(d):
        value = jnp.concatenate([numer[q, :, lanes(d)] for q in range(4)], axis=1)
        for h in range(2):
            picks = []
            for q in range(4):
                for r in range(2):
                    hit = jnp.logical_and(same, col_block == block(d, q, r) - 4 * h)
                    picks.append(jnp.where(hit, 1.0, 0.0).astype(BF16))
            pick = jnp.concatenate(picks, axis=0)
            part[d, h] = jnp.dot(value, pick, preferred_element_type=F32).astype(BF16)

    def merge(terms):
        stats = [st[...] for _, st in terms]
        joint = lse(stats)
        total = None
        for (value, _), st in zip(terms, stats):
            term = value[...].astype(F32).reshape(32, 8, 256) * jnp.exp2(st - joint)
            total = term if total is None else total + term
        return total.reshape(256, 256).astype(BF16), joint

    def own_part(d, h):
        return part.at[d, h], stat.at[d, h]

    def from_core(kx, h):
        return pin.at[kx, h], pstat.at[kx, h]

    to_core = {}

    def give(kx):
        d = kx * 2 + 1
        assemble(d)
        to_core[kx] = [go(transfer(part.at[d], pin.at[kx], at(kc=1))),
                       go(transfer(stat.at[d], pstat.at[kx], at(kc=1)))]

    def take(copies):
        for t in copies:
            t.wait_recv()

    def join(kx, h, extra=()):
        comb[kx, h], cstat[kx, h] = merge([own_part(2 * kx, h), from_core(kx, h), *extra])

    def pass_on(kx, h, n, far, device):
        values, stats = (hin, hstat) if far else (rin, rstat)
        index = (n,) if far else (n, h)
        return [go(transfer(comb.at[kx, h], values.at[index], device)),
                go(transfer(cstat.at[kx, h], stats.at[index], device))]

    right, left = at(kx=1), at(kx=3)
    prepare(2)
    give(2)
    assemble(4)
    prepare(1)
    take(to_core[2])
    join(2, 0)
    h_p = pass_on(2, 0, 0, True, right)
    join(2, 1)
    h_m = pass_on(2, 1, 1, True, left)
    give(1)
    assemble(2)
    prepare(3)
    take(to_core[1])
    join(1, 1)
    r_p1 = pass_on(1, 1, 0, False, right)
    give(3)
    assemble(6)
    prepare(0)
    take(to_core[3])
    join(3, 0)
    r_m0 = pass_on(3, 0, 1, False, left)
    give(0)
    assemble(0)
    take(h_p)
    join(1, 0, [(hin.at[0], hstat.at[0])])
    r_p0 = pass_on(1, 0, 0, False, right)
    take(h_m)
    join(3, 1, [(hin.at[1], hstat.at[1])])
    r_m1 = pass_on(3, 1, 1, False, left)
    take(to_core[0])
    for h, copies in ((0, r_p0 + r_m0), (1, r_p1 + r_m1)):
        take(copies)
        out, _ = merge([own_part(0, h), from_core(0, h),
                        (rin.at[0, h], rstat.at[0, h]), (rin.at[1, h], rstat.at[1, h])])
        turned = lax.dot_general(eye, out, NT, preferred_element_type=F32)
        mapped[pl.ds(h * 256, 256), :] = turned.astype(BF16)

    for t in sent:
        t.wait_send()


COPIES = 42 + 7 * ITERS + 24 * ITERS + 20


def hand_over(f_in, g_in, m_in, f_out, g_out, m_out, f, g, m, in_sem, out_sem):
    jobs = [(m_in.at[pl.ds(i * 128, 128)], m.at[pl.ds(i * 128, 128)], m_out.at[pl.ds(i * 128, 128)]) for i in range(4)]
    jobs += [(f_in, f, f_out), (g_in, g, g_out)]
    first = [pltpu.make_async_copy(a, b, in_sem.at[n]) for n, (a, b, _) in enumerate(jobs)]
    second = [pltpu.make_async_copy(b, o, out_sem.at[n]) for n, (_, b, o) in enumerate(jobs)]
    for copy in first:
        copy.start()
    for copy, follow in zip(first, second):
        copy.wait()
        follow.start()
    for copy in second:
        copy.wait()


def shards(source, target, pairs, owner_map):
    any_space = pl.BlockSpec(memory_space=pl.ANY)
    smem = pl.BlockSpec(memory_space=pltpu.SMEM)
    vmem = pl.BlockSpec(memory_space=pltpu.VMEM)
    f, g, mapped = pl.pallas_call(
        kernel,
        out_shape=(
            jax.ShapeDtypeStruct((4, 128), F32),
            jax.ShapeDtypeStruct((8, 128), F32),
            jax.ShapeDtypeStruct((512, 256), BF16),
        ),
        in_specs=[any_space, any_space, smem, smem],
        out_specs=(vmem, vmem, vmem),
        scratch_shapes=[
            *[pltpu.VMEM((8, 64, 256), BF16)] * 8,
            pltpu.VMEM((4, 1024, 256), BF16),
            pltpu.VMEM((8, 8, 128), jnp.int32),
            pltpu.VMEM((8, 128), jnp.int32),
            pltpu.SMEM((4, 128), jnp.int32),
            pltpu.VMEM((1024, 256), BF16),
            pltpu.VMEM((4, 1024, 1024), F32),
            pltpu.VMEM((4, 1024, 1024), BF16),
            pltpu.VMEM((4, 256, 1024), BF16),
            pltpu.VMEM((4, 1024, 128), F32),
            pltpu.VMEM((1024, 128), F32),
            pltpu.VMEM((1024, 128), F32),
            pltpu.VMEM((4, 8, 1024), F32),
            pltpu.VMEM((4, 8, 1024), F32),
            pltpu.VMEM((ITERS, 8, 4, 8, 128), F32),
            pltpu.VMEM((128, 8, 128), F32),
            pltpu.VMEM((128, 8, 128), F32),
            pltpu.VMEM((4, 8, 1024), F32),
            pltpu.VMEM((ITERS, 4, 4, 8, 128), F32),
            pltpu.VMEM((ITERS, 4, 4, 8, 128), F32),
            pltpu.VMEM((4, 8, 128), F32),
            pltpu.VMEM((4, 256, 1024), BF16),
            pltpu.VMEM((8, 2, 256, 256), BF16),
            pltpu.VMEM((4, 2, 256, 256), BF16),
            pltpu.VMEM((4, 2, 256, 256), BF16),
            pltpu.VMEM((2, 2, 256, 256), BF16),
            pltpu.VMEM((2, 256, 256), BF16),
            pltpu.VMEM((8, 2, 8, 256), F32),
            pltpu.VMEM((4, 2, 8, 256), F32),
            pltpu.VMEM((4, 2, 8, 256), F32),
            pltpu.VMEM((2, 2, 8, 256), F32),
            pltpu.VMEM((2, 8, 256), F32),
            pltpu.SemaphoreType.DMA((COPIES,)),
            pltpu.SemaphoreType.DMA((COPIES,)),
            pltpu.SemaphoreType.DMA((3,)),
        ],
        compiler_params=pltpu.CompilerParams(
            collective_id=0, has_side_effects=True, vmem_limit_bytes=60 * 1024 * 1024
        ),
        name="sinkhorn",
    )(source.reshape(8, 64, 256), target, pairs.T, owner_map)
    f, g, mapped = pl.pallas_call(
        hand_over,
        out_shape=(
            jax.ShapeDtypeStruct((4, 128), F32),
            jax.ShapeDtypeStruct((8, 128), F32),
            jax.ShapeDtypeStruct((512, 256), BF16),
        ),
        in_specs=[any_space] * 3,
        out_specs=(any_space,) * 3,
        scratch_shapes=[
            pltpu.VMEM((4, 128), F32),
            pltpu.VMEM((8, 128), F32),
            pltpu.VMEM((512, 256), BF16),
            pltpu.SemaphoreType.DMA((8,)),
            pltpu.SemaphoreType.DMA((8,)),
        ],
        name="hand_over",
    )(f, g, mapped)
    return f.reshape(512), g.reshape(1024), mapped


def solution(mesh):
    return jax.shard_map(
        shards,
        mesh=mesh,
        in_specs=(P(("side", "blk"), None), P("blk", None), P(("side", "blk"), None), P()),
        out_specs=(P(("side", "blk")), P("blk"), P(("side", "blk"), None)),
        check_vma=False,
    )
```

```python
import functools
import math

import jax
import jax.numpy as jnp
from jax import lax
from jax.experimental import pallas as pl
from jax.experimental.pallas import tpu as pltpu
from jax.sharding import PartitionSpec as P

MESH = pl.DeviceIdType.MESH
NEG = -1e30
LOG2E = 1.4426950408889634
LN2 = 0.6931471805599453
REG = 0.3
ITERS = 2
NT = (((1,), (1,)), ((), ()))
F32 = jnp.float32
BF16 = jnp.bfloat16


def lse(parts):
    top = functools.reduce(jnp.maximum, parts)
    total = functools.reduce(jnp.add, [jnp.exp2(p - top) for p in parts])
    return top + jnp.log2(total)


def kernel(
    source, target, pairs, owner_map, f_out, g_out, mapped,
    src0, src1, src2, src3, src4, src5, src6, src7, tgt, tab, tabp, stab, sq, logits, weights, tgt_t, gcol, cmax, csum,
    rmax, rsum, rowbuf, ftab, ltab, frow, colbuf, ztot, gpack, numer, part, comb, pin, rin, hin,
    stat, cstat, pstat, rstat, hstat, send_sem, recv_sem, local_sem,
):
    src = (src0, src1, src2, src3, src4, src5, src6, src7)
    side = lax.axis_index("side")
    blk = lax.axis_index("blk")
    x = blk // 8
    y = (blk // 2) % 4
    c = blk % 2

    def at(kx=0, kc=0, ky=0, kz=0):
        xx = (x + kx) % 4
        yy = (y + ky) % 4
        cc = (c + kc) % 2
        zz = (side + kz) % 4
        return (zz, (xx * 4 + yy) * 2 + cc)

    def yi(k):
        return (y + k) % 4

    count = [0]

    def transfer(source_ref, dest_ref, device):
        n = count[0]
        count[0] += 1
        return pltpu.make_async_remote_copy(
            src_ref=source_ref, dst_ref=dest_ref,
            send_sem=send_sem.at[n], recv_sem=recv_sem.at[n],
            device_id=device, device_id_type=MESH,
        )

    sent = []

    def go(copy):
        copy.start()
        sent.append(copy)
        return copy

    row_peers = [(kx, kc) for kx in range(4) for kc in range(2)][1:]
    peers = [at(kx=kx, kc=kc) for kx, kc in row_peers]
    peers += [at(ky=k) for k in (1, 2, 3)] + [at(kz=k) for k in (1, 2, 3)]
    barrier = pltpu.get_barrier_semaphore()
    for peer in peers:
        pl.semaphore_signal(barrier, inc=1, device_id=peer, device_id_type=MESH)

    own_src = pltpu.make_async_copy(source, src[0], local_sem.at[0])
    own_src.start()
    own_tgt = pltpu.make_async_copy(target, tgt.at[y], local_sem.at[1])
    own_tgt.start()

    lane = lax.broadcasted_iota(jnp.int32, (8, 128), 1)
    sub = lax.broadcasted_iota(jnp.int32, (8, 128), 0)
    low = lane < 64
    low1 = low[0:1]

    target_lane = lane % 32
    turn_lane = lane // 32
    seen = jnp.zeros((8, 128), jnp.int32)
    table = jnp.full((8, 128), 8, jnp.int32)
    for s in range(8):
        hit = target_lane == owner_map[pairs[0, s]]
        for k in range(1, 4):
            hit = jnp.logical_or(hit, target_lane == owner_map[pairs[k, s]])
        table = jnp.where(jnp.logical_and(hit, seen == turn_lane), s, table)
        seen = seen + jnp.where(hit, 1, 0)
    tab[0] = table

    pl.semaphore_wait(barrier, len(peers))

    A, B = pl.ds(0, 256), pl.ds(256, 256)
    tabs = []
    for kx, kc in row_peers:
        slot = ((-kx) % 4) * 2 + kc
        tabs.append(go(transfer(tab.at[0], tab.at[slot], at(kx=kx, kc=kc))))

    D1, D2 = pl.ds(0, 224), pl.ds(224, 224)

    def part_of(kz, half=None):
        start = 448 + 144 * ((side + kz) % 4)
        if half is None:
            return pl.ds(pl.multiple_of(start, 16), 144)
        return pl.ds(pl.multiple_of(start + 80 * half, 16), (80, 64)[half])

    own = part_of(0)
    up, down = at(ky=1), at(ky=3)
    FA, FB = pl.ds(0, 4), pl.ds(4, 4)
    s_pa = go(transfer(source.at[FA], src[6].at[FA], at(kx=1)))
    s_mb = go(transfer(source.at[FB], src[2].at[FB], at(kx=3)))
    s_pb = go(transfer(source.at[FB], src[6].at[FB], at(kx=1)))
    s_ma = go(transfer(source.at[FA], src[2].at[FA], at(kx=3)))
    ys_p = go(transfer(target.at[own], tgt.at[y, own], up))
    ys_m = go(transfer(target.at[own], tgt.at[y, own], down))
    y1_p = go(transfer(target.at[D1], tgt.at[y, D1], up))
    y2_m = go(transfer(target.at[D2], tgt.at[y, D2], down))
    s_c = go(transfer(source, src[1], at(kc=1)))

    def z_both(k, rows):
        return (go(transfer(tgt.at[yi(k), rows], tgt.at[yi(k), rows], at(kz=1))),
                go(transfer(tgt.at[yi(k), rows], tgt.at[yi(k), rows], at(kz=3))))

    def z_on(k, z_p, z_m):
        out = []
        if z_p is not None:
            z_p.wait_recv()
            rows = part_of(3, 0)
            out.append(go(transfer(tgt.at[yi(k), rows], tgt.at[yi(k), rows], at(kz=1))))
        if z_m is not None:
            z_m.wait_recv()
            rows = part_of(1, 1)
            out.append(go(transfer(tgt.at[yi(k), rows], tgt.at[yi(k), rows], at(kz=3))))
        return out

    for t in tabs:
        t.wait_recv()
    listing = jnp.full((8, 128), 8, jnp.int32)
    for i in range(4):
        line = jnp.where(low, tab[2 * i], pltpu.roll(tab[2 * i + 1], 64, 1))
        listing = jnp.where(sub == i, line, listing)
    tabp[...] = listing
    copy_tab = pltpu.make_async_copy(tabp.at[pl.ds(0, 4)], stab, local_sem.at[2])
    copy_tab.start()

    ys_p.wait_recv()
    ya = part_of(0, 0)
    yb = part_of(0, 1)
    y2a = go(transfer(tgt.at[yi(3), ya], tgt.at[yi(3), ya], up))
    z3 = z_both(3, own)
    ys_m.wait_recv()
    y2b = go(transfer(tgt.at[yi(1), yb], tgt.at[yi(1), yb], down))
    z1 = z_both(1, own)
    y2_p = go(transfer(target.at[D2], tgt.at[y, D2], up))
    y1_m = go(transfer(target.at[D1], tgt.at[y, D1], down))

    def block(d, q, r):
        return stab[d // 2, (d % 2) * 64 + r * 32 + (x * 4 + q) * 2 + c]

    ones = jnp.full((8, 128), NEG, F32)
    for d in range(8):
        ftab[d * 16 + 8] = ones
        ltab[d * 16 + 8] = -ones

    scale = LOG2E / (REG * 16.0)
    eye = jnp.where(
        lax.broadcasted_iota(jnp.int32, (256, 256), 0)
        == lax.broadcasted_iota(jnp.int32, (256, 256), 1), 1.0, 0.0).astype(BF16)

    def unit(ky, kx):
        q = yi(ky)
        for d in (2 * kx, 2 * kx + 1):
            for r in range(2):
                b = jnp.minimum(block(d, q, r), 7)
                sq[pl.ds(d * 128 + r * 64, 64), :] = src[d][b]
        wide = pl.ds(kx * 256, 256)
        out = lax.dot_general(tgt[q], sq[wide, :], NT, preferred_element_type=F32) * scale
        logits[q, :, wide] = out
        top = jnp.max(jnp.max(out.reshape(128, 8, 256), axis=0), axis=0, keepdims=True)

        sums = jnp.zeros((8, 256), F32)
        for j in range(8):
            p = jnp.exp2(logits[q, pl.ds(j * 128, 128), wide] - top)
            sums = sums + jnp.sum(p.reshape(16, 8, 256), axis=0)
        rmax[q, 0:1, wide] = top
        rsum[q, 0:1, wide] = jnp.sum(sums, axis=0, keepdims=True)

    def turn(q):
        def body(j, _):
            rows = pl.ds(pl.multiple_of(j * 512, 512), 512)
            out = lax.dot_general(eye, tgt[q, rows, :], NT, preferred_element_type=F32)
            tgt_t[q, :, rows] = out.astype(BF16)
            return 0

        lax.fori_loop(0, 2, body, 0)

    R = 128

    def fold(value, op):
        return op(value.reshape(R // 8, 8, 128), axis=0)

    def lanes(d):
        return pl.ds(d * 128, 128)

    def row_single(q):
        def body(i, carry):
            for j in range(2):
                rows = pl.ds(pl.multiple_of(i * R + j * 64, 64), 64)
                g = gcol[q, rows, :]
                new = []
                for d in range(8):
                    m, total = carry[d]
                    t = (logits[q, rows, lanes(d)] + g).reshape(8, 8, 128)
                    top = jnp.maximum(m, jnp.max(t, axis=0))
                    p = jnp.exp2(t - top)
                    new.append((top, total * jnp.exp2(m - top) + jnp.sum(p, axis=0)))
                carry = tuple(new)
            return carry

        def twice(i, carry):
            return body(2 * i + 1, body(2 * i, carry))

        start = (jnp.full((8, 128), NEG, F32), jnp.zeros((8, 128), F32))
        done = lax.fori_loop(0, 512 // R, twice, (start,) * 8)
        for d, (m, total) in enumerate(done):
            top = jnp.max(m, axis=0, keepdims=True)
            rmax[q, 0:1, lanes(d)] = top
            rsum[q, 0:1, lanes(d)] = jnp.sum(total * jnp.exp2(m - top), axis=0, keepdims=True)

    def row_keep(q, ds):
        height = 64 if len(ds) > 2 else 256

        def group(value, op):
            return op(value.reshape(height // 8, 8, 128), axis=0)

        def first(i, tops):
            rows = pl.ds(pl.multiple_of(i * height, height), height)
            g = gcol[q, rows, :]
            return tuple(jnp.maximum(t, group(logits[q, rows, lanes(d)] + g, jnp.max)) for d, t in zip(ds, tops))

        def second(i, sums):
            rows = pl.ds(pl.multiple_of(i * height, height), height)
            g = gcol[q, rows, :]
            new = []
            for d, top, total in zip(ds, tops, sums):
                p = jnp.exp2(logits[q, rows, lanes(d)] + g - top)
                weights[q, rows, lanes(d)] = p.astype(BF16)
                new.append(total + group(p, jnp.sum))
            return tuple(new)

        def sweep(step, start):
            count = 1024 // height
            pair = lambda i, carry: step(2 * i + 1, step(2 * i, carry))
            return lax.fori_loop(0, count // 2, pair, start)

        tops = sweep(first, (jnp.full((8, 128), NEG, F32),) * len(ds))
        tops = [jnp.max(t, axis=0, keepdims=True) for t in tops]
        sums = sweep(second, (jnp.zeros((8, 128), F32),) * len(ds))
        for d, top, total in zip(ds, tops, sums):
            rmax[q, 0:1, lanes(d)] = top
            rsum[q, 0:1, lanes(d)] = jnp.sum(total, axis=0, keepdims=True)

    def row_sum(d):
        terms = []
        for q in range(4):
            v = rmax[q, 0:1, lanes(d)] + jnp.log2(rsum[q, 0:1, lanes(d)])
            w = pltpu.roll(v, 64, 1)
            terms.append(jnp.where(sub == block(d, q, 0), jnp.where(low1, v, w), NEG))
            terms.append(jnp.where(sub == block(d, q, 1), jnp.where(low1, w, v), NEG))
        return lse(terms)

    def row_local(phase):
        for i in range(4):
            rowbuf[phase, 0, i] = jnp.where(low, row_sum(2 * i), row_sum(2 * i + 1))

    def row_start(phase):
        copies = []
        for kx, kc in row_peers:
            slot = ((-kx) % 4) * 2 + kc
            copies.append(go(transfer(rowbuf.at[phase, 0], rowbuf.at[phase, slot], at(kx=kx, kc=kc))))
        return copies

    def row_finish(phase, copies):
        for t in copies:
            t.wait_recv()
        for i in range(4):
            terms = [rowbuf[phase, 0, i]]
            for kx, kc in row_peers:
                v = rowbuf[phase, kx * 2 + kc, (i - kx) % 4]
                terms.append(pltpu.roll(v, 64, 1) if kc else v)
            total = -lse(terms)
            other = pltpu.roll(total, 64, 1)
            even = jnp.where(low, total, other)
            odd = jnp.where(low, other, total)
            for b in range(8):
                ftab[32 * i + b] = jnp.broadcast_to(even[b:b + 1], (8, 128))
                ftab[32 * i + 16 + b] = jnp.broadcast_to(odd[b:b + 1], (8, 128))

    def row_spread():
        for q in range(4):
            for d in range(8):
                f0 = ftab[d * 16 + block(d, q, 0)]
                f1 = ftab[d * 16 + block(d, q, 1)]
                frow[q, :, lanes(d)] = jnp.where(low, f0, f1)

    diag = (lax.broadcasted_iota(jnp.int32, (128, 128), 0)
            == lax.broadcasted_iota(jnp.int32, (128, 128), 1))
    C = 8

    def column(q, phase):
        fs = [frow[q, 0:1, lanes(d)] for d in range(8)]

        def chunk(i):
            for j in range(128 // C):
                rows = pl.ds(pl.multiple_of(i * 128 + j * C, C), C)
                ts = [logits[q, rows, lanes(d)] + fs[d] for d in range(8)]
                m = functools.reduce(jnp.maximum, ts)
                cmax[rows, :] = m
                csum[rows, :] = functools.reduce(jnp.add, [jnp.exp2(t - m) for t in ts])

        def merge(i):
            rows = pl.ds(pl.multiple_of(i * 128, 128), 128)
            m = cmax[rows, :]
            top = jnp.max(m, axis=1, keepdims=True)
            total = jnp.sum(csum[rows, :] * jnp.exp2(m - top), axis=1, keepdims=True)
            spread = jnp.broadcast_to(top + jnp.log2(total), (128, 128))
            line = jnp.sum(jnp.where(diag, spread, 0.0), axis=0, keepdims=True)
            colbuf[phase, 0, q, pl.ds(i, 1), :] = line

        def body(i, _):
            merge(2 * i - 2)
            merge(2 * i - 1)
            chunk(2 * i)
            chunk(2 * i + 1)
            return 0

        chunk(0)
        chunk(1)
        lax.fori_loop(1, 4, body, 0)
        merge(6)
        merge(7)

    def over_y(phase, q):
        return [go(transfer(colbuf.at[phase, 0, q], colbuf.at[phase, (-k) % 4, q], at(ky=k))) for k in (1, 2, 3)]

    def over_z(phase, q, copies):
        for t in copies:
            t.wait_recv()
        ztot[phase, 0, q] = lse([colbuf[phase, k, q] for k in range(4)])
        return [go(transfer(ztot.at[phase, 0, q], ztot.at[phase, (-k) % 4, q], at(kz=k))) for k in (1, 2, 3)]

    def column_done(phase, q, copies):
        for t in copies:
            t.wait_recv()
        total = -lse([ztot[phase, (z - side + 4) % 4, q] for z in range(4)])
        gpack[q] = total
        for h in range(2):
            cols = []
            for i in range(4):
                line = jnp.broadcast_to(total[h * 4 + i:h * 4 + i + 1], (128, 128))
                cols.append(jnp.sum(jnp.where(diag, line, 0.0), axis=1, keepdims=True))
            for i in range(4):
                gcol[q, pl.ds((h * 4 + i) * 128, 128), :] = jnp.broadcast_to(cols[i], (128, 128))

    def columns_then_rows(phase):
        ys, zs = {}, {}
        for q in range(4):
            column(q, phase)
            ys[q] = over_y(phase, q)
            if q >= 2:
                zs[q - 2] = over_z(phase, q - 2, ys[q - 2])
        zs[2] = over_z(phase, 2, ys[2])
        for q in range(4):
            column_done(phase, q, zs[q])
            if phase < ITERS - 1:
                row_single(q)
            elif q < 3:
                row_keep(q, range(8))
            if q == 0:
                zs[3] = over_z(phase, 3, ys[3])

    own_src.wait()
    own_tgt.wait()
    s_c.wait_recv()
    copy_tab.wait()
    unit(0, 0)
    s_pa.wait_recv()
    s_fp = go(transfer(src[6].at[FA], src[4].at[FA], at(kx=1)))
    s_mb.wait_recv()
    s_fm = go(transfer(src[2].at[FB], src[4].at[FB], at(kx=3)))
    y1_p.wait_recv()
    y21 = go(transfer(tgt.at[yi(3), D1], tgt.at[yi(3), D1], up))
    y2_m.wait_recv()
    y22 = go(transfer(tgt.at[yi(1), D2], tgt.at[yi(1), D2], down))
    y2a.wait_recv()
    z2a = z_both(2, ya)
    y2b.wait_recv()
    z2b = z_both(2, yb)
    z3f = z_on(3, *z3)
    s_pb.wait_recv()
    s_cp = go(transfer(src[6], src[7], at(kc=1)))
    s_ma.wait_recv()
    s_cm = go(transfer(src[2], src[3], at(kc=1)))
    z1f = z_on(1, *z1)
    s_cp.wait_recv()
    unit(0, 3)
    s_cm.wait_recv()
    unit(0, 1)
    s_fp.wait_recv()
    s_c2a = go(transfer(src[4].at[FA], src[5].at[FA], at(kc=1)))
    s_fm.wait_recv()
    s_c2b = go(transfer(src[4].at[FB], src[5].at[FB], at(kc=1)))
    z2f = z_on(2, z2a[0], z2b[1])
    for t in (y2_p, *z3f):
        t.wait_recv()
    for kx in (0, 1, 3):
        unit(3, kx)
    s_c2a.wait_recv()
    s_c2b.wait_recv()
    unit(0, 2)
    unit(3, 2)
    for t in (y1_m, *z1f):
        t.wait_recv()
    for kx in range(4):
        unit(1, kx)
    for t in (y21, y22, z2a[1], z2b[0], *z2f):
        t.wait_recv()
    for kx in range(4):
        unit(2, kx)

    for phase in range(ITERS):
        row_local(phase)
        copies = row_start(phase)
        if phase == 0:
            for q in range(4):
                turn(q)
        row_finish(phase, copies)
        row_spread()
        if phase == ITERS - 1:
            even = jnp.concatenate([ftab[2 * i][0:1] for i in range(4)], axis=0)
            odd = jnp.concatenate([ftab[2 * i + 1][0:1] for i in range(4)], axis=0)
            f_out[...] = jnp.where(low[0:4], even, odd) * (REG * LN2)
        columns_then_rows(phase)

    g_out[...] = gpack[y] * (REG * LN2)
    row_id = lax.broadcasted_iota(jnp.int32, (64, 256), 0)
    col_id = lax.broadcasted_iota(jnp.int32, (64, 256), 1)
    same = row_id == col_id % 64
    col_block = col_id // 64

    def prepare(kx):
        for d in (2 * kx, 2 * kx + 1):
            out = row_sum(d)
            for b in range(8):
                ltab[d * 16 + b] = jnp.broadcast_to(out[b:b + 1], (8, 128))
            for h in range(2):
                pieces = [jnp.where(low1, out[b:b + 1], out[b + 1:b + 2]) for b in (4 * h, 4 * h + 2)]
                stat[d, h] = jnp.broadcast_to(jnp.concatenate(pieces, axis=1), (8, 256))
        wide = pl.ds(kx * 256, 256)
        for q in range(4):
            out = jnp.dot(tgt_t[q], weights[q, :, wide], preferred_element_type=F32)
            for i in range(2):
                d = 2 * kx + i
                one = jnp.where(low, ltab[d * 16 + block(d, q, 0)], ltab[d * 16 + block(d, q, 1)])
                factor = jnp.exp2(rmax[q, 0:1, lanes(d)] - one[0:1])
                numer[q, :, lanes(d)] = (out[:, i * 128:(i + 1) * 128] * factor).astype(BF16)

    def assemble(d, halves=(0, 1)):
        value = jnp.concatenate([numer[q, :, lanes(d)] for q in range(4)], axis=1)
        for h in halves:
            picks = []
            for q in range(4):
                for r in range(2):
                    hit = jnp.logical_and(same, col_block == block(d, q, r) - 4 * h)
                    picks.append(jnp.where(hit, 1.0, 0.0).astype(BF16))
            pick = jnp.concatenate(picks, axis=0)
            part[d, h] = jnp.dot(value, pick, preferred_element_type=F32).astype(BF16)

    def merge(terms):
        stats = [st[...] for _, st in terms]
        joint = lse(stats)
        total = None
        for (value, _), st in zip(terms, stats):
            term = value[...].astype(F32).reshape(32, 8, 256) * jnp.exp2(st - joint)
            total = term if total is None else total + term
        return total.reshape(256, 256).astype(BF16), joint

    def own_part(d, h):
        return part.at[d, h], stat.at[d, h]

    def from_core(kx, h):
        return pin.at[kx, h], pstat.at[kx, h]

    to_core = {}

    def give(kx):
        d = kx * 2 + 1
        assemble(d)
        to_core[kx] = [go(transfer(part.at[d], pin.at[kx], at(kc=1))),
                       go(transfer(stat.at[d], pstat.at[kx], at(kc=1)))]

    def give_half(kx, h):
        d = kx * 2 + 1
        assemble(d, (h,))
        to_core[kx, h] = [go(transfer(part.at[d, h], pin.at[kx, h], at(kc=1))),
                          go(transfer(stat.at[d, h], pstat.at[kx, h], at(kc=1)))]

    def take(copies):
        for t in copies:
            t.wait_recv()

    def join(kx, h, extra=()):
        comb[kx, h], cstat[kx, h] = merge([own_part(2 * kx, h), from_core(kx, h), *extra])

    def pass_on(kx, h, n, far, device):
        values, stats = (hin, hstat) if far else (rin, rstat)
        index = (n,) if far else (n, h)
        return [go(transfer(comb.at[kx, h], values.at[index], device)),
                go(transfer(cstat.at[kx, h], stats.at[index], device))]

    right, left = at(kx=1), at(kx=3)
    row_keep(3, (4, 5))
    prepare(2)
    give(2)
    assemble(4)
    row_keep(3, (2, 3))
    take(to_core[2])
    join(2, 0)
    h_p = pass_on(2, 0, 0, True, right)
    join(2, 1)
    h_m = pass_on(2, 1, 1, True, left)
    prepare(1)
    give_half(1, 1)
    row_keep(3, (6, 7))
    prepare(3)
    give_half(3, 0)
    assemble(2, (1,))
    take(to_core[1, 1])
    join(1, 1)
    r_p1 = pass_on(1, 1, 0, False, right)
    assemble(6, (0,))
    take(to_core[3, 0])
    join(3, 0)
    r_m0 = pass_on(3, 0, 1, False, left)
    give_half(1, 0)
    give_half(3, 1)
    assemble(2, (0,))
    assemble(6, (1,))
    take(to_core[1, 0])
    take(h_p)
    join(1, 0, [(hin.at[0], hstat.at[0])])
    r_p0 = pass_on(1, 0, 0, False, right)
    take(to_core[3, 1])
    take(h_m)
    join(3, 1, [(hin.at[1], hstat.at[1])])
    r_m1 = pass_on(3, 1, 1, False, left)
    row_keep(3, (0, 1))
    prepare(0)
    give(0)
    assemble(0)
    take(to_core[0])
    for h, copies in ((0, r_p0 + r_m0), (1, r_p1 + r_m1)):
        take(copies)
        out, _ = merge([own_part(0, h), from_core(0, h),
                        (rin.at[0, h], rstat.at[0, h]), (rin.at[1, h], rstat.at[1, h])])
        turned = lax.dot_general(eye, out, NT, preferred_element_type=F32)
        mapped[pl.ds(h * 256, 256), :] = turned.astype(BF16)

    for t in sent:
        t.wait_send()


COPIES = 42 + 7 * ITERS + 24 * ITERS + 24


def hand_over(f_in, g_in, m_in, f_out, g_out, m_out, f, g, m, in_sem, out_sem):
    jobs = [(m_in.at[pl.ds(i * 128, 128)], m.at[pl.ds(i * 128, 128)], m_out.at[pl.ds(i * 128, 128)]) for i in range(4)]
    jobs += [(f_in, f, f_out), (g_in, g, g_out)]
    first = [pltpu.make_async_copy(a, b, in_sem.at[n]) for n, (a, b, _) in enumerate(jobs)]
    second = [pltpu.make_async_copy(b, o, out_sem.at[n]) for n, (_, b, o) in enumerate(jobs)]
    for copy in first:
        copy.start()
    for copy, follow in zip(first, second):
        copy.wait()
        follow.start()
    for copy in second:
        copy.wait()


def shards(source, target, pairs, owner_map):
    any_space = pl.BlockSpec(memory_space=pl.ANY)
    smem = pl.BlockSpec(memory_space=pltpu.SMEM)
    vmem = pl.BlockSpec(memory_space=pltpu.VMEM)
    f, g, mapped = pl.pallas_call(
        kernel,
        out_shape=(
            jax.ShapeDtypeStruct((4, 128), F32),
            jax.ShapeDtypeStruct((8, 128), F32),
            jax.ShapeDtypeStruct((512, 256), BF16),
        ),
        in_specs=[any_space, any_space, smem, smem],
        out_specs=(vmem, vmem, vmem),
        scratch_shapes=[
            *[pltpu.VMEM((8, 64, 256), BF16)] * 8,
            pltpu.VMEM((4, 1024, 256), BF16),
            pltpu.VMEM((8, 8, 128), jnp.int32),
            pltpu.VMEM((8, 128), jnp.int32),
            pltpu.SMEM((4, 128), jnp.int32),
            pltpu.VMEM((1024, 256), BF16),
            pltpu.VMEM((4, 1024, 1024), F32),
            pltpu.VMEM((4, 1024, 1024), BF16),
            pltpu.VMEM((4, 256, 1024), BF16),
            pltpu.VMEM((4, 1024, 128), F32),
            pltpu.VMEM((1024, 128), F32),
            pltpu.VMEM((1024, 128), F32),
            pltpu.VMEM((4, 8, 1024), F32),
            pltpu.VMEM((4, 8, 1024), F32),
            pltpu.VMEM((ITERS, 8, 4, 8, 128), F32),
            pltpu.VMEM((128, 8, 128), F32),
            pltpu.VMEM((128, 8, 128), F32),
            pltpu.VMEM((4, 8, 1024), F32),
            pltpu.VMEM((ITERS, 4, 4, 8, 128), F32),
            pltpu.VMEM((ITERS, 4, 4, 8, 128), F32),
            pltpu.VMEM((4, 8, 128), F32),
            pltpu.VMEM((4, 256, 1024), BF16),
            pltpu.VMEM((8, 2, 256, 256), BF16),
            pltpu.VMEM((4, 2, 256, 256), BF16),
            pltpu.VMEM((4, 2, 256, 256), BF16),
            pltpu.VMEM((2, 2, 256, 256), BF16),
            pltpu.VMEM((2, 256, 256), BF16),
            pltpu.VMEM((8, 2, 8, 256), F32),
            pltpu.VMEM((4, 2, 8, 256), F32),
            pltpu.VMEM((4, 2, 8, 256), F32),
            pltpu.VMEM((2, 2, 8, 256), F32),
            pltpu.VMEM((2, 8, 256), F32),
            pltpu.SemaphoreType.DMA((COPIES,)),
            pltpu.SemaphoreType.DMA((COPIES,)),
            pltpu.SemaphoreType.DMA((3,)),
        ],
        compiler_params=pltpu.CompilerParams(
            collective_id=0, has_side_effects=True, vmem_limit_bytes=60 * 1024 * 1024
        ),
        name="sinkhorn",
    )(source.reshape(8, 64, 256), target, pairs.T, owner_map)
    f, g, mapped = pl.pallas_call(
        hand_over,
        out_shape=(
            jax.ShapeDtypeStruct((4, 128), F32),
            jax.ShapeDtypeStruct((8, 128), F32),
            jax.ShapeDtypeStruct((512, 256), BF16),
        ),
        in_specs=[any_space] * 3,
        out_specs=(any_space,) * 3,
        scratch_shapes=[
            pltpu.VMEM((4, 128), F32),
            pltpu.VMEM((8, 128), F32),
            pltpu.VMEM((512, 256), BF16),
            pltpu.SemaphoreType.DMA((8,)),
            pltpu.SemaphoreType.DMA((8,)),
        ],
        name="hand_over",
    )(f, g, mapped)
    return f.reshape(512), g.reshape(1024), mapped


def solution(mesh):
    return jax.shard_map(
        shards,
        mesh=mesh,
        in_specs=(P(("side", "blk"), None), P("blk", None), P(("side", "blk"), None), P()),
        out_specs=(P(("side", "blk")), P("blk"), P(("side", "blk"), None)),
        check_vma=False,
    )
```

```python
import functools
import math

import jax
import jax.numpy as jnp
from jax import lax
from jax.experimental import pallas as pl
from jax.experimental.pallas import tpu as pltpu
from jax.sharding import PartitionSpec as P

MESH = pl.DeviceIdType.MESH
NEG = -1e30
LOG2E = 1.4426950408889634
LN2 = 0.6931471805599453
REG = 0.3
ITERS = 2
NT = (((1,), (1,)), ((), ()))
F32 = jnp.float32
BF16 = jnp.bfloat16


def lse(parts):
    top = functools.reduce(jnp.maximum, parts)
    total = functools.reduce(jnp.add, [jnp.exp2(p - top) for p in parts])
    return top + jnp.log2(total)


def kernel(
    source, target, pairs, owner_map, f_out, g_out, mapped,
    src0, src1, src2, src3, src4, src5, src6, src7, tgt, tab, tabp, stab, sq, logits, weights, tgt_t, gcol, cmax, csum,
    rmax, rsum, rowbuf, ftab, ltab, frow, colbuf, ztot, gpack, numer, part, comb, pin, rin, hin,
    stat, cstat, pstat, rstat, hstat, picks, early, estat, send_sem, recv_sem, local_sem,
):
    src = (src0, src1, src2, src3, src4, src5, src6, src7)
    side = lax.axis_index("side")
    blk = lax.axis_index("blk")
    x = blk // 8
    y = (blk // 2) % 4
    c = blk % 2

    def at(kx=0, kc=0, ky=0, kz=0):
        xx = (x + kx) % 4
        yy = (y + ky) % 4
        cc = (c + kc) % 2
        zz = (side + kz) % 4
        return (zz, (xx * 4 + yy) * 2 + cc)

    def yi(k):
        return (y + k) % 4

    count = [0]

    def transfer(source_ref, dest_ref, device):
        n = count[0]
        count[0] += 1
        return pltpu.make_async_remote_copy(
            src_ref=source_ref, dst_ref=dest_ref,
            send_sem=send_sem.at[n], recv_sem=recv_sem.at[n],
            device_id=device, device_id_type=MESH,
        )

    sent = []

    def go(copy):
        copy.start()
        sent.append(copy)
        return copy

    row_peers = [(kx, kc) for kx in range(4) for kc in range(2)][1:]
    peers = [at(kx=kx, kc=kc) for kx, kc in row_peers]
    peers += [at(ky=k) for k in (1, 2, 3)] + [at(kz=k) for k in (1, 2, 3)]
    barrier = pltpu.get_barrier_semaphore()
    for peer in peers:
        pl.semaphore_signal(barrier, inc=1, device_id=peer, device_id_type=MESH)

    own_src = pltpu.make_async_copy(source, src[0], local_sem.at[0])
    own_src.start()
    own_tgt = pltpu.make_async_copy(target, tgt.at[y], local_sem.at[1])
    own_tgt.start()

    lane = lax.broadcasted_iota(jnp.int32, (8, 128), 1)
    sub = lax.broadcasted_iota(jnp.int32, (8, 128), 0)
    low = lane < 64
    low1 = low[0:1]

    target_lane = lane % 32
    turn_lane = lane // 32
    seen = jnp.zeros((8, 128), jnp.int32)
    table = jnp.full((8, 128), 8, jnp.int32)
    for s in range(8):
        hit = target_lane == owner_map[pairs[0, s]]
        for k in range(1, 4):
            hit = jnp.logical_or(hit, target_lane == owner_map[pairs[k, s]])
        table = jnp.where(jnp.logical_and(hit, seen == turn_lane), s, table)
        seen = seen + jnp.where(hit, 1, 0)
    tab[0] = table

    pl.semaphore_wait(barrier, len(peers))

    A, B = pl.ds(0, 256), pl.ds(256, 256)
    tabs = []
    for kx, kc in row_peers:
        slot = ((-kx) % 4) * 2 + kc
        tabs.append(go(transfer(tab.at[0], tab.at[slot], at(kx=kx, kc=kc))))

    D1, D2 = pl.ds(0, 224), pl.ds(224, 224)

    def part_of(kz, half=None):
        start = 448 + 144 * ((side + kz) % 4)
        if half is None:
            return pl.ds(pl.multiple_of(start, 16), 144)
        return pl.ds(pl.multiple_of(start + 80 * half, 16), (80, 64)[half])

    own = part_of(0)
    up, down = at(ky=1), at(ky=3)
    FA, FB = pl.ds(0, 4), pl.ds(4, 4)
    s_pa = go(transfer(source.at[FA], src[6].at[FA], at(kx=1)))
    s_mb = go(transfer(source.at[FB], src[2].at[FB], at(kx=3)))
    s_pb = go(transfer(source.at[FB], src[6].at[FB], at(kx=1)))
    s_ma = go(transfer(source.at[FA], src[2].at[FA], at(kx=3)))
    ys_p = go(transfer(target.at[own], tgt.at[y, own], up))
    ys_m = go(transfer(target.at[own], tgt.at[y, own], down))
    y1_p = go(transfer(target.at[D1], tgt.at[y, D1], up))
    y2_m = go(transfer(target.at[D2], tgt.at[y, D2], down))
    s_c = go(transfer(source, src[1], at(kc=1)))

    def z_both(k, rows):
        return (go(transfer(tgt.at[yi(k), rows], tgt.at[yi(k), rows], at(kz=1))),
                go(transfer(tgt.at[yi(k), rows], tgt.at[yi(k), rows], at(kz=3))))

    def z_on(k, z_p, z_m):
        out = []
        if z_p is not None:
            z_p.wait_recv()
            rows = part_of(3, 0)
            out.append(go(transfer(tgt.at[yi(k), rows], tgt.at[yi(k), rows], at(kz=1))))
        if z_m is not None:
            z_m.wait_recv()
            rows = part_of(1, 1)
            out.append(go(transfer(tgt.at[yi(k), rows], tgt.at[yi(k), rows], at(kz=3))))
        return out

    for t in tabs:
        t.wait_recv()
    listing = jnp.full((8, 128), 8, jnp.int32)
    for i in range(4):
        line = jnp.where(low, tab[2 * i], pltpu.roll(tab[2 * i + 1], 64, 1))
        listing = jnp.where(sub == i, line, listing)
    tabp[...] = listing
    copy_tab = pltpu.make_async_copy(tabp.at[pl.ds(0, 4)], stab, local_sem.at[2])
    copy_tab.start()

    ys_p.wait_recv()
    ya = part_of(0, 0)
    yb = part_of(0, 1)
    y2a = go(transfer(tgt.at[yi(3), ya], tgt.at[yi(3), ya], up))
    z3 = z_both(3, own)
    ys_m.wait_recv()
    y2b = go(transfer(tgt.at[yi(1), yb], tgt.at[yi(1), yb], down))
    z1 = z_both(1, own)
    y2_p = go(transfer(target.at[D2], tgt.at[y, D2], up))
    y1_m = go(transfer(target.at[D1], tgt.at[y, D1], down))

    def block(d, q, r):
        return stab[d // 2, (d % 2) * 64 + r * 32 + (x * 4 + q) * 2 + c]

    ones = jnp.full((8, 128), NEG, F32)
    for d in range(8):
        ftab[d * 16 + 8] = ones
        ltab[d * 16 + 8] = -ones

    scale = LOG2E / (REG * 16.0)
    eye = jnp.where(
        lax.broadcasted_iota(jnp.int32, (256, 256), 0)
        == lax.broadcasted_iota(jnp.int32, (256, 256), 1), 1.0, 0.0).astype(BF16)

    def unit(ky, kx):
        q = yi(ky)
        for d in (2 * kx, 2 * kx + 1):
            for r in range(2):
                b = jnp.minimum(block(d, q, r), 7)
                sq[pl.ds(d * 128 + r * 64, 64), :] = src[d][b]
        wide = pl.ds(kx * 256, 256)
        out = lax.dot_general(tgt[q], sq[wide, :], NT, preferred_element_type=F32) * scale
        logits[q, :, wide] = out
        top = jnp.max(jnp.max(out.reshape(128, 8, 256), axis=0), axis=0, keepdims=True)

        sums = jnp.zeros((8, 256), F32)
        for j in range(8):
            p = jnp.exp2(logits[q, pl.ds(j * 128, 128), wide] - top)
            sums = sums + jnp.sum(p.reshape(16, 8, 256), axis=0)
        rmax[q, 0:1, wide] = top
        rsum[q, 0:1, wide] = jnp.sum(sums, axis=0, keepdims=True)

    def turn(q):
        def body(j, _):
            rows = pl.ds(pl.multiple_of(j * 512, 512), 512)
            out = lax.dot_general(eye, tgt[q, rows, :], NT, preferred_element_type=F32)
            tgt_t[q, :, rows] = out.astype(BF16)
            return 0

        lax.fori_loop(0, 2, body, 0)

    R = 128

    def fold(value, op):
        return op(value.reshape(R // 8, 8, 128), axis=0)

    def lanes(d):
        return pl.ds(d * 128, 128)

    def row_single(q):
        def body(i, carry):
            for j in range(2):
                rows = pl.ds(pl.multiple_of(i * R + j * 64, 64), 64)
                g = gcol[q, rows, :]
                new = []
                for d in range(8):
                    m, total = carry[d]
                    t = (logits[q, rows, lanes(d)] + g).reshape(8, 8, 128)
                    top = jnp.maximum(m, jnp.max(t, axis=0))
                    p = jnp.exp2(t - top)
                    new.append((top, total * jnp.exp2(m - top) + jnp.sum(p, axis=0)))
                carry = tuple(new)
            return carry

        def twice(i, carry):
            return body(2 * i + 1, body(2 * i, carry))

        start = (jnp.full((8, 128), NEG, F32), jnp.zeros((8, 128), F32))
        done = lax.fori_loop(0, 512 // R, twice, (start,) * 8)
        for d, (m, total) in enumerate(done):
            top = jnp.max(m, axis=0, keepdims=True)
            rmax[q, 0:1, lanes(d)] = top
            rsum[q, 0:1, lanes(d)] = jnp.sum(total * jnp.exp2(m - top), axis=0, keepdims=True)

    def row_keep(q, ds):
        height = 64 if len(ds) > 2 else 256

        def group(value, op):
            return op(value.reshape(height // 8, 8, 128), axis=0)

        def first(i, tops):
            rows = pl.ds(pl.multiple_of(i * height, height), height)
            g = gcol[q, rows, :]
            return tuple(jnp.maximum(t, group(logits[q, rows, lanes(d)] + g, jnp.max)) for d, t in zip(ds, tops))

        def second(i, sums):
            rows = pl.ds(pl.multiple_of(i * height, height), height)
            g = gcol[q, rows, :]
            new = []
            for d, top, total in zip(ds, tops, sums):
                p = jnp.exp2(logits[q, rows, lanes(d)] + g - top)
                weights[q, rows, lanes(d)] = p.astype(BF16)
                new.append(total + group(p, jnp.sum))
            return tuple(new)

        def sweep(step, start):
            count = 1024 // height
            pair = lambda i, carry: step(2 * i + 1, step(2 * i, carry))
            return lax.fori_loop(0, count // 2, pair, start)

        tops = sweep(first, (jnp.full((8, 128), NEG, F32),) * len(ds))
        tops = [jnp.max(t, axis=0, keepdims=True) for t in tops]
        sums = sweep(second, (jnp.zeros((8, 128), F32),) * len(ds))
        for d, top, total in zip(ds, tops, sums):
            rmax[q, 0:1, lanes(d)] = top
            rsum[q, 0:1, lanes(d)] = jnp.sum(total, axis=0, keepdims=True)

    def row_sum(d):
        terms = []
        for q in range(4):
            v = rmax[q, 0:1, lanes(d)] + jnp.log2(rsum[q, 0:1, lanes(d)])
            w = pltpu.roll(v, 64, 1)
            terms.append(jnp.where(sub == block(d, q, 0), jnp.where(low1, v, w), NEG))
            terms.append(jnp.where(sub == block(d, q, 1), jnp.where(low1, w, v), NEG))
        return lse(terms)

    def row_local(phase):
        for i in range(4):
            rowbuf[phase, 0, i] = jnp.where(low, row_sum(2 * i), row_sum(2 * i + 1))

    def row_start(phase):
        copies = []
        for kx, kc in row_peers:
            slot = ((-kx) % 4) * 2 + kc
            copies.append(go(transfer(rowbuf.at[phase, 0], rowbuf.at[phase, slot], at(kx=kx, kc=kc))))
        return copies

    def row_finish(phase, copies):
        for t in copies:
            t.wait_recv()
        for i in range(4):
            terms = [rowbuf[phase, 0, i]]
            for kx, kc in row_peers:
                v = rowbuf[phase, kx * 2 + kc, (i - kx) % 4]
                terms.append(pltpu.roll(v, 64, 1) if kc else v)
            total = -lse(terms)
            other = pltpu.roll(total, 64, 1)
            even = jnp.where(low, total, other)
            odd = jnp.where(low, other, total)
            for b in range(8):
                ftab[32 * i + b] = jnp.broadcast_to(even[b:b + 1], (8, 128))
                ftab[32 * i + 16 + b] = jnp.broadcast_to(odd[b:b + 1], (8, 128))

    def row_spread():
        for q in range(4):
            for d in range(8):
                f0 = ftab[d * 16 + block(d, q, 0)]
                f1 = ftab[d * 16 + block(d, q, 1)]
                frow[q, :, lanes(d)] = jnp.where(low, f0, f1)

    diag = (lax.broadcasted_iota(jnp.int32, (128, 128), 0)
            == lax.broadcasted_iota(jnp.int32, (128, 128), 1))
    C = 8

    def column(q, phase):
        fs = [frow[q, 0:1, lanes(d)] for d in range(8)]

        def chunk(i):
            for j in range(128 // C):
                rows = pl.ds(pl.multiple_of(i * 128 + j * C, C), C)
                ts = [logits[q, rows, lanes(d)] + fs[d] for d in range(8)]
                m = functools.reduce(jnp.maximum, ts)
                cmax[rows, :] = m
                csum[rows, :] = functools.reduce(jnp.add, [jnp.exp2(t - m) for t in ts])

        def merge(i):
            rows = pl.ds(pl.multiple_of(i * 128, 128), 128)
            m = cmax[rows, :]
            top = jnp.max(m, axis=1, keepdims=True)
            total = jnp.sum(csum[rows, :] * jnp.exp2(m - top), axis=1, keepdims=True)
            spread = jnp.broadcast_to(top + jnp.log2(total), (128, 128))
            line = jnp.sum(jnp.where(diag, spread, 0.0), axis=0, keepdims=True)
            colbuf[phase, 0, q, pl.ds(i, 1), :] = line

        def body(i, _):
            merge(2 * i - 2)
            merge(2 * i - 1)
            chunk(2 * i)
            chunk(2 * i + 1)
            return 0

        chunk(0)
        chunk(1)
        lax.fori_loop(1, 4, body, 0)
        merge(6)
        merge(7)

    def over_y(phase, q):
        return [go(transfer(colbuf.at[phase, 0, q], colbuf.at[phase, (-k) % 4, q], at(ky=k))) for k in (1, 2, 3)]

    def over_z(phase, q, copies):
        for t in copies:
            t.wait_recv()
        ztot[phase, 0, q] = lse([colbuf[phase, k, q] for k in range(4)])
        return [go(transfer(ztot.at[phase, 0, q], ztot.at[phase, (-k) % 4, q], at(kz=k))) for k in (1, 2, 3)]

    def column_done(phase, q, copies):
        for t in copies:
            t.wait_recv()
        total = -lse([ztot[phase, (z - side + 4) % 4, q] for z in range(4)])
        gpack[q] = total
        for h in range(2):
            cols = []
            for i in range(4):
                line = jnp.broadcast_to(total[h * 4 + i:h * 4 + i + 1], (128, 128))
                cols.append(jnp.sum(jnp.where(diag, line, 0.0), axis=1, keepdims=True))
            for i in range(4):
                gcol[q, pl.ds((h * 4 + i) * 128, 128), :] = jnp.broadcast_to(cols[i], (128, 128))

    def pick(d):
        same = (lax.broadcasted_iota(jnp.int32, (64, 256), 0)
                == lax.broadcasted_iota(jnp.int32, (64, 256), 1) % 64)
        col_block = lax.broadcasted_iota(jnp.int32, (64, 256), 1) // 64
        for h in range(2):
            for q in range(4):
                for r in range(2):
                    hit = jnp.logical_and(same, col_block == block(d, q, r) - 4 * h)
                    picks[d, h, pl.ds(q * 128 + r * 64, 64), :] = jnp.where(hit, 1.0, 0.0).astype(BF16)

    def columns_then_rows(phase):
        ys, zs = {}, {}
        for q in range(4):
            column(q, phase)
            ys[q] = over_y(phase, q)
            if q >= 2:
                zs[q - 2] = over_z(phase, q - 2, ys[q - 2])
        zs[2] = over_z(phase, 2, ys[2])
        for q in range(4):
            column_done(phase, q, zs[q])
            if phase < ITERS - 1:
                row_single(q)
            elif q < 3:
                row_keep(q, range(2, 8))
            if q == 0:
                zs[3] = over_z(phase, 3, ys[3])

    own_src.wait()
    own_tgt.wait()
    s_c.wait_recv()
    copy_tab.wait()
    unit(0, 0)
    s_pa.wait_recv()
    s_fp = go(transfer(src[6].at[FA], src[4].at[FA], at(kx=1)))
    s_mb.wait_recv()
    s_fm = go(transfer(src[2].at[FB], src[4].at[FB], at(kx=3)))
    y1_p.wait_recv()
    y21 = go(transfer(tgt.at[yi(3), D1], tgt.at[yi(3), D1], up))
    y2_m.wait_recv()
    y22 = go(transfer(tgt.at[yi(1), D2], tgt.at[yi(1), D2], down))
    y2a.wait_recv()
    z2a = z_both(2, ya)
    y2b.wait_recv()
    z2b = z_both(2, yb)
    z3f = z_on(3, *z3)
    s_pb.wait_recv()
    s_cp = go(transfer(src[6], src[7], at(kc=1)))
    s_ma.wait_recv()
    s_cm = go(transfer(src[2], src[3], at(kc=1)))
    z1f = z_on(1, *z1)
    s_cp.wait_recv()
    unit(0, 3)
    s_cm.wait_recv()
    unit(0, 1)
    s_fp.wait_recv()
    s_c2a = go(transfer(src[4].at[FA], src[5].at[FA], at(kc=1)))
    s_fm.wait_recv()
    s_c2b = go(transfer(src[4].at[FB], src[5].at[FB], at(kc=1)))
    z2f = z_on(2, z2a[0], z2b[1])
    for t in (y2_p, *z3f):
        t.wait_recv()
    for kx in (0, 1, 3):
        unit(3, kx)
    s_c2a.wait_recv()
    s_c2b.wait_recv()
    unit(0, 2)
    unit(3, 2)
    for t in (y1_m, *z1f):
        t.wait_recv()
    for kx in range(4):
        unit(1, kx)
    for t in (y21, y22, z2a[1], z2b[0], *z2f):
        t.wait_recv()
    for kx in range(4):
        unit(2, kx)

    for phase in range(ITERS):
        row_local(phase)
        copies = row_start(phase)
        if phase == 0:
            for q in range(4):
                turn(q)
            for d in range(4):
                pick(d)
        else:
            for d in range(4, 8):
                pick(d)
        row_finish(phase, copies)
        row_spread()
        if phase == ITERS - 1:
            even = jnp.concatenate([ftab[2 * i][0:1] for i in range(4)], axis=0)
            odd = jnp.concatenate([ftab[2 * i + 1][0:1] for i in range(4)], axis=0)
            f_out[...] = jnp.where(low[0:4], even, odd) * (REG * LN2)
        columns_then_rows(phase)

    g_out[...] = gpack[y] * (REG * LN2)
    def prepare(kx):
        for d in (2 * kx, 2 * kx + 1):
            out = row_sum(d)
            for b in range(8):
                ltab[d * 16 + b] = jnp.broadcast_to(out[b:b + 1], (8, 128))
            for h in range(2):
                pieces = [jnp.where(low1, out[b:b + 1], out[b + 1:b + 2]) for b in (4 * h, 4 * h + 2)]
                stat[d, h] = jnp.broadcast_to(jnp.concatenate(pieces, axis=1), (8, 256))
        wide = pl.ds(kx * 256, 256)
        for q in range(4):
            out = jnp.dot(tgt_t[q], weights[q, :, wide], preferred_element_type=F32)
            for i in range(2):
                d = 2 * kx + i
                one = jnp.where(low, ltab[d * 16 + block(d, q, 0)], ltab[d * 16 + block(d, q, 1)])
                factor = jnp.exp2(rmax[q, 0:1, lanes(d)] - one[0:1])
                numer[q, :, lanes(d)] = (out[:, i * 128:(i + 1) * 128] * factor).astype(BF16)

    def assemble(d, halves=(0, 1)):
        value = jnp.concatenate([numer[q, :, lanes(d)] for q in range(4)], axis=1)
        for h in halves:
            part[d, h] = jnp.dot(value, picks[d, h], preferred_element_type=F32).astype(BF16)

    def merge(terms):
        stats = [st[...] for _, st in terms]
        joint = lse(stats)
        total = None
        for (value, _), st in zip(terms, stats):
            term = value[...].astype(F32).reshape(32, 8, 256) * jnp.exp2(st - joint)
            total = term if total is None else total + term
        return total.reshape(256, 256), joint

    def own_part(d, h):
        return part.at[d, h], stat.at[d, h]

    def from_core(kx, h):
        return pin.at[kx, h], pstat.at[kx, h]

    to_core = {}

    def give(kx):
        d = kx * 2 + 1
        assemble(d)
        to_core[kx] = [go(transfer(part.at[d], pin.at[kx], at(kc=1))),
                       go(transfer(stat.at[d], pstat.at[kx], at(kc=1)))]

    def give_half(kx, h):
        d = kx * 2 + 1
        assemble(d, (h,))
        to_core[kx, h] = [go(transfer(part.at[d, h], pin.at[kx, h], at(kc=1))),
                          go(transfer(stat.at[d, h], pstat.at[kx, h], at(kc=1)))]

    def take(copies):
        for t in copies:
            t.wait_recv()

    def join(kx, h, extra=()):
        total, cstat[kx, h] = merge([own_part(2 * kx, h), from_core(kx, h), *extra])
        comb[kx, h] = total.astype(BF16)

    def pass_on(kx, h, n, far, device):
        values, stats = (hin, hstat) if far else (rin, rstat)
        index = (n,) if far else (n, h)
        return [go(transfer(comb.at[kx, h], values.at[index], device)),
                go(transfer(cstat.at[kx, h], stats.at[index], device))]

    right, left = at(kx=1), at(kx=3)
    row_keep(3, (4, 5))
    prepare(2)
    give(2)
    assemble(4)
    row_keep(3, (2, 3))
    take(to_core[2])
    join(2, 0)
    h_p = pass_on(2, 0, 0, True, right)
    join(2, 1)
    h_m = pass_on(2, 1, 1, True, left)
    prepare(1)
    give_half(1, 1)
    row_keep(3, (6, 7))
    prepare(3)
    give_half(3, 0)
    assemble(2, (1,))
    take(to_core[1, 1])
    join(1, 1)
    r_p1 = pass_on(1, 1, 0, False, right)
    assemble(6, (0,))
    take(to_core[3, 0])
    join(3, 0)
    r_m0 = pass_on(3, 0, 1, False, left)
    give_half(1, 0)
    give_half(3, 1)
    assemble(2, (0,))
    assemble(6, (1,))
    take(to_core[1, 0])
    take(h_p)
    join(1, 0, [(hin.at[0], hstat.at[0])])
    r_p0 = pass_on(1, 0, 0, False, right)
    take(to_core[3, 1])
    take(h_m)
    join(3, 1, [(hin.at[1], hstat.at[1])])
    r_m1 = pass_on(3, 1, 1, False, left)
    for q in range(4):
        row_keep(q, (0, 1))
    prepare(0)
    give(0)
    assemble(0)
    take(to_core[0])
    for h, copies, n in ((0, r_m0, 1), (1, r_p1, 0)):
        take(copies)
        early[h], estat[h] = merge([own_part(0, h), from_core(0, h), (rin.at[n, h], rstat.at[n, h])])
    for h, copies, n in ((0, r_p0, 0), (1, r_m1, 1)):
        take(copies)
        out, _ = merge([(early.at[h], estat.at[h]), (rin.at[n, h], rstat.at[n, h])])
        turned = lax.dot_general(eye, out.astype(BF16), NT, preferred_element_type=F32)
        mapped[pl.ds(h * 256, 256), :] = turned.astype(BF16)

    for t in sent:
        t.wait_send()


COPIES = 42 + 7 * ITERS + 24 * ITERS + 24


def hand_over(f_in, g_in, m_in, f_out, g_out, m_out, f, g, m, in_sem, out_sem):
    jobs = [(m_in.at[pl.ds(i * 128, 128)], m.at[pl.ds(i * 128, 128)], m_out.at[pl.ds(i * 128, 128)]) for i in range(4)]
    jobs += [(f_in, f, f_out), (g_in, g, g_out)]
    first = [pltpu.make_async_copy(a, b, in_sem.at[n]) for n, (a, b, _) in enumerate(jobs)]
    second = [pltpu.make_async_copy(b, o, out_sem.at[n]) for n, (_, b, o) in enumerate(jobs)]
    for copy in first:
        copy.start()
    for copy, follow in zip(first, second):
        copy.wait()
        follow.start()
    for copy in second:
        copy.wait()


def shards(source, target, pairs, owner_map):
    any_space = pl.BlockSpec(memory_space=pl.ANY)
    smem = pl.BlockSpec(memory_space=pltpu.SMEM)
    vmem = pl.BlockSpec(memory_space=pltpu.VMEM)
    f, g, mapped = pl.pallas_call(
        kernel,
        out_shape=(
            jax.ShapeDtypeStruct((4, 128), F32),
            jax.ShapeDtypeStruct((8, 128), F32),
            jax.ShapeDtypeStruct((512, 256), BF16),
        ),
        in_specs=[any_space, any_space, smem, smem],
        out_specs=(vmem, vmem, vmem),
        scratch_shapes=[
            *[pltpu.VMEM((8, 64, 256), BF16)] * 8,
            pltpu.VMEM((4, 1024, 256), BF16),
            pltpu.VMEM((8, 8, 128), jnp.int32),
            pltpu.VMEM((8, 128), jnp.int32),
            pltpu.SMEM((4, 128), jnp.int32),
            pltpu.VMEM((1024, 256), BF16),
            pltpu.VMEM((4, 1024, 1024), F32),
            pltpu.VMEM((4, 1024, 1024), BF16),
            pltpu.VMEM((4, 256, 1024), BF16),
            pltpu.VMEM((4, 1024, 128), F32),
            pltpu.VMEM((1024, 128), F32),
            pltpu.VMEM((1024, 128), F32),
            pltpu.VMEM((4, 8, 1024), F32),
            pltpu.VMEM((4, 8, 1024), F32),
            pltpu.VMEM((ITERS, 8, 4, 8, 128), F32),
            pltpu.VMEM((128, 8, 128), F32),
            pltpu.VMEM((128, 8, 128), F32),
            pltpu.VMEM((4, 8, 1024), F32),
            pltpu.VMEM((ITERS, 4, 4, 8, 128), F32),
            pltpu.VMEM((ITERS, 4, 4, 8, 128), F32),
            pltpu.VMEM((4, 8, 128), F32),
            pltpu.VMEM((4, 256, 1024), BF16),
            pltpu.VMEM((8, 2, 256, 256), BF16),
            pltpu.VMEM((4, 2, 256, 256), BF16),
            pltpu.VMEM((4, 2, 256, 256), BF16),
            pltpu.VMEM((2, 2, 256, 256), BF16),
            pltpu.VMEM((2, 256, 256), BF16),
            pltpu.VMEM((8, 2, 8, 256), F32),
            pltpu.VMEM((4, 2, 8, 256), F32),
            pltpu.VMEM((4, 2, 8, 256), F32),
            pltpu.VMEM((2, 2, 8, 256), F32),
            pltpu.VMEM((2, 8, 256), F32),
            pltpu.VMEM((8, 2, 512, 256), BF16),
            pltpu.VMEM((2, 256, 256), F32),
            pltpu.VMEM((2, 8, 256), F32),
            pltpu.SemaphoreType.DMA((COPIES,)),
            pltpu.SemaphoreType.DMA((COPIES,)),
            pltpu.SemaphoreType.DMA((3,)),
        ],
        compiler_params=pltpu.CompilerParams(
            collective_id=0, has_side_effects=True, vmem_limit_bytes=60 * 1024 * 1024
        ),
        name="sinkhorn",
    )(source.reshape(8, 64, 256), target, pairs.T, owner_map)
    f, g, mapped = pl.pallas_call(
        hand_over,
        out_shape=(
            jax.ShapeDtypeStruct((4, 128), F32),
            jax.ShapeDtypeStruct((8, 128), F32),
            jax.ShapeDtypeStruct((512, 256), BF16),
        ),
        in_specs=[any_space] * 3,
        out_specs=(any_space,) * 3,
        scratch_shapes=[
            pltpu.VMEM((4, 128), F32),
            pltpu.VMEM((8, 128), F32),
            pltpu.VMEM((512, 256), BF16),
            pltpu.SemaphoreType.DMA((8,)),
            pltpu.SemaphoreType.DMA((8,)),
        ],
        name="hand_over",
    )(f, g, mapped)
    return f.reshape(512), g.reshape(1024), mapped


def solution(mesh):
    return jax.shard_map(
        shards,
        mesh=mesh,
        in_specs=(P(("side", "blk"), None), P("blk", None), P(("side", "blk"), None), P()),
        out_specs=(P(("side", "blk")), P("blk"), P(("side", "blk"), None)),
        check_vma=False,
    )
```

```python
import functools
import math

import jax
import jax.numpy as jnp
from jax import lax
from jax.experimental import pallas as pl
from jax.experimental.pallas import tpu as pltpu
from jax.sharding import PartitionSpec as P

MESH = pl.DeviceIdType.MESH
NEG = -1e30
LOG2E = 1.4426950408889634
LN2 = 0.6931471805599453
REG = 0.3
ITERS = 2
NT = (((1,), (1,)), ((), ()))
F32 = jnp.float32
BF16 = jnp.bfloat16


def lse(parts):
    top = functools.reduce(jnp.maximum, parts)
    total = functools.reduce(jnp.add, [jnp.exp2(p - top) for p in parts])
    return top + jnp.log2(total)


def kernel(
    source, target, pairs, owner_map, f_out, g_out, mapped,
    src0, src1, src2, src3, src4, src5, src6, src7, tgt, tab, tabp, stab, sq, logits, weights, tgt_t, gcol, cmax, csum,
    rmax, rsum, rowbuf, ftab, ltab, frow, colbuf, ztot, gpack, numer, part, comb, pin, rin, hin,
    stat, cstat, pstat, rstat, hstat, picks, early, estat, send_sem, recv_sem, local_sem,
):
    src = (src0, src1, src2, src3, src4, src5, src6, src7)
    side = lax.axis_index("side")
    blk = lax.axis_index("blk")
    x = blk // 8
    y = (blk // 2) % 4
    c = blk % 2

    def at(kx=0, kc=0, ky=0, kz=0):
        xx = (x + kx) % 4
        yy = (y + ky) % 4
        cc = (c + kc) % 2
        zz = (side + kz) % 4
        return (zz, (xx * 4 + yy) * 2 + cc)

    def yi(k):
        return (y + k) % 4

    count = [0]

    def transfer(source_ref, dest_ref, device):
        n = count[0]
        count[0] += 1
        return pltpu.make_async_remote_copy(
            src_ref=source_ref, dst_ref=dest_ref,
            send_sem=send_sem.at[n], recv_sem=recv_sem.at[n],
            device_id=device, device_id_type=MESH,
        )

    sent = []

    def go(copy):
        copy.start()
        sent.append(copy)
        return copy

    row_peers = [(kx, kc) for kx in range(4) for kc in range(2)][1:]
    peers = [at(kx=kx, kc=kc) for kx, kc in row_peers]
    peers += [at(ky=k) for k in (1, 2, 3)] + [at(kz=k) for k in (1, 2, 3)]
    barrier = pltpu.get_barrier_semaphore()
    for peer in peers:
        pl.semaphore_signal(barrier, inc=1, device_id=peer, device_id_type=MESH)

    own_src = pltpu.make_async_copy(source, src[0], local_sem.at[0])
    own_src.start()
    own_tgt = pltpu.make_async_copy(target, tgt.at[y], local_sem.at[1])
    own_tgt.start()

    lane = lax.broadcasted_iota(jnp.int32, (8, 128), 1)
    sub = lax.broadcasted_iota(jnp.int32, (8, 128), 0)
    low = lane < 64
    low1 = low[0:1]

    target_lane = lane % 32
    turn_lane = lane // 32
    seen = jnp.zeros((8, 128), jnp.int32)
    table = jnp.full((8, 128), 8, jnp.int32)
    for s in range(8):
        hit = target_lane == owner_map[pairs[0, s]]
        for k in range(1, 4):
            hit = jnp.logical_or(hit, target_lane == owner_map[pairs[k, s]])
        table = jnp.where(jnp.logical_and(hit, seen == turn_lane), s, table)
        seen = seen + jnp.where(hit, 1, 0)
    tab[0] = table

    pl.semaphore_wait(barrier, len(peers))

    A, B = pl.ds(0, 256), pl.ds(256, 256)
    tabs = []
    for kx, kc in row_peers:
        slot = ((-kx) % 4) * 2 + kc
        tabs.append(go(transfer(tab.at[0], tab.at[slot], at(kx=kx, kc=kc))))

    D1, D2 = pl.ds(0, 224), pl.ds(224, 224)

    def part_of(kz, half=None):
        start = 448 + 144 * ((side + kz) % 4)
        if half is None:
            return pl.ds(pl.multiple_of(start, 16), 144)
        return pl.ds(pl.multiple_of(start + 80 * half, 16), (80, 64)[half])

    own = part_of(0)
    up, down = at(ky=1), at(ky=3)
    FA, FB = pl.ds(0, 4), pl.ds(4, 4)
    s_pa = go(transfer(source.at[FA], src[6].at[FA], at(kx=1)))
    s_mb = go(transfer(source.at[FB], src[2].at[FB], at(kx=3)))
    s_pb = go(transfer(source.at[FB], src[6].at[FB], at(kx=1)))
    s_ma = go(transfer(source.at[FA], src[2].at[FA], at(kx=3)))
    ys_p = go(transfer(target.at[own], tgt.at[y, own], up))
    ys_m = go(transfer(target.at[own], tgt.at[y, own], down))
    y1_p = go(transfer(target.at[D1], tgt.at[y, D1], up))
    y2_m = go(transfer(target.at[D2], tgt.at[y, D2], down))
    s_c = go(transfer(source, src[1], at(kc=1)))

    def z_both(k, rows):
        return (go(transfer(tgt.at[yi(k), rows], tgt.at[yi(k), rows], at(kz=1))),
                go(transfer(tgt.at[yi(k), rows], tgt.at[yi(k), rows], at(kz=3))))

    def z_on(k, z_p, z_m):
        out = []
        if z_p is not None:
            z_p.wait_recv()
            rows = part_of(3, 0)
            out.append(go(transfer(tgt.at[yi(k), rows], tgt.at[yi(k), rows], at(kz=1))))
        if z_m is not None:
            z_m.wait_recv()
            rows = part_of(1, 1)
            out.append(go(transfer(tgt.at[yi(k), rows], tgt.at[yi(k), rows], at(kz=3))))
        return out

    for t in tabs:
        t.wait_recv()
    listing = jnp.full((8, 128), 8, jnp.int32)
    for i in range(4):
        line = jnp.where(low, tab[2 * i], pltpu.roll(tab[2 * i + 1], 64, 1))
        listing = jnp.where(sub == i, line, listing)
    tabp[...] = listing
    copy_tab = pltpu.make_async_copy(tabp.at[pl.ds(0, 4)], stab, local_sem.at[2])
    copy_tab.start()

    ys_p.wait_recv()
    ya = part_of(0, 0)
    yb = part_of(0, 1)
    y2a = go(transfer(tgt.at[yi(3), ya], tgt.at[yi(3), ya], up))
    z3 = z_both(3, own)
    ys_m.wait_recv()
    y2b = go(transfer(tgt.at[yi(1), yb], tgt.at[yi(1), yb], down))
    z1 = z_both(1, own)
    y2_p = go(transfer(target.at[D2], tgt.at[y, D2], up))
    y1_m = go(transfer(target.at[D1], tgt.at[y, D1], down))

    def block(d, q, r):
        return stab[d // 2, (d % 2) * 64 + r * 32 + (x * 4 + q) * 2 + c]

    ones = jnp.full((8, 128), NEG, F32)
    for d in range(8):
        ftab[d * 16 + 8] = ones
        ltab[d * 16 + 8] = -ones

    scale = LOG2E / (REG * 16.0)
    eye = jnp.where(
        lax.broadcasted_iota(jnp.int32, (256, 256), 0)
        == lax.broadcasted_iota(jnp.int32, (256, 256), 1), 1.0, 0.0).astype(BF16)

    def unit(ky, kx):
        q = yi(ky)
        for d in (2 * kx, 2 * kx + 1):
            for r in range(2):
                b = jnp.minimum(block(d, q, r), 7)
                sq[pl.ds(d * 128 + r * 64, 64), :] = src[d][b]
        wide = pl.ds(kx * 256, 256)
        out = lax.dot_general(tgt[q], sq[wide, :], NT, preferred_element_type=F32) * scale
        logits[q, :, wide] = out
        top = jnp.max(jnp.max(out.reshape(128, 8, 256), axis=0), axis=0, keepdims=True)

        sums = jnp.zeros((8, 256), F32)
        for j in range(8):
            p = jnp.exp2(logits[q, pl.ds(j * 128, 128), wide] - top)
            sums = sums + jnp.sum(p.reshape(16, 8, 256), axis=0)
        rmax[q, 0:1, wide] = top
        rsum[q, 0:1, wide] = jnp.sum(sums, axis=0, keepdims=True)

    def turn(q):
        def body(j, _):
            rows = pl.ds(pl.multiple_of(j * 512, 512), 512)
            out = lax.dot_general(eye, tgt[q, rows, :], NT, preferred_element_type=F32)
            tgt_t[q, :, rows] = out.astype(BF16)
            return 0

        lax.fori_loop(0, 2, body, 0)

    R = 128

    def fold(value, op):
        return op(value.reshape(R // 8, 8, 128), axis=0)

    def lanes(d):
        return pl.ds(d * 128, 128)

    def row_single(q):
        def body(i, carry):
            for j in range(2):
                rows = pl.ds(pl.multiple_of(i * R + j * 64, 64), 64)
                g = gcol[q, rows, :]
                new = []
                for d in range(8):
                    m, total = carry[d]
                    t = (logits[q, rows, lanes(d)] + g).reshape(8, 8, 128)
                    top = jnp.maximum(m, jnp.max(t, axis=0))
                    p = jnp.exp2(t - top)
                    new.append((top, total * jnp.exp2(m - top) + jnp.sum(p, axis=0)))
                carry = tuple(new)
            return carry

        def twice(i, carry):
            return body(2 * i + 1, body(2 * i, carry))

        start = (jnp.full((8, 128), NEG, F32), jnp.zeros((8, 128), F32))
        done = lax.fori_loop(0, 512 // R, twice, (start,) * 8)
        for d, (m, total) in enumerate(done):
            top = jnp.max(m, axis=0, keepdims=True)
            rmax[q, 0:1, lanes(d)] = top
            rsum[q, 0:1, lanes(d)] = jnp.sum(total * jnp.exp2(m - top), axis=0, keepdims=True)

    def row_keep(q, ds):
        height = 64 if len(ds) > 2 else 256

        def group(value, op):
            return op(value.reshape(height // 8, 8, 128), axis=0)

        def first(i, tops):
            rows = pl.ds(pl.multiple_of(i * height, height), height)
            g = gcol[q, rows, :]
            return tuple(jnp.maximum(t, group(logits[q, rows, lanes(d)] + g, jnp.max)) for d, t in zip(ds, tops))

        def second(i, sums):
            rows = pl.ds(pl.multiple_of(i * height, height), height)
            g = gcol[q, rows, :]
            new = []
            for d, top, total in zip(ds, tops, sums):
                p = jnp.exp2(logits[q, rows, lanes(d)] + g - top)
                weights[q, rows, lanes(d)] = p.astype(BF16)
                new.append(total + group(p, jnp.sum))
            return tuple(new)

        def sweep(step, start):
            count = 1024 // height
            pair = lambda i, carry: step(2 * i + 1, step(2 * i, carry))
            return lax.fori_loop(0, count // 2, pair, start)

        tops = sweep(first, (jnp.full((8, 128), NEG, F32),) * len(ds))
        tops = [jnp.max(t, axis=0, keepdims=True) for t in tops]
        sums = sweep(second, (jnp.zeros((8, 128), F32),) * len(ds))
        for d, top, total in zip(ds, tops, sums):
            rmax[q, 0:1, lanes(d)] = top
            rsum[q, 0:1, lanes(d)] = jnp.sum(total, axis=0, keepdims=True)

    def row_sum(d):
        terms = []
        for q in range(4):
            v = rmax[q, 0:1, lanes(d)] + jnp.log2(rsum[q, 0:1, lanes(d)])
            w = pltpu.roll(v, 64, 1)
            terms.append(jnp.where(sub == block(d, q, 0), jnp.where(low1, v, w), NEG))
            terms.append(jnp.where(sub == block(d, q, 1), jnp.where(low1, w, v), NEG))
        return lse(terms)

    def row_local(phase):
        for i in range(4):
            rowbuf[phase, 0, i] = jnp.where(low, row_sum(2 * i), row_sum(2 * i + 1))

    def row_start(phase):
        copies = []
        for kx, kc in row_peers:
            slot = ((-kx) % 4) * 2 + kc
            copies.append(go(transfer(rowbuf.at[phase, 0], rowbuf.at[phase, slot], at(kx=kx, kc=kc))))
        return copies

    def row_finish(phase, copies):
        for t in copies:
            t.wait_recv()
        for i in range(4):
            terms = [rowbuf[phase, 0, i]]
            for kx, kc in row_peers:
                v = rowbuf[phase, kx * 2 + kc, (i - kx) % 4]
                terms.append(pltpu.roll(v, 64, 1) if kc else v)
            total = -lse(terms)
            other = pltpu.roll(total, 64, 1)
            even = jnp.where(low, total, other)
            odd = jnp.where(low, other, total)
            for b in range(8):
                ftab[32 * i + b] = jnp.broadcast_to(even[b:b + 1], (8, 128))
                ftab[32 * i + 16 + b] = jnp.broadcast_to(odd[b:b + 1], (8, 128))

    def row_spread():
        for q in range(4):
            for d in range(8):
                f0 = ftab[d * 16 + block(d, q, 0)]
                f1 = ftab[d * 16 + block(d, q, 1)]
                frow[q, :, lanes(d)] = jnp.where(low, f0, f1)

    diag = (lax.broadcasted_iota(jnp.int32, (128, 128), 0)
            == lax.broadcasted_iota(jnp.int32, (128, 128), 1))
    C = 8

    def column(q, phase):
        fs = [frow[q, 0:1, lanes(d)] for d in range(8)]

        def chunk(i):
            for j in range(128 // C):
                rows = pl.ds(pl.multiple_of(i * 128 + j * C, C), C)
                ts = [logits[q, rows, lanes(d)] + fs[d] for d in range(8)]
                m = functools.reduce(jnp.maximum, ts)
                cmax[rows, :] = m
                csum[rows, :] = functools.reduce(jnp.add, [jnp.exp2(t - m) for t in ts])

        def merge(i):
            rows = pl.ds(pl.multiple_of(i * 128, 128), 128)
            m = cmax[rows, :]
            top = jnp.max(m, axis=1, keepdims=True)
            total = jnp.sum(csum[rows, :] * jnp.exp2(m - top), axis=1, keepdims=True)
            spread = jnp.broadcast_to(top + jnp.log2(total), (128, 128))
            line = jnp.sum(jnp.where(diag, spread, 0.0), axis=0, keepdims=True)
            colbuf[phase, 0, q, pl.ds(i, 1), :] = line

        def body(i, _):
            merge(2 * i - 2)
            merge(2 * i - 1)
            chunk(2 * i)
            chunk(2 * i + 1)
            return 0

        chunk(0)
        chunk(1)
        lax.fori_loop(1, 4, body, 0)
        merge(6)
        merge(7)

    def over_y(phase, q):
        return [go(transfer(colbuf.at[phase, 0, q], colbuf.at[phase, (-k) % 4, q], at(ky=k))) for k in (1, 2, 3)]

    def over_z(phase, q, copies):
        for t in copies:
            t.wait_recv()
        ztot[phase, 0, q] = lse([colbuf[phase, k, q] for k in range(4)])
        return [go(transfer(ztot.at[phase, 0, q], ztot.at[phase, (-k) % 4, q], at(kz=k))) for k in (1, 2, 3)]

    def column_done(phase, q, copies):
        for t in copies:
            t.wait_recv()
        total = -lse([ztot[phase, (z - side + 4) % 4, q] for z in range(4)])
        gpack[q] = total
        for h in range(2):
            cols = []
            for i in range(4):
                line = jnp.broadcast_to(total[h * 4 + i:h * 4 + i + 1], (128, 128))
                cols.append(jnp.sum(jnp.where(diag, line, 0.0), axis=1, keepdims=True))
            for i in range(4):
                gcol[q, pl.ds((h * 4 + i) * 128, 128), :] = jnp.broadcast_to(cols[i], (128, 128))

    def pick(d):
        same = (lax.broadcasted_iota(jnp.int32, (64, 256), 0)
                == lax.broadcasted_iota(jnp.int32, (64, 256), 1) % 64)
        col_block = lax.broadcasted_iota(jnp.int32, (64, 256), 1) // 64
        for h in range(2):
            for q in range(4):
                for r in range(2):
                    hit = jnp.logical_and(same, col_block == block(d, q, r) - 4 * h)
                    picks[d, h, pl.ds(q * 128 + r * 64, 64), :] = jnp.where(hit, 1.0, 0.0).astype(BF16)

    def columns_then_rows(phase):
        ys, zs = {}, {}
        for q in range(4):
            column(q, phase)
            ys[q] = over_y(phase, q)
            if q >= 2:
                zs[q - 2] = over_z(phase, q - 2, ys[q - 2])
        zs[2] = over_z(phase, 2, ys[2])
        for q in range(4):
            column_done(phase, q, zs[q])
            if phase < ITERS - 1:
                row_single(q)
            elif q < 3:
                row_keep(q, range(8))
            if q == 0:
                zs[3] = over_z(phase, 3, ys[3])

    own_src.wait()
    own_tgt.wait()
    s_c.wait_recv()
    copy_tab.wait()
    unit(0, 0)
    s_pa.wait_recv()
    s_fp = go(transfer(src[6].at[FA], src[4].at[FA], at(kx=1)))
    s_mb.wait_recv()
    s_fm = go(transfer(src[2].at[FB], src[4].at[FB], at(kx=3)))
    y1_p.wait_recv()
    y21 = go(transfer(tgt.at[yi(3), D1], tgt.at[yi(3), D1], up))
    y2_m.wait_recv()
    y22 = go(transfer(tgt.at[yi(1), D2], tgt.at[yi(1), D2], down))
    y2a.wait_recv()
    z2a = z_both(2, ya)
    y2b.wait_recv()
    z2b = z_both(2, yb)
    z3f = z_on(3, *z3)
    s_pb.wait_recv()
    s_cp = go(transfer(src[6], src[7], at(kc=1)))
    s_ma.wait_recv()
    s_cm = go(transfer(src[2], src[3], at(kc=1)))
    z1f = z_on(1, *z1)
    s_cp.wait_recv()
    unit(0, 3)
    s_cm.wait_recv()
    unit(0, 1)
    s_fp.wait_recv()
    s_c2a = go(transfer(src[4].at[FA], src[5].at[FA], at(kc=1)))
    s_fm.wait_recv()
    s_c2b = go(transfer(src[4].at[FB], src[5].at[FB], at(kc=1)))
    z2f = z_on(2, z2a[0], z2b[1])
    for t in (y2_p, *z3f):
        t.wait_recv()
    for kx in (0, 1, 3):
        unit(3, kx)
    s_c2a.wait_recv()
    s_c2b.wait_recv()
    unit(0, 2)
    unit(3, 2)
    for t in (y1_m, *z1f):
        t.wait_recv()
    for kx in range(4):
        unit(1, kx)
    for t in (y21, y22, z2a[1], z2b[0], *z2f):
        t.wait_recv()
    for kx in range(4):
        unit(2, kx)

    for phase in range(ITERS):
        row_local(phase)
        copies = row_start(phase)
        if phase == 0:
            for q in range(4):
                turn(q)
            for d in range(4):
                pick(d)
        else:
            for d in range(4, 8):
                pick(d)
        row_finish(phase, copies)
        row_spread()
        if phase == ITERS - 1:
            even = jnp.concatenate([ftab[2 * i][0:1] for i in range(4)], axis=0)
            odd = jnp.concatenate([ftab[2 * i + 1][0:1] for i in range(4)], axis=0)
            f_out[...] = jnp.where(low[0:4], even, odd) * (REG * LN2)
        columns_then_rows(phase)

    g_out[...] = gpack[y] * (REG * LN2)
    def prepare(kx):
        for d in (2 * kx, 2 * kx + 1):
            out = row_sum(d)
            for b in range(8):
                ltab[d * 16 + b] = jnp.broadcast_to(out[b:b + 1], (8, 128))
            for h in range(2):
                pieces = [jnp.where(low1, out[b:b + 1], out[b + 1:b + 2]) for b in (4 * h, 4 * h + 2)]
                stat[d, h] = jnp.broadcast_to(jnp.concatenate(pieces, axis=1), (8, 256))
        wide = pl.ds(kx * 256, 256)
        for q in range(4):
            out = jnp.dot(tgt_t[q], weights[q, :, wide], preferred_element_type=F32)
            for i in range(2):
                d = 2 * kx + i
                one = jnp.where(low, ltab[d * 16 + block(d, q, 0)], ltab[d * 16 + block(d, q, 1)])
                factor = jnp.exp2(rmax[q, 0:1, lanes(d)] - one[0:1])
                numer[q, :, lanes(d)] = (out[:, i * 128:(i + 1) * 128] * factor).astype(BF16)

    def assemble(d, halves=(0, 1)):
        value = jnp.concatenate([numer[q, :, lanes(d)] for q in range(4)], axis=1)
        for h in halves:
            part[d, h] = jnp.dot(value, picks[d, h], preferred_element_type=F32).astype(BF16)

    def merge(terms):
        stats = [st[...] for _, st in terms]
        joint = lse(stats)
        total = None
        for (value, _), st in zip(terms, stats):
            term = value[...].astype(F32).reshape(32, 8, 256) * jnp.exp2(st - joint)
            total = term if total is None else total + term
        return total.reshape(256, 256), joint

    def own_part(d, h):
        return part.at[d, h], stat.at[d, h]

    def from_core(kx, h):
        return pin.at[kx, h], pstat.at[kx, h]

    to_core = {}

    def give(kx):
        d = kx * 2 + 1
        assemble(d)
        to_core[kx] = [go(transfer(part.at[d], pin.at[kx], at(kc=1))),
                       go(transfer(stat.at[d], pstat.at[kx], at(kc=1)))]

    def give_half(kx, h):
        d = kx * 2 + 1
        assemble(d, (h,))
        to_core[kx, h] = [go(transfer(part.at[d, h], pin.at[kx, h], at(kc=1))),
                          go(transfer(stat.at[d, h], pstat.at[kx, h], at(kc=1)))]

    def take(copies):
        for t in copies:
            t.wait_recv()

    def join(kx, h, extra=()):
        total, cstat[kx, h] = merge([own_part(2 * kx, h), from_core(kx, h), *extra])
        comb[kx, h] = total.astype(BF16)

    def pass_on(kx, h, n, far, device):
        values, stats = (hin, hstat) if far else (rin, rstat)
        index = (n,) if far else (n, h)
        return [go(transfer(comb.at[kx, h], values.at[index], device)),
                go(transfer(cstat.at[kx, h], stats.at[index], device))]

    right, left = at(kx=1), at(kx=3)
    row_keep(3, (4, 5))
    prepare(2)
    give(2)
    assemble(4)
    row_keep(3, (2, 3))
    take(to_core[2])
    join(2, 0)
    h_p = pass_on(2, 0, 0, True, right)
    join(2, 1)
    h_m = pass_on(2, 1, 1, True, left)
    prepare(1)
    give_half(1, 1)
    row_keep(3, (6, 7))
    prepare(3)
    give_half(3, 0)
    assemble(2, (1,))
    take(to_core[1, 1])
    join(1, 1)
    r_p1 = pass_on(1, 1, 0, False, right)
    assemble(6, (0,))
    take(to_core[3, 0])
    join(3, 0)
    r_m0 = pass_on(3, 0, 1, False, left)
    give_half(1, 0)
    give_half(3, 1)
    assemble(2, (0,))
    assemble(6, (1,))
    take(to_core[1, 0])
    take(h_p)
    join(1, 0, [(hin.at[0], hstat.at[0])])
    r_p0 = pass_on(1, 0, 0, False, right)
    take(to_core[3, 1])
    take(h_m)
    join(3, 1, [(hin.at[1], hstat.at[1])])
    r_m1 = pass_on(3, 1, 1, False, left)
    row_keep(3, (0, 1))
    prepare(0)
    give(0)
    assemble(0)
    take(to_core[0])
    for h, copies, n in ((0, r_m0, 1), (1, r_p1, 0)):
        take(copies)
        early[h], estat[h] = merge([own_part(0, h), from_core(0, h), (rin.at[n, h], rstat.at[n, h])])
    for h, copies, n in ((0, r_p0, 0), (1, r_m1, 1)):
        take(copies)
        out, _ = merge([(early.at[h], estat.at[h]), (rin.at[n, h], rstat.at[n, h])])
        turned = lax.dot_general(eye, out.astype(BF16), NT, preferred_element_type=F32)
        mapped[pl.ds(h * 256, 256), :] = turned.astype(BF16)

    for t in sent:
        t.wait_send()


COPIES = 42 + 7 * ITERS + 24 * ITERS + 24


def hand_over(f_in, g_in, m_in, f_out, g_out, m_out, f, g, m, in_sem, out_sem):
    jobs = [(m_in.at[pl.ds(i * 128, 128)], m.at[pl.ds(i * 128, 128)], m_out.at[pl.ds(i * 128, 128)]) for i in range(4)]
    jobs += [(f_in, f, f_out), (g_in, g, g_out)]
    first = [pltpu.make_async_copy(a, b, in_sem.at[n]) for n, (a, b, _) in enumerate(jobs)]
    second = [pltpu.make_async_copy(b, o, out_sem.at[n]) for n, (_, b, o) in enumerate(jobs)]
    for copy in first:
        copy.start()
    for copy, follow in zip(first, second):
        copy.wait()
        follow.start()
    for copy in second:
        copy.wait()


def shards(source, target, pairs, owner_map):
    any_space = pl.BlockSpec(memory_space=pl.ANY)
    smem = pl.BlockSpec(memory_space=pltpu.SMEM)
    vmem = pl.BlockSpec(memory_space=pltpu.VMEM)
    f, g, mapped = pl.pallas_call(
        kernel,
        out_shape=(
            jax.ShapeDtypeStruct((4, 128), F32),
            jax.ShapeDtypeStruct((8, 128), F32),
            jax.ShapeDtypeStruct((512, 256), BF16),
        ),
        in_specs=[any_space, any_space, smem, smem],
        out_specs=(vmem, vmem, vmem),
        scratch_shapes=[
            *[pltpu.VMEM((8, 64, 256), BF16)] * 8,
            pltpu.VMEM((4, 1024, 256), BF16),
            pltpu.VMEM((8, 8, 128), jnp.int32),
            pltpu.VMEM((8, 128), jnp.int32),
            pltpu.SMEM((4, 128), jnp.int32),
            pltpu.VMEM((1024, 256), BF16),
            pltpu.VMEM((4, 1024, 1024), F32),
            pltpu.VMEM((4, 1024, 1024), BF16),
            pltpu.VMEM((4, 256, 1024), BF16),
            pltpu.VMEM((4, 1024, 128), F32),
            pltpu.VMEM((1024, 128), F32),
            pltpu.VMEM((1024, 128), F32),
            pltpu.VMEM((4, 8, 1024), F32),
            pltpu.VMEM((4, 8, 1024), F32),
            pltpu.VMEM((ITERS, 8, 4, 8, 128), F32),
            pltpu.VMEM((128, 8, 128), F32),
            pltpu.VMEM((128, 8, 128), F32),
            pltpu.VMEM((4, 8, 1024), F32),
            pltpu.VMEM((ITERS, 4, 4, 8, 128), F32),
            pltpu.VMEM((ITERS, 4, 4, 8, 128), F32),
            pltpu.VMEM((4, 8, 128), F32),
            pltpu.VMEM((4, 256, 1024), BF16),
            pltpu.VMEM((8, 2, 256, 256), BF16),
            pltpu.VMEM((4, 2, 256, 256), BF16),
            pltpu.VMEM((4, 2, 256, 256), BF16),
            pltpu.VMEM((2, 2, 256, 256), BF16),
            pltpu.VMEM((2, 256, 256), BF16),
            pltpu.VMEM((8, 2, 8, 256), F32),
            pltpu.VMEM((4, 2, 8, 256), F32),
            pltpu.VMEM((4, 2, 8, 256), F32),
            pltpu.VMEM((2, 2, 8, 256), F32),
            pltpu.VMEM((2, 8, 256), F32),
            pltpu.VMEM((8, 2, 512, 256), BF16),
            pltpu.VMEM((2, 256, 256), F32),
            pltpu.VMEM((2, 8, 256), F32),
            pltpu.SemaphoreType.DMA((COPIES,)),
            pltpu.SemaphoreType.DMA((COPIES,)),
            pltpu.SemaphoreType.DMA((3,)),
        ],
        compiler_params=pltpu.CompilerParams(
            collective_id=0, has_side_effects=True, vmem_limit_bytes=60 * 1024 * 1024
        ),
        name="sinkhorn",
    )(source.reshape(8, 64, 256), target, pairs.T, owner_map)
    f, g, mapped = pl.pallas_call(
        hand_over,
        out_shape=(
            jax.ShapeDtypeStruct((4, 128), F32),
            jax.ShapeDtypeStruct((8, 128), F32),
            jax.ShapeDtypeStruct((512, 256), BF16),
        ),
        in_specs=[any_space] * 3,
        out_specs=(any_space,) * 3,
        scratch_shapes=[
            pltpu.VMEM((4, 128), F32),
            pltpu.VMEM((8, 128), F32),
            pltpu.VMEM((512, 256), BF16),
            pltpu.SemaphoreType.DMA((8,)),
            pltpu.SemaphoreType.DMA((8,)),
        ],
        name="hand_over",
    )(f, g, mapped)
    return f.reshape(512), g.reshape(1024), mapped


def solution(mesh):
    return jax.shard_map(
        shards,
        mesh=mesh,
        in_specs=(P(("side", "blk"), None), P("blk", None), P(("side", "blk"), None), P()),
        out_specs=(P(("side", "blk")), P("blk"), P(("side", "blk"), None)),
        check_vma=False,
    )
```
